128 devices in a mesh: dp: 64 (over y, x_lo, z, core), tensor: 2 (over x_hi).
Axes of the slice: x: 4 (x_hi: 2, x_lo: 2; x = x_hi * 2 + x_lo), y: 4, z: 4, core: 2. Of those that a mesh axis runs over, the one named last changes fastest.
Arguments:
- tokens: bfloat16 [64, 512, 896], P(None, 'dp'), may hold values from -6 to 6
- cotangent: bfloat16 [64, 512, 896], P(None, 'dp'), may hold values from -6 to 6
- lengths: int32 [64], replicated, may hold values from 1 to 512, 24576 in all
- deal_order: int32 [64], replicated, may hold values from 0 to 63, each once
- gain_attn: bfloat16 [896], replicated, may hold values from 0.099609375 to 1.8984375
- w_query: bfloat16 [896, 896], P(None, 'tensor'), may hold values from -0.1875 to 0.1875
- b_query: bfloat16 [896], P('tensor'), may hold values from -3 to 3
- w_key: bfloat16 [896, 128], P(None, 'tensor'), may hold values from -0.1875 to 0.1875
- b_key: bfloat16 [128], P('tensor'), may hold values from -3 to 3
- w_value: bfloat16 [896, 128], P(None, 'tensor'), may hold values from -0.1875 to 0.1875
- b_value: bfloat16 [128], P('tensor'), may hold values from -3 to 3
- w_out: bfloat16 [896, 896], P('tensor'), may hold values from -1 to 1
- gain_mlp: bfloat16 [896], replicated, may hold values from 0.099609375 to 1.8984375
- w_gate: bfloat16 [896, 4864], P(None, 'tensor'), may hold values from -0.1875 to 0.1875
- w_up: bfloat16 [896, 4864], P(None, 'tensor'), may hold values from -0.1875 to 0.1875
- w_down: bfloat16 [4864, 896], P('tensor'), may hold values from -0.078125 to 0.078125
Outputs:
- layer_out: bfloat16 [64, 512, 896], P(None, 'dp')
- grad_tokens: bfloat16 [64, 512, 896], P(None, 'dp')
- grad_gain_attn: float32 [896], replicated
- grad_w_query: float32 [896, 896], P(None, 'tensor')
- grad_b_query: float32 [896], P('tensor')
- grad_w_key: float32 [896, 128], P(None, 'tensor')
- grad_b_key: float32 [128], P('tensor')
- grad_w_value: float32 [896, 128], P(None, 'tensor')
- grad_b_value: float32 [128], P('tensor')
- grad_w_out: float32 [896, 896], P('tensor')
- grad_gain_mlp: float32 [896], replicated
- grad_w_gate: float32 [896, 4864], P(None, 'tensor')
- grad_w_up: float32 [896, 4864], P(None, 'tensor')
- grad_w_down: float32 [4864, 896], P('tensor')
- rms_values: float32 [3], replicated
The draws below stay inside these ranges and needn't reach their ends.
Inputs may be any that keep to these rules, and one draw needn't show every extreme that they name: Group g receives stored slot deal_order[g]; every slot goes to exactly one group. The first lengths[g] rows of the slot that group g receives are valid.
All inputs are finite; a program needn't handle non-finite values.
Results may differ from the reference program's by a relative error of at most 0.022.
Values may be sent and summed in bfloat16 or wider, within the bound.
A program may use at most 192 MiB of HBM per device.

```python
import math
import jax
import jax.numpy as jnp
import numpy as np
from jax import lax

D = 896
H = 14
KV = 2
HD = 64
FF = 4864
CAP = 512
N_SEQ = 64


def levels(own_key, extent, split, least, high):
    level = 1.0
    for position, blocks in split:
        heights = jax.random.uniform(jax.random.fold_in(jax.random.fold_in(own_key, 6), position), (blocks,), jnp.float32, least / len(split), high / len(split))
        level = level * jnp.repeat(jnp.exp(heights), extent[position] // blocks).reshape((-1,) + (1,) * (len(extent) - 1 - position))
    return level


def split_up(number_of, total, limit, slope):
    weights = [(1 << 20) // math.isqrt(standing ** slope) + 1 for standing in range(2, number_of + 1)]
    surplus, holding = total - limit - (number_of - 1), [1] * (number_of - 1)
    while surplus > 0:
        candidates = [i for i in range(number_of - 1) if holding[i] < limit]
        mass, remaining = sum([weights[i] for i in candidates]), surplus
        for i in candidates:
            addition = min(limit - holding[i], max(1, remaining * weights[i] // mass), surplus)
            holding[i] = holding[i] + addition
            surplus = surplus - addition
    return np.array([limit] + holding)


def uneven(key, count, total, reach, lean):
    if count == 2:
        one = jax.random.randint(key, (), max(1, total - reach), min(reach, total - 1) + 1)
        return jnp.stack([one, total - one])
    sizes = jnp.asarray(split_up(count, total, reach, lean), jnp.int32)
    couples = (count - 1) // 2
    giver, sink = sizes[1:1 + 2 * couples:2], sizes[2:2 + 2 * couples:2]
    slack = jnp.minimum(giver - 1, reach - sink)
    moved = jax.random.randint(jax.random.fold_in(key, 1), (couples,), 0, 1 << 20) % (slack + 1)
    sizes = sizes.at[1:1 + 2 * couples:2].set(giver - moved).at[2:2 + 2 * couples:2].set(sink + moved)
    return sizes[jax.random.permutation(jax.random.fold_in(key, 2), count)]


def noise(stream_key, extent, scale, bound, shards=(), kind=jnp.bfloat16):
    level = levels(stream_key, extent, shards, -0.22, 0.18) if shards else 1.0
    array = jax.random.normal(stream_key, extent, jnp.float32) * scale * level
    return jnp.minimum(jnp.maximum(array, -bound), bound).astype(kind)


def setup_inputs(seed: int = 0) -> dict:
    arg_keys = jax.random.split(jax.random.key(seed), 17)
    tokens = noise(arg_keys[0], (N_SEQ, CAP, D), 1.0, 6.0, ((1, 64),))
    cotangent = noise(arg_keys[1], (N_SEQ, CAP, D), 1.0, 6.0, ((1, 64),))
    lengths = uneven(arg_keys[2], N_SEQ, N_SEQ * CAP * 3 // 4, CAP, 1).astype(jnp.int32)
    deal_order = jax.random.permutation(arg_keys[3], N_SEQ).astype(jnp.int32)
    gain_attn = jnp.clip(1.0 + 0.18 * jax.random.normal(arg_keys[4], (D,), jnp.float32), 0.099609375, 1.8984375).astype(jnp.bfloat16)
    w_query = noise(arg_keys[5], (D, H * HD), D ** -0.5, 0.1875, ((1, 2),))
    b_query = noise(arg_keys[6], (H * HD,), 0.5, 3.0, ((0, 2),))
    w_key = noise(arg_keys[7], (D, KV * HD), D ** -0.5, 0.1875, ((1, 2),))
    b_key = noise(arg_keys[8], (KV * HD,), 0.5, 3.0, ((0, 2),))
    w_value = noise(arg_keys[9], (D, KV * HD), D ** -0.5, 0.1875, ((1, 2),))
    b_value = noise(arg_keys[10], (KV * HD,), 0.5, 3.0, ((0, 2),))
    w_out = noise(arg_keys[11], (H * HD, D), (H * HD // 32) ** -0.5, 1.0, ((0, 2),))
    gain_mlp = jnp.clip(1.0 + 0.18 * jax.random.normal(arg_keys[12], (D,), jnp.float32), 0.099609375, 1.8984375).astype(jnp.bfloat16)
    w_gate = noise(arg_keys[13], (D, FF), D ** -0.5, 0.1875, ((1, 2),))
    w_up = noise(arg_keys[14], (D, FF), D ** -0.5, 0.1875, ((1, 2),))
    w_down = noise(arg_keys[15], (FF, D), FF ** -0.5, 0.078125, ((0, 2),))
    return dict(tokens=tokens, cotangent=cotangent, lengths=lengths, deal_order=deal_order, gain_attn=gain_attn, w_query=w_query, b_query=b_query, w_key=w_key, b_key=b_key, w_value=w_value, b_value=b_value, w_out=w_out, gain_mlp=gain_mlp, w_gate=w_gate, w_up=w_up, w_down=w_down)


@jax.custom_vjp
def low(v):
    return lax.optimization_barrier(v.astype(jnp.bfloat16)).astype(jnp.float32)

@jax.custom_vjp
def low_back(v):
    return v

def low_keep(v):
    return (low(v), None)

def low_pass(kept, grad):
    return (grad,)

def back_keep(v):
    return (v, None)

def back_low(kept, grad):
    return (low(grad),)
low.defvjp(low_keep, low_pass)
low_back.defvjp(back_keep, back_low)
epsilon = 1e-06
rope_base = 1000000.0
highest = lax.Precision.HIGHEST

def rotate(tensor, cos_table, sine_table):
    half_width = tensor.shape[-1] // 2
    first_half = tensor[..., :half_width]
    second_half = tensor[..., half_width:]
    return jnp.concatenate([first_half * cos_table - second_half * sine_table, second_half * cos_table + first_half * sine_table], axis=-1)

def rms_scale(stream, gain):
    return stream * lax.rsqrt(lax.optimization_barrier(jnp.mean(stream * stream, axis=-1, keepdims=True)) + epsilon) * gain

def forward(stream, gain_one, w_query, b_query, w_key, b_key, w_value, b_value, w_out, gain_two, w_gate, w_up, w_down, length):
    seq_rows = stream.shape[0]
    places = jnp.arange(seq_rows)
    usable = places < length
    row_mask = usable[:, None]
    frequency = rope_base ** (-jnp.arange(HD // 2).astype(jnp.float32) * 2.0 / HD)
    angles = places.astype(jnp.float32)[:, None] * frequency[None, :]
    cos_table = jnp.cos(angles)[:, None, :]
    sine_table = jnp.sin(angles)[:, None, :]
    score_scale = 1.0 / math.sqrt(HD)
    normed = low(rms_scale(stream, gain_one))
    q_lin = low_back(jnp.dot(normed, w_query, precision=highest) + b_query)
    k_lin = low_back(jnp.dot(normed, w_key, precision=highest) + b_key)
    v_lin = low_back(jnp.dot(normed, w_value, precision=highest) + b_value)
    queries = low(rotate(q_lin.reshape(seq_rows, H, HD), cos_table, sine_table))
    keys_rot = low(rotate(k_lin.reshape(seq_rows, KV, HD), cos_table, sine_table))
    values = low(v_lin.reshape(seq_rows, KV, HD))
    queries = queries.reshape(seq_rows, KV, H // KV, HD)
    raw_scores = low_back(jnp.einsum('qkgd,pkd->kgqp', queries, keys_rot, precision=highest))
    allowed = (places[None, :] <= places[:, None]) & usable[None, :]
    scores = jnp.where(allowed, raw_scores * score_scale, -1e+30)
    probs = jax.nn.softmax(scores, axis=-1)
    mixed = jnp.einsum('kgqp,pkd->qkgd', low(probs), values, precision=highest)
    mixed = low(low_back(mixed.reshape(seq_rows, H * HD)))
    attention = low_back(jnp.dot(mixed, w_out, precision=highest))
    residual = stream + attention
    normed_two = low(rms_scale(residual, gain_two))
    gate_lin = low_back(jnp.dot(normed_two, w_gate, precision=highest))
    up_lin = low_back(jnp.dot(normed_two, w_up, precision=highest))
    hidden = low(jax.nn.silu(gate_lin) * up_lin)
    mlp_branch = low_back(jnp.dot(hidden, w_down, precision=highest))
    result = jnp.where(row_mask, residual + mlp_branch, 0.0)
    statistics = jnp.stack([jnp.sum(result * result), jnp.sum(jnp.where(row_mask, attention * attention, 0.0)), jnp.sum(jnp.where(row_mask, mlp_branch * mlp_branch, 0.0))])
    return (result, statistics)

def reference(tokens, cotangent, lengths, deal_order, gain_attn, w_query, b_query, w_key, b_key, w_value, b_value, w_out, gain_mlp, w_gate, w_up, w_down):
    params = tuple((param.astype(jnp.float32) for param in (gain_attn, w_query, b_query, w_key, b_key, w_value, b_value, w_out, gain_mlp, w_gate, w_up, w_down)))
    sequences = tokens[deal_order].astype(jnp.float32)
    cotangents = cotangent[deal_order].astype(jnp.float32)

    def scan_step(carried, inputs):
        totals, sums_sq = carried
        stream, grad_in, length = inputs

        def run_layer(stream_in, *weights):
            return forward(stream_in, *weights, length)
        result, pullback, statistics = jax.vjp(run_layer, stream, *params, has_aux=True)
        gradients = pullback(grad_in)
        totals = tuple((left + right for left, right in zip(totals, gradients[1:])))
        return ((totals, sums_sq + statistics), (result.astype(jnp.bfloat16), gradients[0].astype(jnp.bfloat16)))
    initial = (tuple((jnp.zeros_like(param) for param in params)), jnp.zeros((3,), jnp.float32))
    (totals, sums_sq), (results, grad_rows) = lax.scan(scan_step, initial, (sequences, cotangents, lengths))
    restore = jnp.argsort(deal_order)
    count = jnp.sum(lengths).astype(jnp.float32) * D
    rms_values = jnp.sqrt(sums_sq / count)
    return (results[restore], grad_rows[restore], totals[0], totals[1], totals[2], totals[3], totals[4], totals[5], totals[6], totals[7], totals[8], totals[9], totals[10], totals[11], rms_values)
```

```python
import functools
import math

import jax
import jax.numpy as jnp
from jax import lax
from jax.experimental import pallas as pl
from jax.experimental.pallas import tpu as pltpu
from jax.sharding import PartitionSpec as P

MESH = pl.DeviceIdType.MESH
HD = 64
epsilon = 1e-06
rope_base = 1000000.0
VMEM_LIMIT = 60 << 20
LINKS = ("x", "ya", "za", "yb", "zb")


def flip(dp):
    return dp + 8 - 16 * ((dp // 8) % 2)


def group_of(dp, t):
    return dp + t * (flip(dp) - dp)


def coords():
    return lax.axis_index("dp"), lax.axis_index("tensor")


def partner(dim, dp, t):
    y, xl, z, c = dp // 16, (dp // 8) % 2, (dp // 2) % 4, dp % 2
    if dim == "core":
        c = 1 - c
    if dim == "x":
        xl = 1 - xl
    if dim == "ya":
        y = y + 1 - 2 * (y % 2)
    if dim == "yb":
        y = 3 - y
    if dim == "za":
        z = z + 1 - 2 * (z % 2)
    if dim == "zb":
        z = 3 - z
    if dim == "tn":
        xl, t = 1 - xl, 1 - t
    return (((y * 2 + xl) * 4 + z) * 2 + c, t)


def bit(dim, dp):
    y, xl, z, c = dp // 16, (dp // 8) % 2, (dp // 2) % 4, dp % 2
    return {
        "core": c,
        "x": xl,
        "ya": ((y + 1) // 2) % 2,
        "yb": y // 2,
        "za": ((z + 1) // 2) % 2,
        "zb": z // 2,
    }[dim]


def greet(partners):
    barrier = pltpu.get_barrier_semaphore()
    for who in partners:
        pl.semaphore_signal(barrier, inc=1, device_id=who, device_id_type=MESH)
    pl.semaphore_wait(barrier, len(partners))


def greet_all(dp, t, extra=()):
    barrier = pltpu.get_barrier_semaphore()

    def hello(k, carry):
        pl.semaphore_signal(barrier, inc=1, device_id=((dp + k) % 64, t), device_id_type=MESH)
        return carry

    lax.fori_loop(1, 64, hello, 0)
    for who in extra:
        pl.semaphore_signal(barrier, inc=1, device_id=who, device_id_type=MESH)
    pl.semaphore_wait(barrier, 63 + len(extra))


def remote(src, dst, send, recv, who):
    return pltpu.make_async_remote_copy(
        src_ref=src, dst_ref=dst, send_sem=send, recv_sem=recv, device_id=who, device_id_type=MESH
    )


def add_rows(dst, row, lane, other, rows, lanes):
    step = 16
    while step * 2 * lanes <= 32768 and rows % (step * 2) == 0:
        step *= 2

    def body(i, carry):
        at = dst.at[pl.ds(pl.multiple_of(row + i * step, 16), step), pl.ds(lane, lanes)]
        at[...] = (
            at[...].astype(jnp.float32)
            + other[pl.ds(pl.multiple_of(i * step, 16), step), :].astype(jnp.float32)
        ).astype(jnp.bfloat16)
        return carry

    lax.fori_loop(0, rows // step, body, 0)


class Chain:
    def __init__(self, ref, full, rows, lanes, kinds, turn, recvs, send, recv, dp, t):
        self.ref, self.full, self.recvs, self.send, self.recv = ref, full, recvs, send, recv
        self.dims = ("core",) + tuple(LINKS[(turn + i) % 5] for i in range(5))
        self.kinds = kinds
        self.last = max(i for i, kind in enumerate(kinds) if kind != "f")
        self.region = [(0, rows, 0, lanes)]
        self.who = [partner(d, dp, t) for d in self.dims]
        self.bits = [bit(d, dp) for d in self.dims]

    def part(self, region, full=False):
        row, rows, lane, lanes = region
        if not isinstance(row, int):
            row = pl.multiple_of(row, 16)
        if not isinstance(lane, int):
            lane = pl.multiple_of(lane, 128)
        return (self.full if full else self.ref).at[pl.ds(row, rows), pl.ds(lane, lanes)]

    def own(self):
        self.part(self.region[6], True)[...] = self.part(self.region[6])[...]

    def scatter_start(self, s):
        row, rows, lane, lanes = self.region[s]
        b = self.bits[s]
        if self.kinds[s] == "r":
            keep = (row + b * (rows // 2), rows // 2, lane, lanes)
            give = (row + (1 - b) * (rows // 2), rows // 2, lane, lanes)
        elif self.kinds[s] == "l":
            keep = (row, rows, lane + b * (lanes // 2), lanes // 2)
            give = (row, rows, lane + (1 - b) * (lanes // 2), lanes // 2)
        else:
            keep = give = self.region[s]
        self.region.append(keep)
        self.copy = remote(self.part(give), self.recvs[s], self.send[s], self.recv[s], self.who[s])
        self.copy.start()

    def scatter_finish(self, s):
        self.copy.wait()
        row, rows, lane, lanes = self.region[s + 1]
        add_rows(self.ref, row, lane if isinstance(lane, int) else pl.multiple_of(lane, 128), self.recvs[s], rows, lanes)

    def gather_start(self, s):
        n = len(self.dims)
        mine = self.part(self.region[s + 1], True)
        self.copy = remote(mine, mine, self.send[n + s], self.recv[n + s], self.who[s])
        self.copy.start()

    def gather_finish(self, s):
        if self.kinds[s] != "f":
            self.copy.wait()


G_KINDS = ("l", "l", "r", "r", "r", "f")
D_KINDS = ("r", "r", "r", "r", "r", "f")
K_KINDS = ("r", "r", "r", "f", "f", "f")


def recv_shapes(rows, lanes, kinds):
    out = []
    for kind in kinds:
        if kind == "r":
            rows //= 2
        elif kind == "l":
            lanes //= 2
        out.append((rows, lanes))
    return out


G_RECV = recv_shapes(896, 512, G_KINDS)
D_RECV = recv_shapes(512, 896, D_KINDS)
K_RECV = recv_shapes(896, 128, K_KINDS)


def dispatch_kernel(order, tok, cot, tok_out, cot_out, tok_buf, cot_buf, send, recv):
    dp, t = coords()
    greet_all(dp, t)

    def pick(g, carry):
        slot = order[g]
        tok_buf[g] = tok[slot]
        return carry

    def pick_two(g, carry):
        cot_buf[g] = cot[order[g]]
        return carry

    def out(buf, dst, i):
        def go(k, carry):
            dest = (dp + k) % 64
            remote(buf.at[group_of(dest, t)], dst.at[dp], send.at[i], recv.at[i], (dest, t)).start()
            return carry

        lax.fori_loop(1, 64, go, 0)
        dst[dp] = buf[group_of(dp, t)]

    lax.fori_loop(0, 64, pick, 0)
    out(tok_buf, tok_out, 0)
    lax.fori_loop(0, 64, pick_two, 0)
    out(cot_buf, cot_out, 1)
    for buf, dst, i in ((tok_buf, tok_out, 0), (cot_buf, cot_out, 1)):
        some = pl.ds(0, 63)
        pltpu.make_async_copy(buf.at[some], dst.at[some], send.at[i]).wait()
        pltpu.make_async_copy(buf.at[some], dst.at[some], recv.at[i]).wait()


def dispatch(order, tokens, cotangent):
    block = jax.ShapeDtypeStruct((64, 8, 896), jnp.bfloat16)
    vmem = pl.BlockSpec(memory_space=pltpu.VMEM)
    return pl.pallas_call(
        dispatch_kernel,
        out_shape=(block, block),
        in_specs=[pl.BlockSpec(memory_space=pltpu.SMEM), vmem, vmem],
        out_specs=(vmem, vmem),
        scratch_shapes=[
            pltpu.VMEM((64, 8, 896), jnp.bfloat16),
            pltpu.VMEM((64, 8, 896), jnp.bfloat16),
            pltpu.SemaphoreType.DMA((2,)),
            pltpu.SemaphoreType.DMA((2,)),
        ],
        compiler_params=pltpu.CompilerParams(collective_id=1, has_side_effects=True, vmem_limit_bytes=VMEM_LIMIT),
        name="dispatch",
    )(order, tokens, cotangent)


def exchange_kernel(x, out, got, send, recv):
    dp, t = coords()
    who = partner("tn", dp, t)
    greet([who])
    copies = []
    n = x.shape[0] // 128
    for i in range(n):
        rows = pl.ds(i * 128, 128)
        copies.append(remote(x.at[rows], got.at[rows], send.at[i], recv.at[i], who))
        copies[-1].start()
    for i in range(n):
        rows = pl.ds(i * 128, 128)
        copies[i].wait()
        out[rows, :] = x[rows, :].astype(jnp.float32) + got[rows, :].astype(jnp.float32)


def exchange(x, cid):
    vmem = pl.BlockSpec(memory_space=pltpu.VMEM)
    n = x.shape[0] // 128
    return pl.pallas_call(
        exchange_kernel,
        out_shape=jax.ShapeDtypeStruct(x.shape, jnp.float32),
        in_specs=[vmem],
        out_specs=vmem,
        scratch_shapes=[
            pltpu.VMEM(x.shape, jnp.bfloat16),
            pltpu.SemaphoreType.DMA((n,)),
            pltpu.SemaphoreType.DMA((n,)),
        ],
        compiler_params=pltpu.CompilerParams(collective_id=cid, has_side_effects=True, vmem_limit_bytes=VMEM_LIMIT),
        name="exchange",
    )(x)


def finish_kernel(
    gate, up, down, query, kv, out_w, small, res, gtok,
    gate_o, up_o, down_o, query_o, kv_o, out_o, small_o, res_o, gtok_o,
    g_buf, d_buf, k_buf, g_full, d_full, k_full, small_buf, small_got,
    g0, g1, g2, g3, g4, g5, d0, d1, d2, d3, d4, d5, k0, k1, k2, k3, k4, k5,
    send, recv, s_send, s_recv, b_send, b_recv, local,
):
    dp, t = coords()
    me = group_of(dp, t)
    loads = []

    def load(src, dst):
        c = pltpu.make_async_copy(src, dst, local.at[len(loads)])
        c.start()
        loads.append(c)

    for i, src in enumerate((gate, up)):
        for p in range(5):
            w = 512 if p < 4 else 384
            load(src.at[:, pl.ds(512 * p, w)], g_buf.at[5 * i + p, :, pl.ds(0, w)])
    load(query, g_buf.at[10, :, pl.ds(0, 512)])
    for p in range(5):
        w = 512 if p < 4 else 384
        load(down.at[pl.ds(512 * p, w), :], d_buf.at[p, pl.ds(0, w), :])
    load(out_w, d_buf.at[5, pl.ds(0, 448), :])
    load(kv, k_buf)
    greet_all(dp, t, [partner("x", dp, t)] * 0)
    for src, dst, i in ((res, res_o, 0), (gtok, gtok_o, 1)):
        def go(k, carry):
            dest = (dp + k) % 64
            remote(src.at[dest], dst.at[me], b_send.at[i], b_recv.at[i], (dest, t)).start()
            return carry

        lax.fori_loop(1, 64, go, 0)
        dst[me] = src[dp]
    for p in (4, 9):
        g_buf[p, :, 384:] = jnp.zeros((896, 128), jnp.bfloat16)
    d_buf[4, 384:, :] = jnp.zeros((128, 896), jnp.bfloat16)
    d_buf[5, 448:, :] = jnp.zeros((64, 896), jnp.bfloat16)
    for c in loads:
        c.wait()
    gr = (g0, g1, g2, g3, g4, g5)
    dr = (d0, d1, d2, d3, d4, d5)
    kr = (k0, k1, k2, k3, k4, k5)
    chains = []
    for p in range(11):
        n = len(chains)
        chains.append(
            Chain(g_buf.at[p], g_full.at[p], 896, 512, G_KINDS, n % 5, [r.at[p] for r in gr],
                  [send.at[n, i] for i in range(12)], [recv.at[n, i] for i in range(12)], dp, t)
        )
    for p in range(6):
        n = len(chains)
        chains.append(
            Chain(d_buf.at[p], d_full.at[p], 512, 896, D_KINDS, n % 5, [r.at[p] for r in dr],
                  [send.at[n, i] for i in range(12)], [recv.at[n, i] for i in range(12)], dp, t)
        )
    n = len(chains)
    chains.append(
        Chain(k_buf, k_full, 896, 128, K_KINDS, n % 5, list(kr),
              [send.at[n, i] for i in range(12)], [recv.at[n, i] for i in range(12)], dp, t)
    )
    for c in chains:
        c.scatter_start(0)
    small_buf[0] = small[...]
    dims = ("core",) + LINKS
    for s in range(6):
        sc = remote(small_buf.at[s], small_got.at[s], s_send.at[s], s_recv.at[s], partner(dims[s], dp, t))
        sc.start()
        for c in chains:
            c.scatter_finish(s)
            if s < 5:
                c.scatter_start(s + 1)
        sc.wait()
        small_buf[s + 1] = small_buf[s] + small_got[s]
    small_o[...] = small_buf[6]
    for c in chains:
        c.own()
        c.gather_start(c.last)
    for s in reversed(range(6)):
        for c in chains:
            c.gather_finish(s)
            if 0 < s <= c.last:
                c.gather_start(s - 1)
    loads.clear()
    for i, dst in enumerate((gate_o, up_o)):
        for p in range(5):
            w = 512 if p < 4 else 384
            load(g_full.at[5 * i + p, :, pl.ds(0, w)], dst.at[:, pl.ds(512 * p, w)])
    load(g_full.at[10], query_o)
    for p in range(5):
        w = 512 if p < 4 else 384
        load(d_full.at[p, pl.ds(0, w), :], down_o.at[pl.ds(512 * p, w), :])
    load(d_full.at[5, pl.ds(0, 448), :], out_o)
    load(k_full, kv_o)
    for src, dst, i in ((res, res_o, 0), (gtok, gtok_o, 1)):
        some = pl.ds(0, 63)
        pltpu.make_async_copy(src.at[some], dst.at[some], b_send.at[i]).wait()
        pltpu.make_async_copy(src.at[some], dst.at[some], b_recv.at[i]).wait()
    for c in loads:
        c.wait()


def finish(gate, up, down, query, kv, out_w, small, res, gtok):
    bf = jnp.bfloat16
    anyw = pl.BlockSpec(memory_space=pl.ANY)
    vmem = pl.BlockSpec(memory_space=pltpu.VMEM)
    block = jax.ShapeDtypeStruct((64, 8, 896), bf)
    return pl.pallas_call(
        finish_kernel,
        out_shape=(
            jax.ShapeDtypeStruct((896, 2432), bf),
            jax.ShapeDtypeStruct((896, 2432), bf),
            jax.ShapeDtypeStruct((2432, 896), bf),
            jax.ShapeDtypeStruct((896, 512), bf),
            jax.ShapeDtypeStruct((896, 128), bf),
            jax.ShapeDtypeStruct((448, 896), bf),
            jax.ShapeDtypeStruct((8, 896), jnp.float32),
            block,
            block,
        ),
        in_specs=[anyw] * 6 + [vmem] * 3,
        out_specs=(anyw,) * 6 + (vmem,) * 3,
        scratch_shapes=[
            pltpu.VMEM((11, 896, 512), bf),
            pltpu.VMEM((6, 512, 896), bf),
            pltpu.VMEM((896, 128), bf),
            pltpu.VMEM((11, 896, 512), bf),
            pltpu.VMEM((6, 512, 896), bf),
            pltpu.VMEM((896, 128), bf),
            pltpu.VMEM((7, 8, 896), jnp.float32),
            pltpu.VMEM((6, 8, 896), jnp.float32),
            *[pltpu.VMEM((11, *s), bf) for s in G_RECV],
            *[pltpu.VMEM((6, *s), bf) for s in D_RECV],
            *[pltpu.VMEM(s, bf) for s in K_RECV],
            pltpu.SemaphoreType.DMA((18, 12)),
            pltpu.SemaphoreType.DMA((18, 12)),
            pltpu.SemaphoreType.DMA((6,)),
            pltpu.SemaphoreType.DMA((6,)),
            pltpu.SemaphoreType.DMA((2,)),
            pltpu.SemaphoreType.DMA((2,)),
            pltpu.SemaphoreType.DMA((20,)),
        ],
        compiler_params=pltpu.CompilerParams(collective_id=2, has_side_effects=True, vmem_limit_bytes=VMEM_LIMIT),
        name="finish",
    )(gate, up, down, query, kv, out_w, small, res, gtok)


def rope_tables(seq_rows, head_size):
    places = jnp.arange(seq_rows).astype(jnp.float32)
    frequency = rope_base ** (-jnp.arange(head_size // 2).astype(jnp.float32) * 2.0 / head_size)
    angles = places[:, None] * frequency[None, :]
    return (jnp.cos(angles)[:, None, :], jnp.sin(angles)[:, None, :])


def rotate(tensor, cos_table, sine_table):
    half_width = tensor.shape[-1] // 2
    first_half = tensor[..., :half_width]
    second_half = tensor[..., half_width:]
    return jnp.concatenate(
        [
            first_half * cos_table - second_half * sine_table,
            second_half * cos_table + first_half * sine_table,
        ],
        axis=-1,
    )


def unrotate(grad_rot, cos_table, sine_table):
    half_width = grad_rot.shape[-1] // 2
    first_half = grad_rot[..., :half_width]
    second_half = grad_rot[..., half_width:]
    return jnp.concatenate(
        [
            first_half * cos_table + second_half * sine_table,
            second_half * cos_table - first_half * sine_table,
        ],
        axis=-1,
    )


def dot_left(matrix, other):
    return lax.dot_general(
        matrix, other, (((0,), (0,)), ((), ())), preferred_element_type=jnp.float32
    )


def dot_right(matrix, other):
    return lax.dot_general(
        matrix, other, (((1,), (1,)), ((), ())), preferred_element_type=jnp.float32
    )


def on_device(
    tokens,
    cotangent,
    lengths,
    deal_order,
    gain_attn,
    w_query,
    b_query,
    w_key,
    b_key,
    w_value,
    b_value,
    w_out,
    gain_mlp,
    w_gate,
    w_up,
    w_down,
):
    slots = jnp.arange(64, dtype=jnp.int32)
    restore = jnp.sum(
        jnp.where(deal_order[None, :] == slots[:, None], slots[None, :], 0), axis=1
    )
    arrived = dispatch(deal_order, tokens, cotangent)
    stream = arrived[0].reshape(512, 896).astype(jnp.float32)
    grad_out = arrived[1].reshape(512, 896).astype(jnp.float32)
    seq_rows, width = stream.shape
    head_size = HD
    length = lengths[group_of(*coords())]
    places = jnp.arange(seq_rows)
    usable = places < length
    row_mask = usable[:, None]
    cos_table, sine_table = rope_tables(seq_rows, head_size)
    local_heads = w_query.shape[1] // head_size
    local_kv = w_key.shape[1] // head_size
    group_size = local_heads // local_kv
    score_scale = 1.0 / math.sqrt(head_size)
    allowed = (places[None, :] <= places[:, None]) & usable[None, :]
    gain_one = gain_attn.astype(jnp.float32)
    gain_two = gain_mlp.astype(jnp.float32)
    inverse_one = lax.rsqrt(jnp.mean(stream * stream, axis=-1, keepdims=True) + epsilon)
    normed = (stream * inverse_one * gain_one).astype(jnp.bfloat16)
    q_lin = jnp.dot(normed, w_query, preferred_element_type=jnp.float32) + b_query.astype(
        jnp.float32
    )
    k_lin = jnp.dot(normed, w_key, preferred_element_type=jnp.float32) + b_key.astype(jnp.float32)
    v_lin = jnp.dot(normed, w_value, preferred_element_type=jnp.float32) + b_value.astype(
        jnp.float32
    )
    queries = rotate(q_lin.reshape(seq_rows, local_heads, head_size), cos_table, sine_table).astype(
        jnp.bfloat16
    )
    queries = queries.reshape(seq_rows, local_kv, group_size, head_size)
    keys_rot = rotate(k_lin.reshape(seq_rows, local_kv, head_size), cos_table, sine_table).astype(
        jnp.bfloat16
    )
    values = v_lin.reshape(seq_rows, local_kv, head_size).astype(jnp.bfloat16)
    raw_scores = jnp.einsum("qkgd,pkd->kgqp", queries, keys_rot, preferred_element_type=jnp.float32)
    scores = jnp.where(allowed, raw_scores * score_scale, -1e30)
    top_score = jnp.max(scores, axis=-1, keepdims=True)
    expo = jnp.exp(scores - top_score)
    total = jnp.sum(expo, axis=-1, keepdims=True)
    log_total = top_score + jnp.log(total)
    probs_low = (expo / total).astype(jnp.bfloat16)
    mixed = jnp.einsum("kgqp,pkd->qkgd", probs_low, values, preferred_element_type=jnp.float32)
    mixed = mixed.reshape(seq_rows, local_heads * head_size).astype(jnp.bfloat16)
    attention = exchange(
        jnp.dot(mixed, w_out, preferred_element_type=jnp.float32).astype(jnp.bfloat16), 3
    )
    residual = stream + attention
    inverse_two = lax.rsqrt(jnp.mean(residual * residual, axis=-1, keepdims=True) + epsilon)
    normed_two = (residual * inverse_two * gain_two).astype(jnp.bfloat16)
    gate_lin = jnp.dot(normed_two, w_gate, preferred_element_type=jnp.float32)
    up_lin = jnp.dot(normed_two, w_up, preferred_element_type=jnp.float32)
    sigmoid_gate = jax.nn.sigmoid(gate_lin)
    silu_gate = gate_lin * sigmoid_gate
    hidden = (silu_gate * up_lin).astype(jnp.bfloat16)
    mlp_branch = exchange(
        jnp.dot(hidden, w_down, preferred_element_type=jnp.float32).astype(jnp.bfloat16), 4
    )
    result = jnp.where(row_mask, residual + mlp_branch, 0.0)
    statistics = jnp.stack(
        [
            jnp.sum(result * result),
            jnp.sum(jnp.where(row_mask, attention * attention, 0.0)),
            jnp.sum(jnp.where(row_mask, mlp_branch * mlp_branch, 0.0)),
        ]
    )
    grad_y = jnp.where(row_mask, grad_out, 0.0)
    grad_low = grad_y.astype(jnp.bfloat16)
    grad_w_down = dot_left(hidden, grad_low)
    grad_hidden = dot_right(grad_low, w_down)
    grad_gate = (
        grad_hidden * up_lin * sigmoid_gate * (1.0 + gate_lin * (1.0 - sigmoid_gate))
    ).astype(jnp.bfloat16)
    grad_up = (grad_hidden * silu_gate).astype(jnp.bfloat16)
    grad_w_gate = dot_left(normed_two, grad_gate)
    grad_w_up = dot_left(normed_two, grad_up)
    grad_normed_two = exchange(
        (dot_right(grad_gate, w_gate) + dot_right(grad_up, w_up)).astype(jnp.bfloat16), 5
    )
    grad_gain_mlp = jnp.sum(grad_normed_two * residual * inverse_two, axis=0)
    scaled_two = grad_normed_two * gain_two
    grad_resid = (
        grad_y
        + inverse_two * scaled_two
        - residual * inverse_two**3 * jnp.mean(scaled_two * residual, axis=-1, keepdims=True)
    )
    grad_attn = grad_resid.astype(jnp.bfloat16)
    grad_w_out = dot_left(mixed, grad_attn)
    grad_mixed = dot_right(grad_attn, w_out).astype(jnp.bfloat16)
    grad_mixed = grad_mixed.reshape(seq_rows, local_kv, group_size, head_size)
    probs = jnp.exp(scores - log_total)
    grad_probs = jnp.einsum(
        "qkgd,pkd->kgqp", grad_mixed, values, preferred_element_type=jnp.float32
    )
    grad_values = jnp.einsum(
        "kgqp,qkgd->pkd", probs_low, grad_mixed, preferred_element_type=jnp.float32
    )
    row_inner = jnp.sum(probs * grad_probs, axis=-1, keepdims=True)
    grad_scores = (probs * (grad_probs - row_inner) * score_scale).astype(jnp.bfloat16)
    grad_queries = jnp.einsum(
        "kgqp,pkd->qkgd", grad_scores, keys_rot, preferred_element_type=jnp.float32
    )
    grad_keys = jnp.einsum(
        "kgqp,qkgd->pkd", grad_scores, queries, preferred_element_type=jnp.float32
    )
    grad_q_lin = unrotate(
        grad_queries.reshape(seq_rows, local_heads, head_size), cos_table, sine_table
    )
    grad_q_lin = grad_q_lin.reshape(seq_rows, local_heads * head_size).astype(jnp.bfloat16)
    grad_k_lin = (
        unrotate(grad_keys, cos_table, sine_table)
        .reshape(seq_rows, local_kv * head_size)
        .astype(jnp.bfloat16)
    )
    grad_v_lin = grad_values.reshape(seq_rows, local_kv * head_size).astype(jnp.bfloat16)
    grad_w_query = dot_left(normed, grad_q_lin)
    grad_w_key = dot_left(normed, grad_k_lin)
    grad_w_value = dot_left(normed, grad_v_lin)
    grad_b_query = jnp.sum(grad_q_lin.astype(jnp.float32), axis=0)
    grad_b_key = jnp.sum(grad_k_lin.astype(jnp.float32), axis=0)
    grad_b_value = jnp.sum(grad_v_lin.astype(jnp.float32), axis=0)
    grad_normed = exchange(
        (
            dot_right(grad_q_lin, w_query)
            + dot_right(grad_k_lin, w_key)
            + dot_right(grad_v_lin, w_value)
        ).astype(jnp.bfloat16),
        6,
    )
    grad_gain_attn = jnp.sum(grad_normed * stream * inverse_one, axis=0)
    scaled_one = grad_normed * gain_one
    grad_stream = (
        grad_resid
        + inverse_one * scaled_one
        - stream * inverse_one**3 * jnp.mean(scaled_one * stream, axis=-1, keepdims=True)
    )
    low = jnp.bfloat16
    small = jnp.zeros((8, 896), jnp.float32)
    small = small.at[0].set(grad_gain_attn).at[1].set(grad_gain_mlp)
    small = small.at[2, :448].set(grad_b_query).at[2, 448:512].set(grad_b_key)
    small = small.at[2, 512:576].set(grad_b_value).at[3, :3].set(statistics)
    query = jnp.pad(grad_w_query.astype(low), ((0, 0), (0, 64)))
    kv = jnp.concatenate([grad_w_key, grad_w_value], axis=1).astype(low)
    gate, up, down, query, kv, out_w, small, sent_res, sent_tok = finish(
        grad_w_gate.astype(low),
        grad_w_up.astype(low),
        grad_w_down.astype(low),
        query,
        kv,
        grad_w_out.astype(low),
        small,
        result.astype(low).reshape(64, 8, 896),
        grad_stream.astype(low).reshape(64, 8, 896),
    )
    layer_out = sent_res[restore]
    grad_tokens = sent_tok[restore]
    wide = jnp.float32
    grad_w_gate, grad_w_up, grad_w_down = gate.astype(wide), up.astype(wide), down.astype(wide)
    grad_w_query = query[:, :448].astype(wide)
    grad_w_key, grad_w_value = kv[:, :64].astype(wide), kv[:, 64:].astype(wide)
    grad_w_out = out_w.astype(wide)
    grad_gain_attn, grad_gain_mlp = small[0], small[1]
    grad_b_query, grad_b_key, grad_b_value = small[2, :448], small[2, 448:512], small[2, 512:576]
    statistics = small[3, :3]
    count = jnp.sum(lengths).astype(jnp.float32) * width
    rms_values = jnp.sqrt(statistics / count)
    return (
        layer_out,
        grad_tokens,
        grad_gain_attn,
        grad_w_query,
        grad_b_query,
        grad_w_key,
        grad_b_key,
        grad_w_value,
        grad_b_value,
        grad_w_out,
        grad_gain_mlp,
        grad_w_gate,
        grad_w_up,
        grad_w_down,
        rms_values,
    )


def solution(mesh):
    in_specs = (
        P(None, "dp", None),
        P(None, "dp", None),
        P(),
        P(),
        P(),
        P(None, "tensor"),
        P("tensor"),
        P(None, "tensor"),
        P("tensor"),
        P(None, "tensor"),
        P("tensor"),
        P("tensor", None),
        P(),
        P(None, "tensor"),
        P(None, "tensor"),
        P("tensor", None),
    )
    out_specs = (
        P(None, "dp", None),
        P(None, "dp", None),
        P(),
        P(None, "tensor"),
        P("tensor"),
        P(None, "tensor"),
        P("tensor"),
        P(None, "tensor"),
        P("tensor"),
        P("tensor", None),
        P(),
        P(None, "tensor"),
        P(None, "tensor"),
        P("tensor", None),
        P(),
    )
    return jax.shard_map(
        on_device, mesh=mesh, in_specs=in_specs, out_specs=out_specs, check_vma=False
    )
```

```python
import functools
import math

import jax
import jax.numpy as jnp
from jax import lax
from jax.experimental import pallas as pl
from jax.experimental.pallas import tpu as pltpu
from jax.sharding import PartitionSpec as P

MESH = pl.DeviceIdType.MESH
HD = 64
epsilon = 1e-06
rope_base = 1000000.0
VMEM_LIMIT = 60 << 20
LINKS = ("x", "ya", "za", "yb", "zb")


def flip(dp):
    return dp + 8 - 16 * ((dp // 8) % 2)


def group_of(dp, t):
    return dp + t * (flip(dp) - dp)


def coords():
    return lax.axis_index("dp"), lax.axis_index("tensor")


def partner(dim, dp, t):
    y, xl, z, c = dp // 16, (dp // 8) % 2, (dp // 2) % 4, dp % 2
    if dim == "core":
        c = 1 - c
    if dim == "x":
        xl = 1 - xl
    if dim == "ya":
        y = y + 1 - 2 * (y % 2)
    if dim == "yb":
        y = 3 - y
    if dim == "za":
        z = z + 1 - 2 * (z % 2)
    if dim == "zb":
        z = 3 - z
    if dim == "tn":
        xl, t = 1 - xl, 1 - t
    return (((y * 2 + xl) * 4 + z) * 2 + c, t)


def bit(dim, dp):
    y, xl, z, c = dp // 16, (dp // 8) % 2, (dp // 2) % 4, dp % 2
    return {
        "core": c,
        "x": xl,
        "ya": ((y + 1) // 2) % 2,
        "yb": y // 2,
        "za": ((z + 1) // 2) % 2,
        "zb": z // 2,
    }[dim]


def greet(partners):
    barrier = pltpu.get_barrier_semaphore()
    for who in partners:
        pl.semaphore_signal(barrier, inc=1, device_id=who, device_id_type=MESH)
    pl.semaphore_wait(barrier, len(partners))


def greet_all(dp, t, extra=()):
    barrier = pltpu.get_barrier_semaphore()

    def hello(k, carry):
        pl.semaphore_signal(barrier, inc=1, device_id=((dp + k) % 64, t), device_id_type=MESH)
        return carry

    lax.fori_loop(1, 64, hello, 0)
    for who in extra:
        pl.semaphore_signal(barrier, inc=1, device_id=who, device_id_type=MESH)
    pl.semaphore_wait(barrier, 63 + len(extra))


def remote(src, dst, send, recv, who):
    return pltpu.make_async_remote_copy(
        src_ref=src, dst_ref=dst, send_sem=send, recv_sem=recv, device_id=who, device_id_type=MESH
    )


def put_sum(dst, src, row, lane, other, rows, lanes):
    step = 16
    while step * 2 * lanes <= 32768 and rows % (step * 2) == 0:
        step *= 2

    def body(i, carry):
        here = pl.ds(pl.multiple_of(i * step, 16), step)
        there = pl.ds(pl.multiple_of(row + i * step, 16), step)
        lane_at = lane if isinstance(lane, int) else pl.multiple_of(lane, 128)
        dst[here, :] = src[there, pl.ds(lane_at, lanes)] + other[here, :]
        return carry

    lax.fori_loop(0, rows // step, body, 0)


def halves(rows, lanes, kinds):
    out = []
    for kind in kinds:
        if kind == "r":
            rows //= 2
        elif kind == "l":
            lanes //= 2
        out.append((rows, lanes))
    return out


class Chain:
    def __init__(self, rows, lanes, kinds, turn, dp, t):
        self.kinds = kinds
        self.dims = ("core",) + tuple(LINKS[(turn + i) % 5] for i in range(5))
        self.who = [partner(d, dp, t) for d in self.dims]
        self.bits = [bit(d, dp) for d in self.dims]
        self.shapes = [(rows, lanes)] + halves(rows, lanes, kinds)
        self.last = max(i for i, kind in enumerate(kinds) if kind != "f")
        self.corner = [(0, 0)]
        for s, kind in enumerate(kinds):
            row, lane = self.corner[-1]
            rows, lanes = self.shapes[s + 1]
            b = self.bits[s]
            self.corner.append((row + (b * rows if kind == "r" else 0), lane + (b * lanes if kind == "l" else 0)))

    def start(self, s, src, got, send, recv):
        rows, lanes = self.shapes[s + 1]
        give, self.keep = (0, 0), (0, 0)
        b = self.bits[s]
        if self.kinds[s] == "r":
            give, self.keep = (pl.multiple_of((1 - b) * rows, 16), 0), (b * rows, 0)
        elif self.kinds[s] == "l":
            give, self.keep = (0, pl.multiple_of((1 - b) * lanes, 128)), (0, b * lanes)
        self.src, self.got = src, got
        self.copy = remote(src.at[pl.ds(give[0], rows), pl.ds(give[1], lanes)], got, send, recv, self.who[s])
        self.copy.start()

    def finish(self, s, dst):
        self.copy.wait()
        rows, lanes = self.shapes[s + 1]
        put_sum(dst, self.src, self.keep[0], self.keep[1], self.got, rows, lanes)

    def spot(self, s, full, base):
        rows, lanes = self.shapes[s]
        row, lane = self.corner[s]
        row, lane = row + base[0], lane + base[1]
        row = row if isinstance(row, int) else pl.multiple_of(row, 16)
        lane = lane if isinstance(lane, int) else pl.multiple_of(lane, 128)
        return full.at[pl.ds(row, rows), pl.ds(lane, lanes)]

    def gather_start(self, s, full, base, send, recv):
        mine = self.spot(s + 1, full, base)
        self.copy = remote(mine, mine, send, recv, self.who[s])
        self.copy.start()

    def gather_finish(self):
        self.copy.wait()


G_KINDS = ("l", "l", "r", "r", "r", "f")
D_KINDS = ("r", "r", "r", "r", "r", "f")
K_KINDS = ("r", "r", "r", "f", "f", "f")
G_SHAPES = halves(896, 512, G_KINDS)
D_SHAPES = halves(512, 896, D_KINDS)
K_SHAPES = halves(896, 128, K_KINDS)
BF, F32 = jnp.bfloat16, jnp.float32
VMEM_SPEC = pl.BlockSpec(memory_space=pltpu.VMEM)
SMEM_SPEC = pl.BlockSpec(memory_space=pltpu.SMEM)
BLOCK = jax.ShapeDtypeStruct((64, 8, 896), BF)
DMA = pltpu.SemaphoreType.DMA


def params(cid):
    return pltpu.CompilerParams(collective_id=cid, has_side_effects=True, vmem_limit_bytes=VMEM_LIMIT)


def deal(order, rows, buf, dst, send, recv, dp, t):
    def go(k, carry):
        dest = (dp + k) % 64
        buf[k] = rows[order[group_of(dest, t)]]
        remote(buf.at[k], dst.at[dp], send, recv, (dest, t)).start()
        return carry

    lax.fori_loop(1, 64, go, 0)
    dst[dp] = rows[order[group_of(dp, t)]]


def all_in(buf, dst, send, recv):
    some = pl.ds(0, 63)
    pltpu.make_async_copy(buf.at[some], buf.at[some], send).wait()
    pltpu.make_async_copy(dst.at[some], dst.at[some], recv).wait()


def dispatch_kernel(order, tok, out, buf, send, recv):
    dp, t = coords()
    greet_all(dp, t)
    deal(order, tok, buf, out, send, recv, dp, t)
    all_in(buf, out, send, recv)


def dispatch(order, tokens):
    return pl.pallas_call(
        dispatch_kernel,
        out_shape=BLOCK,
        in_specs=[SMEM_SPEC, VMEM_SPEC],
        out_specs=VMEM_SPEC,
        scratch_shapes=[pltpu.VMEM((64, 8, 896), BF), DMA, DMA],
        compiler_params=params(1),
        name="dispatch",
    )(order, tokens)


class Swap:
    def __init__(self, x, got, send, recv, dp, t):
        self.who = partner("tn", dp, t)
        self.x, self.got, self.send, self.recv = x, got, send, recv

    def start(self):
        self.copies = []
        for i in range(4):
            rows = pl.ds(i * 128, 128)
            self.copies.append(remote(self.x.at[rows], self.got.at[rows], self.send.at[i], self.recv.at[i], self.who))
            self.copies[-1].start()

    def take(self, i):
        self.copies[i].wait()
        rows = pl.ds(i * 128, 128)
        return self.x[rows, :].astype(F32) + self.got[rows, :].astype(F32)


def meet_kernel(order, x, cot, out, cot_out, got, buf, send, recv, c_send, c_recv):
    dp, t = coords()
    swap = Swap(x, got, send, recv, dp, t)
    greet_all(dp, t, [swap.who])
    swap.start()
    deal(order, cot, buf, cot_out, c_send, c_recv, dp, t)
    for i in range(4):
        out[pl.ds(i * 128, 128), :] = swap.take(i)
    all_in(buf, cot_out, c_send, c_recv)


def meet(order, x, cotangent):
    return pl.pallas_call(
        meet_kernel,
        out_shape=(jax.ShapeDtypeStruct((512, 896), F32), BLOCK),
        in_specs=[SMEM_SPEC, VMEM_SPEC, VMEM_SPEC],
        out_specs=(VMEM_SPEC, VMEM_SPEC),
        scratch_shapes=[pltpu.VMEM((512, 896), BF), pltpu.VMEM((64, 8, 896), BF), DMA((4,)), DMA((4,)), DMA, DMA],
        compiler_params=params(2),
        name="meet",
    )(order, x, cotangent)


EARLY = 2


def mm(a, b):
    return jnp.dot(a, b, preferred_element_type=F32)


def wide_kernel(
    gn, normed, hid, gg, gu, gy, gn_out, g_out, d_out,
    got, turned, g_src, d_src, g0, d0, g1, d1, x_send, x_recv, send, recv,
):
    dp, t = coords()
    swap = Swap(gn, got, x_send, x_recv, dp, t)
    greet([swap.who] + [partner(d, dp, t) for d in ("core",) + LINKS])
    swap.start()
    turned[...] = normed[...].T
    chains = []

    def advance(n):
        if n < 0 or n >= 15:
            return
        kind, p, c = chains[n]
        c.finish(0, (g0 if kind == "g" else d0).at[p])
        c.start(1, (g0 if kind == "g" else d0).at[p], (g1 if kind == "g" else d1).at[p], send.at[1, n], recv.at[1, n])

    for p in range(5):
        w = 512 if p < 4 else 384
        lanes = pl.ds(512 * p, w)
        for j in range(3):
            n = len(chains)
            if j < 2:
                q, src = 5 * j + p, (gg, gu)[j]
                dst = g_src.at[q]

                def rows(i, carry):
                    at = pl.ds(pl.multiple_of(i * 128, 128), 128)
                    dst[at, pl.ds(0, w)] = mm(turned[at, :], src[:, lanes]).astype(BF)
                    return carry

                lax.fori_loop(0, 7, rows, 0)
                if w < 512:
                    dst[:, pl.ds(w, 512 - w)] = jnp.zeros((896, 512 - w), BF)
                c = Chain(896, 512, G_KINDS, n, dp, t)
                chains.append(("g", q, c))
                c.start(0, dst, g0.at[q], send.at[0, n], recv.at[0, n])
            else:
                dst = d_src.at[p]

                def some(i, carry):
                    at = pl.ds(pl.multiple_of(i * 128, 128), 128)
                    part = hid[:, pl.ds(pl.multiple_of(512 * p + i * 128, 128), 128)]
                    dst[at, :] = mm(part.T, gy[...]).astype(BF)
                    return carry

                lax.fori_loop(0, w // 128, some, 0)
                if w < 512:
                    dst[pl.ds(w, 512 - w), :] = jnp.zeros((512 - w, 896), BF)
                c = Chain(512, 896, D_KINDS, n, dp, t)
                chains.append(("d", p, c))
                c.start(0, dst, d0.at[p], send.at[0, n], recv.at[0, n])
            advance(n - 2)
    advance(13)
    advance(14)
    for i in range(4):
        gn_out[pl.ds(i * 128, 128), :] = swap.take(i)
    for kind, p, c in chains:
        c.finish(1, (g_out if kind == "g" else d_out).at[p])


def wide(gn, normed, hid, gg, gu, gy):
    return pl.pallas_call(
        wide_kernel,
        out_shape=(
            jax.ShapeDtypeStruct((512, 896), F32),
            jax.ShapeDtypeStruct((10, *G_SHAPES[1]), BF),
            jax.ShapeDtypeStruct((5, *D_SHAPES[1]), BF),
        ),
        in_specs=[VMEM_SPEC] * 6,
        out_specs=(VMEM_SPEC,) * 3,
        scratch_shapes=[
            pltpu.VMEM((512, 896), BF),
            pltpu.VMEM((896, 512), BF),
            pltpu.VMEM((10, 896, 512), BF),
            pltpu.VMEM((5, 512, 896), BF),
            pltpu.VMEM((10, *G_SHAPES[0]), BF),
            pltpu.VMEM((5, *D_SHAPES[0]), BF),
            pltpu.VMEM((10, *G_SHAPES[1]), BF),
            pltpu.VMEM((5, *D_SHAPES[1]), BF),
            DMA((4,)), DMA((4,)), DMA((2, 15)), DMA((2, 15)),
        ],
        compiler_params=params(3),
        name="wide",
    )(gn, normed, hid, gg, gu, gy)


def finish_kernel(
    length, g_in, d_in, normed, gq, gkv, mixed, ga, mlp, residual, gn, stream, gain, grad_res, small,
    gate_o, up_o, down_o, query_o, kv_o, out_o, small_o, res_o, gtok_o,
    mlp_got, gn_got, turned, q_src, o_src, k_src, res_buf, gtok_buf, small_buf, small_got,
    g2, g3, g4, g5, d2, d3, d4, d5, q0, q1, q2, q3, q4, q5, o0, o1, o2, o3, o4, o5, k0, k1, k2, k3, k4, k5,
    x_send, x_recv, send, recv, s_send, s_recv, b_send, b_recv,
):
    dp, t = coords()
    me = group_of(dp, t)
    swap_gn = Swap(gn, gn_got, x_send.at[0], x_recv.at[0], dp, t)
    swap_mlp = Swap(mlp, mlp_got, x_send.at[1], x_recv.at[1], dp, t)
    greet_all(dp, t, [swap_gn.who])
    gg, dg = (None, None, g2, g3, g4, g5), (None, None, d2, d3, d4, d5)
    qg, og, kg = (q0, q1, q2, q3, q4, q5), (o0, o1, o2, o3, o4, o5), (k0, k1, k2, k3, k4, k5)
    chains, late = [], []
    for p in range(5):
        for j in range(3):
            n = len(chains)
            if j < 2:
                q = 5 * j + p
                c = Chain(896, 512, G_KINDS, n, dp, t)
                c.bufs = [None, g_in.at[q]] + [r.at[q] for r in gg[2:]]
                c.full, c.base = (gate_o, up_o)[j], (0, 512 * p)
            else:
                c = Chain(512, 896, D_KINDS, n, dp, t)
                c.bufs = [None, d_in.at[p]] + [r.at[p] for r in dg[2:]]
                c.full, c.base = down_o, (512 * p, 0)
            c.n = n
            chains.append(c)
    for i, (c, bufs, full) in enumerate((
        (Chain(896, 512, G_KINDS, 0, dp, t), qg, query_o),
        (Chain(512, 896, D_KINDS, 2, dp, t), og, out_o),
        (Chain(896, 128, K_KINDS, 4, dp, t), kg, kv_o),
    )):
        c.n, c.bufs, c.full, c.base = 15 + i, list(bufs), full, (0, 0)
        late.append(c)

    def go(c, s, src=None):
        c.start(s, c.bufs[s - 1] if src is None else src, c.bufs[s], send.at[c.n, s], recv.at[c.n, s])

    def back(c, s):
        c.gather_start(s, c.full, c.base, send.at[c.n, 6 + s], recv.at[c.n, 6 + s])

    def scattered(c):
        c.spot(6, c.full, c.base)[...] = c.bufs[5][...]
        back(c, c.last)

    def step_of(c, k):
        if k < 6:
            c.finish(k, c.bufs[k])
            if k < 5:
                go(c, k + 1)
            else:
                scattered(c)
        else:
            s = c.last - (k - 6)
            if s < 0:
                return
            c.gather_finish()
            if s > 0:
                back(c, s - 1)

    for c in chains:
        go(c, 2)
    swap_gn.start()
    swap_mlp.start()
    turned[...] = normed[...].T

    def q_rows(i, carry):
        at = pl.ds(pl.multiple_of(i * 128, 128), 128)
        q_src[at, pl.ds(0, 448)] = mm(turned[at, :], gq[...]).astype(BF)
        k_src[at, :] = mm(turned[at, :], gkv[...]).astype(BF)
        return carry

    q_src[:, 448:] = jnp.zeros((896, 64), BF)
    lax.fori_loop(0, 7, q_rows, 0)
    go(late[0], 0, q_src)
    go(late[2], 0, k_src)
    o_src[pl.ds(448, 64), :] = jnp.zeros((64, 896), BF)
    o_src[pl.ds(0, 448), :] = mm(mixed[...].T, ga[...]).astype(BF)
    go(late[1], 0, o_src)

    def tick(k):
        for c in chains:
            step_of(c, k)
        for c in late:
            step_of(c, k - 2)

    def home(buf, dst, i):
        def send_row(k, carry):
            dest = (dp + k) % 64
            remote(buf.at[dest], dst.at[me], b_send.at[i], b_recv.at[i], (dest, t)).start()
            return carry

        lax.fori_loop(1, 64, send_row, 0)
        dst[me] = buf[dp]

    tick(2)
    tick(3)
    tick(4)
    gains = gain[...]
    total = jnp.zeros((8, 896), F32)
    for i in range(4):
        at = pl.ds(i * 128, 128)
        grad = swap_gn.take(i)
        row = stream[at, :].astype(F32)
        inverse = lax.rsqrt(jnp.mean(row * row, axis=-1, keepdims=True) + epsilon)
        unit = row * inverse
        total = total + jnp.sum((grad * unit).reshape(16, 8, 896), axis=0)
        scaled = grad * gains
        mean = jnp.mean(scaled * unit, axis=-1, keepdims=True)
        final = grad_res[at, :] + inverse * (scaled - unit * mean)
        gtok_buf[pl.ds(i * 16, 16)] = final.reshape(16, 8, 896).astype(BF)
    home(gtok_buf, gtok_o, 0)
    small_buf[0] = small[...]
    small_buf[0, 0:1, :] = jnp.sum(total, axis=0, keepdims=True)
    tick(5)
    tick(6)
    squares = [jnp.zeros((8, 896), F32), jnp.zeros((8, 896), F32)]
    for i in range(4):
        at = pl.ds(i * 128, 128)
        valid = lax.broadcasted_iota(jnp.int32, (128, 896), 0) + i * 128 < length[0]
        branch = jnp.where(valid, swap_mlp.take(i), 0.0)
        result = jnp.where(valid, residual[at, :] + branch, 0.0)
        res_buf[pl.ds(i * 16, 16)] = result.reshape(16, 8, 896).astype(BF)
        squares[0] = squares[0] + jnp.sum((result * result).reshape(16, 8, 896), axis=0)
        squares[1] = squares[1] + jnp.sum((branch * branch).reshape(16, 8, 896), axis=0)
    home(res_buf, res_o, 1)
    small_buf[0, 4:5, :] = jnp.sum(squares[0], axis=0, keepdims=True)
    small_buf[0, 5:6, :] = jnp.sum(squares[1], axis=0, keepdims=True)
    dims = ("core",) + LINKS
    for k in range(7, 13):
        s = k - 7
        small_copy = remote(small_buf.at[s], small_got.at[s], s_send.at[s], s_recv.at[s], partner(dims[s], dp, t))
        small_copy.start()
        tick(k)
        small_copy.wait()
        small_buf[s + 1] = small_buf[s] + small_got[s]
    small_o[...] = small_buf[6]
    all_in(gtok_buf, gtok_o, b_send.at[0], b_recv.at[0])
    all_in(res_buf, res_o, b_send.at[1], b_recv.at[1])


def finish(*operands):
    return pl.pallas_call(
        finish_kernel,
        out_shape=(
            jax.ShapeDtypeStruct((896, 2560), BF),
            jax.ShapeDtypeStruct((896, 2560), BF),
            jax.ShapeDtypeStruct((2560, 896), BF),
            jax.ShapeDtypeStruct((896, 512), BF),
            jax.ShapeDtypeStruct((896, 128), BF),
            jax.ShapeDtypeStruct((512, 896), BF),
            jax.ShapeDtypeStruct((8, 896), F32),
            BLOCK,
            BLOCK,
        ),
        in_specs=[SMEM_SPEC] + [VMEM_SPEC] * 14,
        out_specs=(VMEM_SPEC,) * 9,
        scratch_shapes=[
            pltpu.VMEM((512, 896), BF),
            pltpu.VMEM((512, 896), BF),
            pltpu.VMEM((896, 512), BF),
            pltpu.VMEM((896, 512), BF),
            pltpu.VMEM((512, 896), BF),
            pltpu.VMEM((896, 128), BF),
            pltpu.VMEM((64, 8, 896), BF),
            pltpu.VMEM((64, 8, 896), BF),
            pltpu.VMEM((7, 8, 896), F32),
            pltpu.VMEM((6, 8, 896), F32),
            *[pltpu.VMEM((10, *s), BF) for s in G_SHAPES[2:]],
            *[pltpu.VMEM((5, *s), BF) for s in D_SHAPES[2:]],
            *[pltpu.VMEM(s, BF) for s in G_SHAPES],
            *[pltpu.VMEM(s, BF) for s in D_SHAPES],
            *[pltpu.VMEM(s, BF) for s in K_SHAPES],
            DMA((2, 4)), DMA((2, 4)), DMA((18, 12)), DMA((18, 12)), DMA((6,)), DMA((6,)), DMA((2,)), DMA((2,)),
        ],
        compiler_params=params(4),
        name="finish",
    )(*operands)


def unpack_kernel(
    restore, gate, up, down, query, kv, out_w, res, gtok,
    gate_o, up_o, down_o, query_o, key_o, value_o, out_o, res_o, gtok_o,
):
    i = pl.program_id(0)
    rows = pl.ds(pl.multiple_of(i * 112, 16), 112)
    gate_o[...] = gate[rows, pl.ds(0, 2432)].astype(F32)
    up_o[...] = up[rows, pl.ds(0, 2432)].astype(F32)
    down_o[...] = down[pl.ds(pl.multiple_of(i * 304, 16), 304), :].astype(F32)
    query_o[...] = query[rows, pl.ds(0, 448)].astype(F32)
    key_o[...] = kv[rows, pl.ds(0, 64)].astype(F32)
    value_o[...] = kv[rows, pl.ds(64, 64)].astype(F32)

    @pl.when(i < 4)
    def _():
        out_o[...] = out_w[rows, :].astype(F32)

    for j in range(8):
        slot = restore[i * 8 + j]
        res_o[j] = res[slot]
        gtok_o[j] = gtok[slot]


def unpack(*operands):
    whole = lambda i: (i, 0)
    return pl.pallas_call(
        unpack_kernel,
        grid=(8,),
        out_shape=(
            jax.ShapeDtypeStruct((896, 2432), F32),
            jax.ShapeDtypeStruct((896, 2432), F32),
            jax.ShapeDtypeStruct((2432, 896), F32),
            jax.ShapeDtypeStruct((896, 448), F32),
            jax.ShapeDtypeStruct((896, 64), F32),
            jax.ShapeDtypeStruct((896, 64), F32),
            jax.ShapeDtypeStruct((448, 896), F32),
            BLOCK,
            BLOCK,
        ),
        in_specs=[SMEM_SPEC] + [VMEM_SPEC] * 8,
        out_specs=(
            pl.BlockSpec((112, 2432), whole),
            pl.BlockSpec((112, 2432), whole),
            pl.BlockSpec((304, 896), whole),
            pl.BlockSpec((112, 448), whole),
            pl.BlockSpec((112, 64), whole),
            pl.BlockSpec((112, 64), whole),
            pl.BlockSpec((112, 896), lambda i: (jnp.minimum(i, 3), 0)),
            pl.BlockSpec((8, 8, 896), lambda i: (i, 0, 0)),
            pl.BlockSpec((8, 8, 896), lambda i: (i, 0, 0)),
        ),
        compiler_params=pltpu.CompilerParams(vmem_limit_bytes=VMEM_LIMIT),
        name="unpack",
    )(*operands)


def rope_tables(seq_rows, head_size):
    places = jnp.arange(seq_rows).astype(jnp.float32)
    frequency = rope_base ** (-jnp.arange(head_size // 2).astype(jnp.float32) * 2.0 / head_size)
    angles = places[:, None] * frequency[None, :]
    return (jnp.cos(angles)[:, None, :], jnp.sin(angles)[:, None, :])


def rotate(tensor, cos_table, sine_table):
    half_width = tensor.shape[-1] // 2
    first_half = tensor[..., :half_width]
    second_half = tensor[..., half_width:]
    return jnp.concatenate(
        [
            first_half * cos_table - second_half * sine_table,
            second_half * cos_table + first_half * sine_table,
        ],
        axis=-1,
    )


def unrotate(grad_rot, cos_table, sine_table):
    half_width = grad_rot.shape[-1] // 2
    first_half = grad_rot[..., :half_width]
    second_half = grad_rot[..., half_width:]
    return jnp.concatenate(
        [
            first_half * cos_table + second_half * sine_table,
            second_half * cos_table - first_half * sine_table,
        ],
        axis=-1,
    )


def dot_left(matrix, other):
    return lax.dot_general(
        matrix, other, (((0,), (0,)), ((), ())), preferred_element_type=jnp.float32
    )


def dot_right(matrix, other):
    return lax.dot_general(
        matrix, other, (((1,), (1,)), ((), ())), preferred_element_type=jnp.float32
    )


def on_device(
    tokens,
    cotangent,
    lengths,
    deal_order,
    gain_attn,
    w_query,
    b_query,
    w_key,
    b_key,
    w_value,
    b_value,
    w_out,
    gain_mlp,
    w_gate,
    w_up,
    w_down,
):
    slots = jnp.arange(64, dtype=jnp.int32)
    restore = jnp.sum(
        jnp.where(deal_order[None, :] == slots[:, None], slots[None, :], 0), axis=1
    )
    stream_low = dispatch(deal_order, tokens).reshape(512, 896)
    stream = stream_low.astype(jnp.float32)
    seq_rows, width = stream.shape
    head_size = HD
    length = lengths[group_of(*coords())]
    places = jnp.arange(seq_rows)
    usable = places < length
    row_mask = usable[:, None]
    cos_table, sine_table = rope_tables(seq_rows, head_size)
    local_heads = w_query.shape[1] // head_size
    local_kv = w_key.shape[1] // head_size
    group_size = local_heads // local_kv
    score_scale = 1.0 / math.sqrt(head_size)
    allowed = (places[None, :] <= places[:, None]) & usable[None, :]
    gain_one = gain_attn.astype(jnp.float32)
    gain_two = gain_mlp.astype(jnp.float32)
    inverse_one = lax.rsqrt(jnp.mean(stream * stream, axis=-1, keepdims=True) + epsilon)
    normed = (stream * inverse_one * gain_one).astype(jnp.bfloat16)
    q_lin = jnp.dot(normed, w_query, preferred_element_type=jnp.float32) + b_query.astype(
        jnp.float32
    )
    k_lin = jnp.dot(normed, w_key, preferred_element_type=jnp.float32) + b_key.astype(jnp.float32)
    v_lin = jnp.dot(normed, w_value, preferred_element_type=jnp.float32) + b_value.astype(
        jnp.float32
    )
    queries = rotate(q_lin.reshape(seq_rows, local_heads, head_size), cos_table, sine_table).astype(
        jnp.bfloat16
    )
    queries = queries.reshape(seq_rows, local_kv, group_size, head_size)
    keys_rot = rotate(k_lin.reshape(seq_rows, local_kv, head_size), cos_table, sine_table).astype(
        jnp.bfloat16
    )
    values = v_lin.reshape(seq_rows, local_kv, head_size).astype(jnp.bfloat16)
    raw_scores = jnp.einsum("qkgd,pkd->kgqp", queries, keys_rot, preferred_element_type=jnp.float32)
    scores = jnp.where(allowed, raw_scores * score_scale, -1e30)
    top_score = jnp.max(scores, axis=-1, keepdims=True)
    expo = jnp.exp(scores - top_score)
    total = jnp.sum(expo, axis=-1, keepdims=True)
    log_total = top_score + jnp.log(total)
    probs_low = (expo / total).astype(jnp.bfloat16)
    mixed = jnp.einsum("kgqp,pkd->qkgd", probs_low, values, preferred_element_type=jnp.float32)
    mixed = mixed.reshape(seq_rows, local_heads * head_size).astype(jnp.bfloat16)
    attention, grad_out = meet(
        deal_order,
        jnp.dot(mixed, w_out, preferred_element_type=jnp.float32).astype(jnp.bfloat16),
        cotangent,
    )
    grad_out = grad_out.reshape(512, 896).astype(jnp.float32)
    residual = stream + attention
    inverse_two = lax.rsqrt(jnp.mean(residual * residual, axis=-1, keepdims=True) + epsilon)
    normed_two = (residual * inverse_two * gain_two).astype(jnp.bfloat16)
    gate_lin = jnp.dot(normed_two, w_gate, preferred_element_type=jnp.float32)
    up_lin = jnp.dot(normed_two, w_up, preferred_element_type=jnp.float32)
    sigmoid_gate = jax.nn.sigmoid(gate_lin)
    silu_gate = gate_lin * sigmoid_gate
    hidden = (silu_gate * up_lin).astype(jnp.bfloat16)
    mlp_part = jnp.dot(hidden, w_down, preferred_element_type=jnp.float32).astype(jnp.bfloat16)
    attention_squares = jnp.sum(jnp.where(row_mask, attention * attention, 0.0), axis=0)
    grad_y = jnp.where(row_mask, grad_out, 0.0)
    grad_low = grad_y.astype(jnp.bfloat16)
    grad_hidden = dot_right(grad_low, w_down)
    grad_gate = (
        grad_hidden * up_lin * sigmoid_gate * (1.0 + gate_lin * (1.0 - sigmoid_gate))
    ).astype(jnp.bfloat16)
    grad_up = (grad_hidden * silu_gate).astype(jnp.bfloat16)
    grad_normed_two, g_part, d_part = wide(
        (dot_right(grad_gate, w_gate) + dot_right(grad_up, w_up)).astype(jnp.bfloat16),
        normed_two,
        hidden,
        grad_gate,
        grad_up,
        grad_low,
    )
    grad_gain_mlp = jnp.sum(grad_normed_two * residual * inverse_two, axis=0)
    scaled_two = grad_normed_two * gain_two
    grad_resid = (
        grad_y
        + inverse_two * scaled_two
        - residual * inverse_two**3 * jnp.mean(scaled_two * residual, axis=-1, keepdims=True)
    )
    grad_attn = grad_resid.astype(jnp.bfloat16)
    grad_mixed = dot_right(grad_attn, w_out).astype(jnp.bfloat16)
    grad_mixed = grad_mixed.reshape(seq_rows, local_kv, group_size, head_size)
    probs = jnp.exp(scores - log_total)
    grad_probs = jnp.einsum(
        "qkgd,pkd->kgqp", grad_mixed, values, preferred_element_type=jnp.float32
    )
    grad_values = jnp.einsum(
        "kgqp,qkgd->pkd", probs_low, grad_mixed, preferred_element_type=jnp.float32
    )
    row_inner = jnp.sum(probs * grad_probs, axis=-1, keepdims=True)
    grad_scores = (probs * (grad_probs - row_inner) * score_scale).astype(jnp.bfloat16)
    grad_queries = jnp.einsum(
        "kgqp,pkd->qkgd", grad_scores, keys_rot, preferred_element_type=jnp.float32
    )
    grad_keys = jnp.einsum(
        "kgqp,qkgd->pkd", grad_scores, queries, preferred_element_type=jnp.float32
    )
    grad_q_lin = unrotate(
        grad_queries.reshape(seq_rows, local_heads, head_size), cos_table, sine_table
    )
    grad_q_lin = grad_q_lin.reshape(seq_rows, local_heads * head_size).astype(jnp.bfloat16)
    grad_k_lin = (
        unrotate(grad_keys, cos_table, sine_table)
        .reshape(seq_rows, local_kv * head_size)
        .astype(jnp.bfloat16)
    )
    grad_v_lin = grad_values.reshape(seq_rows, local_kv * head_size).astype(jnp.bfloat16)
    grad_b_query = jnp.sum(grad_q_lin.astype(jnp.float32), axis=0)
    grad_b_key = jnp.sum(grad_k_lin.astype(jnp.float32), axis=0)
    grad_b_value = jnp.sum(grad_v_lin.astype(jnp.float32), axis=0)
    grad_normed = (
        dot_right(grad_q_lin, w_query) + dot_right(grad_k_lin, w_key) + dot_right(grad_v_lin, w_value)
    ).astype(jnp.bfloat16)
    biases = jnp.concatenate([grad_b_query, grad_b_key, grad_b_value, jnp.zeros((320,), jnp.float32)])
    blank = jnp.zeros((896,), jnp.float32)
    small = jnp.stack([blank, grad_gain_mlp, biases, attention_squares, blank, blank, blank, blank])
    gate, up, down, query, kv, out_w, small, sent_res, sent_tok = finish(
        length[None],
        g_part,
        d_part,
        normed,
        grad_q_lin,
        jnp.concatenate([grad_k_lin, grad_v_lin], axis=1),
        mixed,
        grad_attn,
        mlp_part,
        residual,
        grad_normed,
        stream_low,
        gain_one[None],
        grad_resid,
        small,
    )
    (
        grad_w_gate,
        grad_w_up,
        grad_w_down,
        grad_w_query,
        grad_w_key,
        grad_w_value,
        grad_w_out,
        layer_out,
        grad_tokens,
    ) = unpack(restore, gate, up, down, query, kv, out_w, sent_res, sent_tok)
    grad_gain_attn, grad_gain_mlp = small[0], small[1]
    grad_b_query, grad_b_key, grad_b_value = small[2, :448], small[2, 448:512], small[2, 512:576]
    statistics = jnp.stack([jnp.sum(small[4]), jnp.sum(small[3]), jnp.sum(small[5])])
    count = jnp.sum(lengths).astype(jnp.float32) * width
    rms_values = jnp.sqrt(statistics / count)
    return (
        layer_out,
        grad_tokens,
        grad_gain_attn,
        grad_w_query,
        grad_b_query,
        grad_w_key,
        grad_b_key,
        grad_w_value,
        grad_b_value,
        grad_w_out,
        grad_gain_mlp,
        grad_w_gate,
        grad_w_up,
        grad_w_down,
        rms_values,
    )


def solution(mesh):
    in_specs = (
        P(None, "dp", None),
        P(None, "dp", None),
        P(),
        P(),
        P(),
        P(None, "tensor"),
        P("tensor"),
        P(None, "tensor"),
        P("tensor"),
        P(None, "tensor"),
        P("tensor"),
        P("tensor", None),
        P(),
        P(None, "tensor"),
        P(None, "tensor"),
        P("tensor", None),
    )
    out_specs = (
        P(None, "dp", None),
        P(None, "dp", None),
        P(),
        P(None, "tensor"),
        P("tensor"),
        P(None, "tensor"),
        P("tensor"),
        P(None, "tensor"),
        P("tensor"),
        P("tensor", None),
        P(),
        P(None, "tensor"),
        P(None, "tensor"),
        P("tensor", None),
        P(),
    )
    return jax.shard_map(
        on_device, mesh=mesh, in_specs=in_specs, out_specs=out_specs, check_vma=False
    )
```

```python
import functools
import math

import jax
import jax.numpy as jnp
import numpy as np
from jax import lax
from jax.experimental import pallas as pl
from jax.experimental.pallas import tpu as pltpu
from jax.sharding import PartitionSpec as P

MESH = pl.DeviceIdType.MESH
HD = 64
epsilon = 1e-06
rope_base = 1000000.0
VMEM_LIMIT = 60 << 20
LINKS = ("x", "ya", "za", "yb", "zb")


def flip(dp):
    return dp + 8 - 16 * ((dp // 8) % 2)


def group_of(dp, t):
    return dp + t * (flip(dp) - dp)


def coords():
    return lax.axis_index("dp"), lax.axis_index("tensor")


def partner(dim, dp, t):
    y, xl, z, c = dp // 16, (dp // 8) % 2, (dp // 2) % 4, dp % 2
    if dim == "core":
        c = 1 - c
    if dim == "x":
        xl = 1 - xl
    if dim == "ya":
        y = y + 1 - 2 * (y % 2)
    if dim == "yb":
        y = 3 - y
    if dim == "za":
        z = z + 1 - 2 * (z % 2)
    if dim == "zb":
        z = 3 - z
    if dim == "tn":
        xl, t = 1 - xl, 1 - t
    return (((y * 2 + xl) * 4 + z) * 2 + c, t)


def bit(dim, dp):
    y, xl, z, c = dp // 16, (dp // 8) % 2, (dp // 2) % 4, dp % 2
    return {
        "core": c,
        "x": xl,
        "ya": ((y + 1) // 2) % 2,
        "yb": y // 2,
        "za": ((z + 1) // 2) % 2,
        "zb": z // 2,
    }[dim]


def greet(partners):
    barrier = pltpu.get_barrier_semaphore()
    for who in partners:
        pl.semaphore_signal(barrier, inc=1, device_id=who, device_id_type=MESH)


def around(dp, t, axis, j):
    a, b = dp // 8, dp % 8
    return (((a + j) % 8 * 8 + b) if axis == 0 else a * 8 + (b + j) % 8, t)


def neighbours(dp, t):
    return [around(dp, t, axis, j) for axis in range(2) for j in range(1, 8)]


def met(n):
    pl.semaphore_wait(pltpu.get_barrier_semaphore(), n)


def remote(src, dst, send, recv, who):
    return pltpu.make_async_remote_copy(
        src_ref=src, dst_ref=dst, send_sem=send, recv_sem=recv, device_id=who, device_id_type=MESH
    )


def put_sum(dst, src, row, lane, other, rows, lanes):
    step = 16
    while step * 2 * lanes <= 32768 and rows % (step * 2) == 0:
        step *= 2

    def body(i, carry):
        here = pl.ds(pl.multiple_of(i * step, 16), step)
        there = pl.ds(pl.multiple_of(row + i * step, 16), step)
        lane_at = lane if isinstance(lane, int) else pl.multiple_of(lane, 128)
        dst[here, :] = src[there, pl.ds(lane_at, lanes)] + other[here, :]
        return carry

    lax.fori_loop(0, rows // step, body, 0)


def halves(rows, lanes, kinds):
    out = []
    for kind in kinds:
        if kind == "r":
            rows //= 2
        elif kind == "l":
            lanes //= 2
        out.append((rows, lanes))
    return out


class Chain:
    def __init__(self, rows, lanes, kinds, turn, dp, t):
        self.kinds = kinds
        self.dims = ("core",) + tuple(LINKS[(turn + i) % 5] for i in range(5))
        self.who = [partner(d, dp, t) for d in self.dims]
        self.bits = [bit(d, dp) for d in self.dims]
        self.shapes = [(rows, lanes)] + halves(rows, lanes, kinds)
        self.last = max(i for i, kind in enumerate(kinds) if kind != "f")
        self.corner = [(0, 0)]
        for s, kind in enumerate(kinds):
            row, lane = self.corner[-1]
            rows, lanes = self.shapes[s + 1]
            b = self.bits[s]
            self.corner.append((row + (b * rows if kind == "r" else 0), lane + (b * lanes if kind == "l" else 0)))

    def start(self, s, src, got, send, recv):
        rows, lanes = self.shapes[s + 1]
        give, self.keep = (0, 0), (0, 0)
        b = self.bits[s]
        if self.kinds[s] == "r":
            give, self.keep = (pl.multiple_of((1 - b) * rows, 16), 0), (b * rows, 0)
        elif self.kinds[s] == "l":
            give, self.keep = (0, pl.multiple_of((1 - b) * lanes, 128)), (0, b * lanes)
        self.src, self.got = src, got
        self.copy = remote(src.at[pl.ds(give[0], rows), pl.ds(give[1], lanes)], got, send, recv, self.who[s])
        self.copy.start()

    def finish(self, s, dst):
        self.copy.wait()
        rows, lanes = self.shapes[s + 1]
        put_sum(dst, self.src, self.keep[0], self.keep[1], self.got, rows, lanes)

    def spot(self, s, full, base):
        rows, lanes = self.shapes[s]
        row, lane = self.corner[s]
        row, lane = row + base[0], lane + base[1]
        row = row if isinstance(row, int) else pl.multiple_of(row, 16)
        lane = lane if isinstance(lane, int) else pl.multiple_of(lane, 128)
        return full.at[pl.ds(row, rows), pl.ds(lane, lanes)]

    def gather_start(self, s, full, base, send, recv):
        mine = self.spot(s + 1, full, base)
        self.copy = remote(mine, mine, send, recv, self.who[s])
        self.copy.start()

    def gather_finish(self):
        self.copy.wait()


G_KINDS = ("l", "l", "r", "r", "r", "f")
D_KINDS = ("r", "r", "r", "r", "r", "f")
K_KINDS = ("r", "r", "r", "f", "f", "f")
ANY_SPEC = pl.BlockSpec(memory_space=pl.ANY)
G_SHAPES = halves(896, 512, G_KINDS)
D_SHAPES = halves(512, 896, D_KINDS)
K_SHAPES = halves(128, 896, K_KINDS)
BF, F32 = jnp.bfloat16, jnp.float32
VMEM_SPEC = pl.BlockSpec(memory_space=pltpu.VMEM)
SMEM_SPEC = pl.BlockSpec(memory_space=pltpu.SMEM)
BLOCK = jax.ShapeDtypeStruct((64, 8, 896), BF)
DMA = pltpu.SemaphoreType.DMA


def params(cid):
    return pltpu.CompilerParams(collective_id=cid, has_side_effects=True, vmem_limit_bytes=VMEM_LIMIT)


class Mail:
    LOW = 512

    def __init__(self, buf, mids, out, spot, send, recv, dp, t):
        self.buf, self.mids, self.out = buf, mids, out
        self.me = (dp // 8, dp % 8)
        self.spot = spot
        self.send, self.recv, self.dp, self.t = send, recv, dp, t
        self.lanes = (pl.ds(0, self.LOW), pl.ds(self.LOW, 896 - self.LOW))

    def first(self):
        self.copies = [[], []]
        for j in range(1, 8):
            for f in range(2):
                to = (self.me[f] + j) % 8
                src = self.buf.at[to, :, :, self.lanes[f]] if f == 0 else self.buf.at[:, to, :, self.lanes[f]]
                c = remote(src, self.mids[f].at[self.spot[f]], self.send.at[0, f, j], self.recv.at[0, f, j],
                           around(self.dp, self.t, f, j))
                c.start()
                self.copies[f].append(c)
        for f in range(2):
            me = self.me[f]
            own = self.buf[me, :, :, self.lanes[f]] if f == 0 else self.buf[:, me, :, self.lanes[f]]
            self.mids[f][self.spot[f]] = own

    def second(self):
        for f in range(2):
            for c in self.copies[f]:
                c.wait()
        self.copies = []
        for j in range(1, 8):
            for f in range(2):
                g = 1 - f
                to = (self.me[g] + j) % 8
                dst = self.out.at[:, self.spot[1], :, self.lanes[f]] if f == 0 else self.out.at[self.spot[0], :, :, self.lanes[f]]
                c = remote(self.mids[f].at[:, to], dst, self.send.at[1, f, j], self.recv.at[1, f, j],
                           around(self.dp, self.t, g, j))
                c.start()
                self.copies.append(c)
        for f in range(2):
            own = self.mids[f][:, self.me[1 - f]]
            if f == 0:
                self.out[:, self.spot[1], :, self.lanes[f]] = own
            else:
                self.out[self.spot[0], :, :, self.lanes[f]] = own

    def last(self):
        for c in self.copies:
            c.wait()


MAIL = jax.ShapeDtypeStruct((8, 8, 8, 896), BF)
MAIL_SCRATCH = [
    pltpu.VMEM((8, 8, 8, 896), BF), pltpu.VMEM((8, 8, 8, 512), BF), pltpu.VMEM((8, 8, 8, 384), BF),
    DMA((2, 2, 8)), DMA((2, 2, 8)),
]


def sort_out(order, rows, buf, dp, t):
    for a in range(8):
        for b in range(8):
            buf[a, b] = rows[order[group_of(a * 8 + b, t)]]


def dispatch_kernel(order, tok, out, buf, mid0, mid1, send, recv):
    dp, t = coords()
    greet(neighbours(dp, t))
    sort_out(order, tok, buf, dp, t)
    mail = Mail(buf, (mid0, mid1), out, (dp // 8, dp % 8), send, recv, dp, t)
    met(14)
    mail.first()
    mail.second()
    mail.last()


def dispatch(order, tokens):
    return pl.pallas_call(
        dispatch_kernel,
        out_shape=MAIL,
        in_specs=[SMEM_SPEC, VMEM_SPEC],
        out_specs=VMEM_SPEC,
        scratch_shapes=MAIL_SCRATCH,
        compiler_params=params(1),
        name="dispatch",
    )(order, tokens)


def mm(a, b):
    return jnp.dot(a, b, preferred_element_type=F32)


def mm_t(a, b):
    return lax.dot_general(a, b, (((1,), (1,)), ((), ())), preferred_element_type=F32)


def t_mm(a, b):
    return lax.dot_general(a, b, (((0,), (0,)), ((), ())), preferred_element_type=F32)


def rope_table():
    places = np.arange(512, dtype=np.float32)
    frequency = np.power(np.float32(rope_base), -np.arange(32, dtype=np.float32) * np.float32(2.0 / HD)).astype(np.float32)
    angles = (places[:, None] * frequency[None, :]).astype(np.float64)
    cos, sin = np.cos(angles), np.sin(angles)
    return np.concatenate([cos, cos, sin, sin], axis=1).astype(np.float32)


def first_half(shape):
    return lax.broadcasted_iota(jnp.int32, shape, 1) % 64 < 32


def spread(table):
    other = pltpu.roll(table, 64, 1)
    low = lax.broadcasted_iota(jnp.int32, table.shape, 1) < 64
    cos, sin = jnp.where(low, table, other), jnp.where(low, other, table)
    return cos, jnp.where(first_half(table.shape), -sin, sin)


def turn(x, cos, sin):
    swapped = jnp.where(first_half(x.shape), pltpu.roll(x, 96, 1), pltpu.roll(x, 32, 1))
    return x * cos + swapped * sin


def one_head(pair, side):
    low = lax.broadcasted_iota(jnp.int32, pair.shape, 1) < 64
    return jnp.where(low if side == 0 else jnp.logical_not(low), pair, jnp.zeros_like(pair))


def fill_mask(mask, length):
    for b in range(2):
        rows = lax.broadcasted_iota(jnp.int32, (256, 512), 0) + b * 256
        cols = lax.broadcasted_iota(jnp.int32, (256, 512), 1)
        mask[pl.ds(b * 256, 256), :] = jnp.where((cols <= rows) & (cols < length), 0.0, -1e30)


class Swap:
    def __init__(self, x, got, send, recv, dp, t):
        self.who = partner("tn", dp, t)
        self.x, self.got, self.send, self.recv = x, got, send, recv
        self.copies = [None] * 4

    def start(self, i):
        rows = pl.ds(i * 128, 128)
        self.copies[i] = remote(self.x.at[rows], self.got.at[rows], self.send.at[i], self.recv.at[i], self.who)
        self.copies[i].start()

    def take(self, i):
        self.copies[i].wait()
        rows = pl.ds(i * 128, 128)
        return self.x[rows, :].astype(F32) + self.got[rows, :].astype(F32)


def meet_kernel(
    order, lengths, stream, cot, wq, wk, wv, wo, vecs, table,
    normed, q_o, k_o, v_o, lse_o, mixed, residual, normed_two, gy, squares,
    sides, mask, x, got, cot_in, send, recv, buf, mid0, mid1, c_send, c_recv,
):
    dp, t = coords()
    swap = Swap(x, got, send, recv, dp, t)
    mail = Mail(buf, (mid0, mid1), cot_in, (dp // 8, dp % 8), c_send, c_recv, dp, t)
    greet(neighbours(dp, t) + [swap.who])
    length = lengths[group_of(dp, t)]
    sort_out(order, cot, buf, dp, t)
    for i in range(4):
        at = pl.ds(i * 128, 128)
        row = stream[at, :].astype(F32)
        inverse = lax.rsqrt(jnp.mean(row * row, axis=-1, keepdims=True) + epsilon)
        normed[at, :] = (row * inverse * vecs[0:1, :]).astype(BF)
    fill_mask(mask, length)
    cos, sin = spread(table[...])
    k = mm_t(normed[...], wk[...]) + vecs[2:3, 448:512]
    v = mm_t(normed[...], wv[...]) + vecs[2:3, 512:576]
    k2 = turn(jnp.concatenate([k, k], axis=1), cos, sin)
    k_o[...] = (k2.astype(BF).astype(F32) * 0.125).astype(BF)
    v_o[...] = jnp.concatenate([v, v], axis=1).astype(BF)
    for side in range(2):
        sides[side] = one_head(k_o[...], side)
        sides[2 + side] = one_head(v_o[...], side)
    met(15)
    mail.first()
    for p in range(4):
        w = 128 if p < 3 else 64
        lanes = pl.ds(128 * p, w)
        q = mm_t(normed[...], wq[lanes, :]) + vecs[2:3, lanes]
        if w < 128:
            q = jnp.concatenate([q, jnp.zeros((512, 64), F32)], axis=1)
        q_o[:, pl.ds(128 * p, 128)] = turn(q, cos, sin).astype(BF)
    for b in range(2):
        rows, keys = pl.ds(256 * b, 256), pl.ds(0, 256 * (b + 1))
        lse_o[rows, :] = jnp.zeros((256, 128), F32)

        def heads(p, both):
            lanes = pl.ds(pl.multiple_of(128 * p, 128), 128)
            pair = q_o[rows, lanes]
            total = jnp.zeros((256, 128), F32)
            for side in range(2 if both else 1):
                score = mm_t(pair, sides[side, keys, :]) + mask[rows, keys]
                top = jnp.max(score, axis=-1, keepdims=True)
                expo = jnp.exp(score - top)
                mass = jnp.sum(expo, axis=-1, keepdims=True)
                probs = (expo * (1.0 / mass)).astype(BF)
                total = total + mm(probs, sides[2 + side, keys, :])
                here = lax.broadcasted_iota(jnp.int32, (256, 128), 1) == 2 * p + side
                lse_o[rows, :] = jnp.where(here, top + jnp.log(mass), lse_o[rows, :])
            mixed[rows, lanes] = total.astype(BF)

        def body(p, carry):
            heads(p, True)
            return carry

        lax.fori_loop(0, 3, body, 0)
        heads(3, False)
        x[rows, :] = mm(mixed[rows, pl.ds(0, 448)], wo[...]).astype(BF)
        swap.start(2 * b)
        swap.start(2 * b + 1)
        if b == 0:
            mail.second()
    total = jnp.zeros((8, 896), F32)
    for i in range(4):
        at = pl.ds(i * 128, 128)
        valid = lax.broadcasted_iota(jnp.int32, (128, 896), 0) + i * 128 < length
        attention = swap.take(i)
        res = stream[at, :].astype(F32) + attention
        residual[at, :] = res
        inverse = lax.rsqrt(jnp.mean(res * res, axis=-1, keepdims=True) + epsilon)
        normed_two[at, :] = (res * inverse * vecs[1:2, :]).astype(BF)
        kept = jnp.where(valid, attention, 0.0)
        total = total + jnp.sum((kept * kept).reshape(16, 8, 896), axis=0)
    squares[...] = total
    mail.last()
    for i in range(4):
        at = pl.ds(i * 128, 128)
        valid = lax.broadcasted_iota(jnp.int32, (128, 896), 0) + i * 128 < length
        gy[at, :] = jnp.where(valid, cot_in[pl.ds(i * 2, 2)].astype(F32).reshape(128, 896), 0.0).astype(BF)


def meet(*operands):
    rows = jax.ShapeDtypeStruct((512, 896), BF)
    wide_rows = jax.ShapeDtypeStruct((512, 512), BF)
    pair = jax.ShapeDtypeStruct((512, 128), BF)
    return pl.pallas_call(
        meet_kernel,
        out_shape=(
            rows, wide_rows, pair, pair, jax.ShapeDtypeStruct((512, 128), F32), wide_rows,
            jax.ShapeDtypeStruct((512, 896), F32), rows, rows, jax.ShapeDtypeStruct((8, 896), F32),
        ),
        in_specs=[SMEM_SPEC] * 2 + [VMEM_SPEC] * 8,
        out_specs=(VMEM_SPEC,) * 10,
        scratch_shapes=[
            pltpu.VMEM((4, 512, 128), BF),
            pltpu.VMEM((512, 512), F32),
            pltpu.VMEM((512, 896), BF),
            pltpu.VMEM((512, 896), BF),
            pltpu.VMEM((8, 8, 8, 896), BF),
            DMA((4,)), DMA((4,)), *MAIL_SCRATCH,
        ],
        compiler_params=params(2),
        name="meet",
    )(*operands)


MORE = {10: 0, 11: 0, 12: 1, 13: 2, 14: 1}


def tile(p):
    return pl.ds(512 * p, 512 if p < 4 else 384)


def wide_kernel(
    normed, gy, w_gate, w_up, w_down, gn_out, mlp_out, g_out, d_out, g_more, d_more,
    gn_total, mlp_total, gn, got, hid, gg, gu, gate_w, up_w, down_w, g_src, d_src, g0, d0, g1, d1,
    x_send, x_recv, send, recv, local,
):
    dp, t = coords()
    swap = Swap(gn, got, x_send, x_recv, dp, t)
    greet([swap.who] + [partner(d, dp, t) for d in ("core",) + LINKS])
    loads = []

    def load(p):
        at, w = tile(p), 512 if p < 4 else 384
        b = p % 2
        copies = [
            pltpu.make_async_copy(w_gate.at[:, at], gate_w.at[b, :, pl.ds(0, w)], local.at[p, 0]),
            pltpu.make_async_copy(w_up.at[:, at], up_w.at[b, :, pl.ds(0, w)], local.at[p, 1]),
            pltpu.make_async_copy(w_down.at[at, :], down_w.at[b, pl.ds(0, w), :], local.at[p, 2]),
        ]
        for c in copies:
            c.start()
        loads.append(copies)

    load(0)
    load(1)
    for p in range(5):
        at, w, b = tile(p), 512 if p < 4 else 384, p % 2
        for c in loads[p]:
            c.wait()
        wg, wu, wd = gate_w.at[b, :, pl.ds(0, w)], up_w.at[b, :, pl.ds(0, w)], down_w.at[b, pl.ds(0, w), :]
        gate = mm(normed[...], wg[...])
        up = mm(normed[...], wu[...])
        back = mm_t(gy[...], wd[...])
        sig = 1.0 / (1.0 + jnp.exp(-gate))
        silu = gate * sig
        hid[:, at] = (silu * up).astype(BF)
        gu[:, at] = (back * silu).astype(BF)
        gg[:, at] = (back * up * sig * (1.0 + gate * (1.0 - sig))).astype(BF)
        mlp = mm(hid[:, at], wd[...])
        grad = mm_t(gg[:, at], wg[...]) + mm_t(gu[:, at], wu[...])
        if p == 0:
            mlp_total[...] = mlp
            gn_total[...] = grad
        elif p < 4:
            mlp_total[...] += mlp
            gn_total[...] += grad
        else:
            mlp_out[...] = (mlp_total[...] + mlp).astype(BF)
            gn[...] = (gn_total[...] + grad).astype(BF)
        if p + 2 < 5:
            load(p + 2)
    met(7)
    for i in range(4):
        swap.start(i)
    chains = []

    def advance(n):
        if n < 0 or n >= 15:
            return
        kind, p, c = chains[n]
        if n in MORE:
            c.finish(0, (g_more if kind == "g" else d_more).at[MORE[n]])
            return
        c.finish(0, (g0 if kind == "g" else d0).at[p])
        c.start(1, (g0 if kind == "g" else d0).at[p], (g1 if kind == "g" else d1).at[p], send.at[1, n], recv.at[1, n])

    for p in range(5):
        w = 512 if p < 4 else 384
        for j in range(3):
            n = len(chains)
            if j < 2:
                q, src = 5 * j + p, (gg, gu)[j]
                dst = g_src.at[q]
                dst[:, pl.ds(0, w)] = t_mm(normed[...], src[:, tile(p)]).astype(BF)
                if w < 512:
                    dst[:, pl.ds(w, 512 - w)] = jnp.zeros((896, 512 - w), BF)
                c = Chain(896, 512, G_KINDS, n, dp, t)
                chains.append(("g", q, c))
                c.start(0, dst, g0.at[q], send.at[0, n], recv.at[0, n])
            else:
                dst = d_src.at[p]
                dst[pl.ds(0, w), :] = t_mm(hid[:, tile(p)], gy[...]).astype(BF)
                if w < 512:
                    dst[pl.ds(w, 512 - w), :] = jnp.zeros((512 - w, 896), BF)
                c = Chain(512, 896, D_KINDS, n, dp, t)
                chains.append(("d", p, c))
                c.start(0, dst, d0.at[p], send.at[0, n], recv.at[0, n])
            advance(n - 2)
    advance(13)
    advance(14)
    for i in range(4):
        gn_out[pl.ds(i * 128, 128), :] = swap.take(i)
    for n, (kind, p, c) in enumerate(chains):
        if n not in MORE:
            c.finish(1, (g_out if kind == "g" else d_out).at[p])


def wide(*operands):
    return pl.pallas_call(
        wide_kernel,
        out_shape=(
            jax.ShapeDtypeStruct((512, 896), F32),
            jax.ShapeDtypeStruct((512, 896), BF),
            jax.ShapeDtypeStruct((10, *G_SHAPES[1]), BF),
            jax.ShapeDtypeStruct((5, *D_SHAPES[1]), BF),
            jax.ShapeDtypeStruct((3, *G_SHAPES[0]), BF),
            jax.ShapeDtypeStruct((2, *D_SHAPES[0]), BF),
        ),
        in_specs=[VMEM_SPEC] * 2 + [ANY_SPEC] * 3,
        out_specs=(VMEM_SPEC,) * 6,
        scratch_shapes=[
            pltpu.VMEM((512, 896), F32),
            pltpu.VMEM((512, 896), F32),
            pltpu.VMEM((512, 896), BF),
            pltpu.VMEM((512, 896), BF),
            pltpu.VMEM((512, 2432), BF),
            pltpu.VMEM((512, 2432), BF),
            pltpu.VMEM((512, 2432), BF),
            pltpu.VMEM((2, 896, 512), BF),
            pltpu.VMEM((2, 896, 512), BF),
            pltpu.VMEM((2, 512, 896), BF),
            pltpu.VMEM((10, 896, 512), BF),
            pltpu.VMEM((5, 512, 896), BF),
            pltpu.VMEM((10, *G_SHAPES[0]), BF),
            pltpu.VMEM((5, *D_SHAPES[0]), BF),
            pltpu.VMEM((10, *G_SHAPES[1]), BF),
            pltpu.VMEM((5, *D_SHAPES[1]), BF),
            DMA((4,)), DMA((4,)), DMA((2, 15)), DMA((2, 15)), DMA((5, 3)),
        ],
        compiler_params=params(3),
        name="wide",
    )(*operands)


class Message:
    def __init__(self, link, size):
        self.link, self.size, self.lands = link, size, None


class Plan:
    LATENCY = 2.2
    RATE = {"core": 600e3, "tn": 46e3}

    def __init__(self):
        self.tasks = []

    def add(self, act, cost, after=(), needs=(), sends=(), rank=5):
        task = dict(act=act, cost=cost, after=list(after), needs=list(needs), sends=list(sends), rank=rank, done=False)
        self.tasks.append(task)
        return task

    def run(self):
        now, free = 0.0, {}
        left = list(self.tasks)
        while left:
            open_ = [x for x in left if all(y["done"] for y in x["after"]) and all(m.lands is not None for m in x["needs"])]
            at = {id(x): max([now] + [m.lands for m in x["needs"]]) for x in open_}
            ready = [x for x in open_ if at[id(x)] <= now]
            task = min(ready, key=lambda x: x["rank"]) if ready else min(open_, key=lambda x: at[id(x)])
            now = at[id(task)] + task["cost"]
            task["act"]()
            task["done"] = True
            left.remove(task)
            for m in task["sends"]:
                links = LINKS if m.link == "all" else (m.link,)
                for link in links:
                    begin = max(now, free.get(link, 0.0))
                    free[link] = begin + m.size / len(links) / self.RATE.get(link, 46e3)
                m.lands = max(free[link] for link in links) + self.LATENCY
        return now


def finish_kernel(
    lengths, g_in, d_in, g_more, d_more, normed, q_in, k_in, v_in, lse, mixed, mlp, residual, gn2, gy, stream,
    wq, wk, wv, wo, vecs, table, squares,
    gate_o, up_o, down_o, query_o, kv_o, out_o, small_o, res_o, gtok_o,
    mlp_got, gn, gn_got, sides, mask, ga, gm, gq, gk_t, gv_t, grad_res,
    q_src, o_src, k_src, small_buf, small_got,
    g1, d1, g2, g3, g4, g5, d2, d3, d4, d5, q0, q1, q2, q3, q4, q5, o0, o1, o2, o3, o4, o5, k0, k1, k2, k3, k4, k5,
    x_send, x_recv, send, recv, s_send, s_recv,
    r_buf, r_mid0, r_mid1, r_send, r_recv, t_buf, t_mid0, t_mid1, t_send, t_recv,
):
    dp, t = coords()
    spot = (dp // 8 + t * (1 - 2 * (dp // 8 % 2)), dp % 8)
    length = lengths[group_of(dp, t)]
    swap_gn = Swap(gn, gn_got, x_send.at[0], x_recv.at[0], dp, t)
    swap_mlp = Swap(mlp, mlp_got, x_send.at[1], x_recv.at[1], dp, t)
    mail_res = Mail(r_buf, (r_mid0, r_mid1), res_o, spot, r_send, r_recv, dp, t)
    mail_tok = Mail(t_buf, (t_mid0, t_mid1), gtok_o, spot, t_send, t_recv, dp, t)
    across = (partner("x", *partner("core", dp, t)))
    greet(neighbours(dp, t) + [swap_gn.who, across])
    plan = Plan()
    qg, og, kg = (q0, q1, q2, q3, q4, q5), (o0, o1, o2, o3, o4, o5), (k0, k1, k2, k3, k4, k5)
    chains = []
    for p in range(5):
        for j in range(3):
            n = len(chains)
            if j < 2:
                q = 5 * j + p
                c = Chain(896, 512, G_KINDS, n, dp, t)
                bufs = [g_more.at[MORE[n]], g1.at[MORE[n]]] if n in MORE else [None, g_in.at[q]]
                c.bufs = bufs + [r.at[q] for r in (g2, g3, g4, g5)]
                c.full, c.base = (gate_o, up_o)[j], (0, 512 * p)
            else:
                c = Chain(512, 896, D_KINDS, n, dp, t)
                bufs = [d_more.at[MORE[n]], d1.at[MORE[n]]] if n in MORE else [None, d_in.at[p]]
                c.bufs = bufs + [r.at[p] for r in (d2, d3, d4, d5)]
                c.full, c.base = down_o, (512 * p, 0)
            c.n = n
            chains.append(c)
    late = []
    for i, (c, bufs, full) in enumerate((
        (Chain(512, 896, D_KINDS, 0, dp, t), qg, query_o),
        (Chain(512, 896, D_KINDS, 2, dp, t), og, out_o),
        (Chain(128, 896, K_KINDS, 4, dp, t), kg, kv_o),
    )):
        c.n, c.bufs, c.full, c.base = 15 + i, list(bufs), full, (0, 0)
        late.append(c)

    def follow(c, s, src, begin, rank):
        def go(s, src=None):
            c.start(s, c.bufs[s - 1] if src is None else src, c.bufs[s], send.at[c.n, s], recv.at[c.n, s])

        def back(s):
            c.gather_start(s, c.full, c.base, send.at[c.n, 6 + s], recv.at[c.n, 6 + s])

        def size(s):
            return 2.0 * c.shapes[s + 1][0] * c.shapes[s + 1][1]

        message = Message(c.dims[s], size(s))
        task = plan.add(functools.partial(go, s, src), 0.1, begin, sends=[message], rank=rank)
        for k in range(s, 6):
            def step(k=k):
                c.finish(k, c.bufs[k])
                if k < 5:
                    go(k + 1)
                else:
                    c.spot(6, c.full, c.base)[...] = c.bufs[5][...]
                    back(c.last)

            after = Message(c.dims[k + 1], size(k + 1)) if k < 5 else Message(c.dims[c.last], size(c.last))
            task = plan.add(step, 0.1 + size(k) / 2e6, [task], [message], [after], rank)
            message = after
        for k in range(c.last, -1, -1):
            def step(k=k):
                c.gather_finish()
                if k > 0:
                    back(k - 1)

            after = Message(c.dims[k - 1], size(k - 1))
            task = plan.add(step, 0.1, [task], [message], [after] if k > 0 else [], rank)
            message = after

    meeting = plan.add(lambda: met(16), 0.5, rank=9)
    for c in chains:
        first = 1 if c.n in MORE else 2
        follow(c, first, None, [meeting], 4)
    swapped = [Message("tn", 128 * 896 * 2.0) for _ in range(4)]
    sent = plan.add(lambda: [swap_mlp.start(j) for j in range(4)], 0.2, [meeting], sends=swapped, rank=3)

    def norm_two(i):
        at = pl.ds(i * 128, 128)
        res, grad = residual[at, :], gn2[at, :]
        inverse = lax.rsqrt(jnp.mean(res * res, axis=-1, keepdims=True) + epsilon)
        unit = res * inverse
        total = jnp.sum((grad * unit).reshape(16, 8, 896), axis=0)
        scaled = grad * vecs[1:2, :]
        mean = jnp.mean(scaled * unit, axis=-1, keepdims=True)
        final = gy[at, :].astype(F32) + inverse * (scaled - unit * mean)
        grad_res[at, :] = final
        ga[at, :] = final.astype(BF)
        if i == 0:
            small_buf[0] = jnp.zeros((8, 896), F32)
        small_buf[0, 1:2, :] += jnp.sum(total, axis=0, keepdims=True)

    normed_back = [plan.add(functools.partial(norm_two, i), 0.6, rank=5) for i in range(4)]

    def prepare():
        fill_mask(mask, length)
        for side in range(2):
            sides[side] = one_head(k_in[...], side)
            sides[2 + side] = one_head(v_in[...], side)
        gk_t[...] = jnp.zeros((64, 512), F32)
        gv_t[...] = jnp.zeros((64, 512), F32)

    prepared = plan.add(prepare, 0.6, rank=5)

    def out_back():
        gm[:, pl.ds(384, 128)] = jnp.zeros((512, 128), BF)
        gm[:, pl.ds(0, 448)] = mm_t(ga[...], wo[...]).astype(BF)

    mixed_back = plan.add(out_back, 0.8, normed_back, rank=5)

    def heads(b, p):
        rows, keys = pl.ds(256 * b, 256), pl.ds(0, 256 * (b + 1))
        lanes = pl.ds(128 * p, 128)
        cos, sin = spread(table[rows, :])
        pair, pair_gm = q_in[rows, lanes], gm[rows, lanes]
        pair_t, pair_gm_t = pair.T, pair_gm.T
        grad = jnp.zeros((256, 128), F32)
        for side in range(2 if p < 3 else 1):
            h = 2 * p + side
            score = mm_t(pair, sides[side, keys, :]) + mask[rows, keys]
            probs = jnp.exp(score - lse[rows, h : h + 1])
            grad_probs = mm_t(pair_gm, sides[2 + side, keys, :])
            inner = jnp.sum(probs * grad_probs, axis=-1, keepdims=True)
            grad_scores = (probs * (grad_probs - inner)).astype(BF)
            grad = grad + mm(grad_scores, sides[side, keys, :])
            half = slice(64 * side, 64 * side + 64)
            gk_t[:, keys] += mm(pair_t[half, :], grad_scores)
            gv_t[:, keys] += mm(pair_gm_t[half, :], probs.astype(BF))
        gq[rows, lanes] = turn(grad, cos, -sin).astype(BF)

    key_grads = [None, None]

    def norm_part(b):
        rows = pl.ds(256 * b, 256)
        flat = table[rows, :].T
        cos_t, sin_t = flat[0:32], flat[64:96]
        one, two = gk_t[0:32, rows] * 0.125, gk_t[32:64, rows] * 0.125
        whole = jnp.concatenate([one * cos_t + two * sin_t, two * cos_t - one * sin_t, gv_t[:, rows]], axis=0).astype(BF)
        gkv = whole.T
        key_grads[b] = (whole, jnp.sum(gkv.astype(F32), axis=0, keepdims=True))
        part = mm(gq[rows, pl.ds(0, 448)], wq[...]) + mm(gkv[:, 0:64], wk[...]) + mm(gkv[:, 64:128], wv[...])
        gn[rows, :] = part.astype(BF)
        swap_gn.start(2 * b)
        swap_gn.start(2 * b + 1)

    returned = [Message("tn", 128 * 896 * 2.0) for _ in range(4)]
    before, parts = [prepared, mixed_back], [None, None]
    for b in (1, 0):
        before = [plan.add(functools.partial(heads, b, p), (1.0 + b) * (1.0 if p < 3 else 0.5), before, rank=5) for p in range(4)][-1:]
        parts[b] = plan.add(functools.partial(norm_part, b), 1.0, before + [meeting], sends=returned[2 * b : 2 * b + 2], rank=5)
        before = [parts[b]]

    def make_kv():
        whole = jnp.concatenate([key_grads[0][0], key_grads[1][0]], axis=1)
        k_src[...] = mm(whole, normed[...]).astype(BF)
        small_buf[0, 2:3, 0:448] = jnp.sum(gq[:, pl.ds(0, 448)].astype(F32), axis=0, keepdims=True)
        small_buf[0, 2:3, 512:640] = key_grads[0][1] + key_grads[1][1]
        small_buf[0, 3:4, :] = jnp.sum(squares[...], axis=0, keepdims=True)

    def make_q():
        q_src[...] = t_mm(gq[...], normed[...]).astype(BF)

    def make_o():
        o_src[...] = t_mm(mixed[...], ga[...]).astype(BF)

    made_q = plan.add(make_q, 0.8, [parts[0]], rank=5)
    made_kv = plan.add(make_kv, 0.6, [parts[0]], rank=5)
    made_o = plan.add(make_o, 0.8, [mixed_back], rank=6)
    follow(late[0], 0, q_src, [made_q, meeting], 2)
    follow(late[2], 0, k_src, [made_kv, meeting], 2)
    follow(late[1], 0, o_src, [made_o, meeting], 2)

    def output(i):
        at = pl.ds(i * 128, 128)
        valid = lax.broadcasted_iota(jnp.int32, (128, 896), 0) + i * 128 < length
        branch = jnp.where(valid, swap_mlp.take(i), 0.0)
        result = jnp.where(valid, residual[at, :] + branch, 0.0)
        r_buf[pl.ds(i * 2, 2)] = result.reshape(2, 8, 8, 896).astype(BF)
        for row, x in ((4, result), (5, branch)):
            some = jnp.sum((x * x).reshape(16, 8, 896), axis=0)
            small_buf[0, row : row + 1, :] += jnp.sum(some, axis=0, keepdims=True)

    outputs = [plan.add(functools.partial(output, i), 0.5, [sent] + normed_back, swapped[i : i + 1], rank=6) for i in range(4)]

    def post(mail, ready, rank):
        one, two = Message("all", 2 * 458752.0), Message("all", 2 * 458752.0)
        a = plan.add(mail.first, 0.8, ready, sends=[one], rank=rank)
        b = plan.add(mail.second, 0.9, [a], [one], [two], rank)
        plan.add(mail.last, 0.2, [b], [two], rank=rank)

    post(mail_res, outputs + [meeting], 6)

    def norm_one(i):
        at = pl.ds(i * 128, 128)
        grad = swap_gn.take(i)
        row = stream[at, :].astype(F32)
        inverse = lax.rsqrt(jnp.mean(row * row, axis=-1, keepdims=True) + epsilon)
        unit = row * inverse
        total = jnp.sum((grad * unit).reshape(16, 8, 896), axis=0)
        scaled = grad * vecs[0:1, :]
        mean = jnp.mean(scaled * unit, axis=-1, keepdims=True)
        final = grad_res[at, :] + inverse * (scaled - unit * mean)
        t_buf[pl.ds(i * 2, 2)] = final.reshape(2, 8, 8, 896).astype(BF)
        small_buf[0, 0:1, :] += jnp.sum(total, axis=0, keepdims=True)

    finals = [plan.add(functools.partial(norm_one, i), 0.6, [parts[i // 2]], returned[i : i + 1], rank=1) for i in range(4)]
    post(mail_tok, finals, 0)

    def quartet(s):
        if s == 0:
            return [partner("core", dp, t), partner("x", dp, t), across]
        one, two = ("ya", "yb") if s == 1 else ("za", "zb")
        return [partner(one, dp, t), partner(two, dp, t), partner(one, *partner(two, dp, t))]

    posted = {}

    def share(s):
        posted[s] = [
            remote(small_buf.at[s], small_got.at[3 * s + i], s_send.at[3 * s + i], s_recv.at[3 * s + i], who)
            for i, who in enumerate(quartet(s))
        ]
        for c in posted[s]:
            c.start()

    def collect(s):
        for c in posted[s]:
            c.wait()
        small_buf[s + 1] = (small_buf[s] + small_got[3 * s]) + (small_got[3 * s + 1] + small_got[3 * s + 2])
        if s < 2:
            share(s + 1)
        else:
            small_o[...] = small_buf[3]

    message = Message("x", 28672.0)
    task = plan.add(functools.partial(share, 0), 0.2, finals + outputs + [made_kv], sends=[message], rank=1)
    for s in range(3):
        after = Message(("ya", "za", "za")[s], 28672.0)
        task = plan.add(functools.partial(collect, s), 0.2, [task], [message], [after] if s < 2 else [], rank=1)
        message = after
    plan.run()


def finish(*operands):
    return pl.pallas_call(
        finish_kernel,
        out_shape=(
            jax.ShapeDtypeStruct((896, 2560), BF),
            jax.ShapeDtypeStruct((896, 2560), BF),
            jax.ShapeDtypeStruct((2560, 896), BF),
            jax.ShapeDtypeStruct((512, 896), BF),
            jax.ShapeDtypeStruct((128, 896), BF),
            jax.ShapeDtypeStruct((512, 896), BF),
            jax.ShapeDtypeStruct((8, 896), F32),
            MAIL,
            MAIL,
        ),
        in_specs=[SMEM_SPEC] + [VMEM_SPEC] * 22,
        out_specs=(VMEM_SPEC,) * 9,
        scratch_shapes=[
            pltpu.VMEM((512, 896), BF),
            pltpu.VMEM((512, 896), BF),
            pltpu.VMEM((512, 896), BF),
            pltpu.VMEM((4, 512, 128), BF),
            pltpu.VMEM((512, 512), F32),
            pltpu.VMEM((512, 896), BF),
            pltpu.VMEM((512, 512), BF),
            pltpu.VMEM((512, 512), BF),
            pltpu.VMEM((64, 512), F32),
            pltpu.VMEM((64, 512), F32),
            pltpu.VMEM((512, 896), F32),
            pltpu.VMEM((512, 896), BF),
            pltpu.VMEM((512, 896), BF),
            pltpu.VMEM((128, 896), BF),
            pltpu.VMEM((4, 8, 896), F32),
            pltpu.VMEM((9, 8, 896), F32),
            pltpu.VMEM((3, *G_SHAPES[1]), BF),
            pltpu.VMEM((2, *D_SHAPES[1]), BF),
            *[pltpu.VMEM((10, *s), BF) for s in G_SHAPES[2:]],
            *[pltpu.VMEM((5, *s), BF) for s in D_SHAPES[2:]],
            *[pltpu.VMEM(s, BF) for s in D_SHAPES],
            *[pltpu.VMEM(s, BF) for s in D_SHAPES],
            *[pltpu.VMEM(s, BF) for s in K_SHAPES],
            DMA((2, 4)), DMA((2, 4)), DMA((18, 12)), DMA((18, 12)), DMA((9,)), DMA((9,)), *MAIL_SCRATCH, *MAIL_SCRATCH,
        ],
        compiler_params=params(4),
        name="finish",
    )(*operands)


def unpack_kernel(
    order, lengths, gate, up, down, query, kv, out_w, small, res, gtok,
    gate_o, up_o, down_o, query_o, key_o, value_o, out_o, res_o, gtok_o, small_o,
    where_from,
):
    i = pl.program_id(0)

    @pl.when(i == 0)
    def _():
        def note(g, carry):
            where_from[order[g]] = g
            return carry + lengths[g]

        count = lax.fori_loop(0, 64, note, 0).astype(F32) * 896.0
        sums = jnp.sum(small[...], axis=-1, keepdims=True)
        small_o[...] = small[...]
        small_o[3:6, 0:128] = jnp.broadcast_to(jnp.sqrt(sums[3:6] / count), (3, 128))

    rows = pl.ds(pl.multiple_of(i * 64, 64), 64)
    gate_o[...] = gate[rows, pl.ds(0, 2432)].astype(F32)
    up_o[...] = up[rows, pl.ds(0, 2432)].astype(F32)
    down_o[...] = down[pl.ds(pl.multiple_of(i * 176, 16), 176), :].astype(F32)

    @pl.when(i < 7)
    def _():
        query_o[...] = query[rows, :].astype(F32)
        out_o[...] = out_w[rows, :].astype(F32)

    @pl.when(i == 0)
    def _():
        key_o[...] = kv[pl.ds(0, 64), :].astype(F32)
        value_o[...] = kv[pl.ds(64, 64), :].astype(F32)

    @pl.when(i < 8)
    def _():
        for j in range(8):
            slot = where_from[jnp.minimum(i, 7) * 8 + j]
            res_o[j] = res[slot]
            gtok_o[j] = gtok[slot]


def unpack(*operands):
    return pl.pallas_call(
        unpack_kernel,
        grid=(14,),
        out_shape=(
            jax.ShapeDtypeStruct((896, 2432), F32),
            jax.ShapeDtypeStruct((896, 2432), F32),
            jax.ShapeDtypeStruct((2432, 896), F32),
            jax.ShapeDtypeStruct((448, 896), F32),
            jax.ShapeDtypeStruct((64, 896), F32),
            jax.ShapeDtypeStruct((64, 896), F32),
            jax.ShapeDtypeStruct((448, 896), F32),
            BLOCK,
            BLOCK,
            jax.ShapeDtypeStruct((8, 896), F32),
        ),
        in_specs=[SMEM_SPEC] * 2 + [VMEM_SPEC] * 9,
        out_specs=(
            pl.BlockSpec((64, 2432), lambda i: (i, 0)),
            pl.BlockSpec((64, 2432), lambda i: (i, 0)),
            pl.BlockSpec((176, 896), lambda i: (i, 0)),
            pl.BlockSpec((64, 896), lambda i: (jnp.minimum(i, 6), 0)),
            pl.BlockSpec((64, 896), lambda i: (0, 0)),
            pl.BlockSpec((64, 896), lambda i: (0, 0)),
            pl.BlockSpec((64, 896), lambda i: (jnp.minimum(i, 6), 0)),
            pl.BlockSpec((8, 8, 896), lambda i: (jnp.minimum(i, 7), 0, 0)),
            pl.BlockSpec((8, 8, 896), lambda i: (jnp.minimum(i, 7), 0, 0)),
            pl.BlockSpec((8, 896), lambda i: (0, 0)),
        ),
        scratch_shapes=[pltpu.SMEM((64,), jnp.int32)],
        compiler_params=pltpu.CompilerParams(vmem_limit_bytes=VMEM_LIMIT),
        name="unpack",
    )(*operands)


def on_device(
    tokens,
    cotangent,
    lengths,
    deal_order,
    gain_attn,
    w_query,
    b_query,
    w_key,
    b_key,
    w_value,
    b_value,
    w_out,
    gain_mlp,
    w_gate,
    w_up,
    w_down,
):
    table = jnp.asarray(rope_table())
    biases = jnp.concatenate([b_query, b_key, b_value, jnp.zeros((320,), BF)])
    blank = jnp.zeros((896,), BF)
    vecs = jnp.stack([gain_attn, gain_mlp, biases] + [blank] * 5).astype(F32)
    stream = dispatch(deal_order, tokens).reshape(512, 896)
    normed, q, k, v, lse, mixed, residual, normed_two, gy, squares = meet(
        deal_order, lengths, stream, cotangent, w_query.T, w_key.T, w_value.T, w_out, vecs, table
    )
    gn2, mlp, g_part, d_part, g_more, d_more = wide(normed_two, gy, w_gate, w_up, w_down)
    gate, up, down, query, kv, out_w, small, sent_res, sent_tok = finish(
        lengths, g_part, d_part, g_more, d_more, normed, q, k, v, lse, mixed, mlp, residual, gn2, gy, stream,
        w_query.T, w_key.T, w_value.T, w_out, vecs, table, squares,
    )
    gate, up, down, query, key, value, out_w, layer_out, grad_tokens, small = unpack(
        deal_order, lengths, gate, up, down, query, kv, out_w, small,
        sent_res.reshape(64, 8, 896), sent_tok.reshape(64, 8, 896),
    )
    rms_values = jnp.stack([small[4, 0], small[3, 0], small[5, 0]])
    return (
        layer_out,
        grad_tokens,
        small[0],
        query.T,
        small[2, :448],
        key.T,
        small[2, 512:576],
        value.T,
        small[2, 576:640],
        out_w,
        small[1],
        gate,
        up,
        down,
        rms_values,
    )


def solution(mesh):
    in_specs = (
        P(None, "dp", None),
        P(None, "dp", None),
        P(),
        P(),
        P(),
        P(None, "tensor"),
        P("tensor"),
        P(None, "tensor"),
        P("tensor"),
        P(None, "tensor"),
        P("tensor"),
        P("tensor", None),
        P(),
        P(None, "tensor"),
        P(None, "tensor"),
        P("tensor", None),
    )
    out_specs = (
        P(None, "dp", None),
        P(None, "dp", None),
        P(),
        P(None, "tensor"),
        P("tensor"),
        P(None, "tensor"),
        P("tensor"),
        P(None, "tensor"),
        P("tensor"),
        P("tensor", None),
        P(),
        P(None, "tensor"),
        P(None, "tensor"),
        P("tensor", None),
        P(),
    )
    return jax.shard_map(
        on_device, mesh=mesh, in_specs=in_specs, out_specs=out_specs, check_vma=False
    )
```

```python
import functools
import math

import jax
import jax.numpy as jnp
import numpy as np
from jax import lax
from jax.experimental import pallas as pl
from jax.experimental.pallas import tpu as pltpu
from jax.sharding import PartitionSpec as P

MESH = pl.DeviceIdType.MESH
HD = 64
epsilon = 1e-06
rope_base = 1000000.0
VMEM_LIMIT = 60 << 20
LINKS = ("x", "ya", "za", "yb", "zb")


def flip(dp):
    return dp + 8 - 16 * ((dp // 8) % 2)


def group_of(dp, t):
    return dp + t * (flip(dp) - dp)


def coords():
    return lax.axis_index("dp"), lax.axis_index("tensor")


def partner(dim, dp, t):
    y, xl, z, c = dp // 16, (dp // 8) % 2, (dp // 2) % 4, dp % 2
    if dim == "core":
        c = 1 - c
    if dim == "x":
        xl = 1 - xl
    if dim == "ya":
        y = y + 1 - 2 * (y % 2)
    if dim == "yb":
        y = 3 - y
    if dim == "za":
        z = z + 1 - 2 * (z % 2)
    if dim == "zb":
        z = 3 - z
    if dim == "tn":
        xl, t = 1 - xl, 1 - t
    return (((y * 2 + xl) * 4 + z) * 2 + c, t)


def bit(dim, dp):
    y, xl, z, c = dp // 16, (dp // 8) % 2, (dp // 2) % 4, dp % 2
    return {
        "core": c,
        "x": xl,
        "ya": ((y + 1) // 2) % 2,
        "yb": y // 2,
        "za": ((z + 1) // 2) % 2,
        "zb": z // 2,
    }[dim]


def greet(partners):
    barrier = pltpu.get_barrier_semaphore()
    for who in partners:
        pl.semaphore_signal(barrier, inc=1, device_id=who, device_id_type=MESH)


def around(dp, t, axis, j):
    a, b = dp // 8, dp % 8
    return (((a + j) % 8 * 8 + b) if axis == 0 else a * 8 + (b + j) % 8, t)


def neighbours(dp, t):
    return [around(dp, t, axis, j) for axis in range(2) for j in range(1, 8)]


def met(n):
    pl.semaphore_wait(pltpu.get_barrier_semaphore(), n)


def remote(src, dst, send, recv, who):
    return pltpu.make_async_remote_copy(
        src_ref=src, dst_ref=dst, send_sem=send, recv_sem=recv, device_id=who, device_id_type=MESH
    )


def put_sum(dst, src, row, lane, other, rows, lanes):
    step = 16
    while step * 2 * lanes <= 32768 and rows % (step * 2) == 0:
        step *= 2

    def body(i, carry):
        here = pl.ds(pl.multiple_of(i * step, 16), step)
        there = pl.ds(pl.multiple_of(row + i * step, 16), step)
        lane_at = lane if isinstance(lane, int) else pl.multiple_of(lane, 128)
        dst[here, :] = src[there, pl.ds(lane_at, lanes)] + other[here, :]
        return carry

    lax.fori_loop(0, rows // step, body, 0)


def halves(rows, lanes, kinds):
    out = []
    for kind in kinds:
        if kind == "r":
            rows //= 2
        elif kind == "l":
            lanes //= 2
        out.append((rows, lanes))
    return out


class Chain:
    def __init__(self, rows, lanes, kinds, turn, dp, t):
        self.kinds = kinds
        self.dims = ("core",) + tuple(LINKS[(turn + i) % 5] for i in range(5))
        self.who = [partner(d, dp, t) for d in self.dims]
        self.bits = [bit(d, dp) for d in self.dims]
        self.shapes = [(rows, lanes)] + halves(rows, lanes, kinds)
        self.last = max(i for i, kind in enumerate(kinds) if kind != "f")
        self.corner = [(0, 0)]
        for s, kind in enumerate(kinds):
            row, lane = self.corner[-1]
            rows, lanes = self.shapes[s + 1]
            b = self.bits[s]
            self.corner.append((row + (b * rows if kind == "r" else 0), lane + (b * lanes if kind == "l" else 0)))

    def start(self, s, src, got, send, recv):
        rows, lanes = self.shapes[s + 1]
        give, self.keep = (0, 0), (0, 0)
        b = self.bits[s]
        if self.kinds[s] == "r":
            give, self.keep = (pl.multiple_of((1 - b) * rows, 16), 0), (b * rows, 0)
        elif self.kinds[s] == "l":
            give, self.keep = (0, pl.multiple_of((1 - b) * lanes, 128)), (0, b * lanes)
        self.src, self.got = src, got
        self.copy = remote(src.at[pl.ds(give[0], rows), pl.ds(give[1], lanes)], got, send, recv, self.who[s])
        self.copy.start()

    def finish(self, s, dst):
        self.copy.wait()
        rows, lanes = self.shapes[s + 1]
        put_sum(dst, self.src, self.keep[0], self.keep[1], self.got, rows, lanes)

    def spot(self, s, full, base):
        rows, lanes = self.shapes[s]
        row, lane = self.corner[s]
        row, lane = row + base[0], lane + base[1]
        row = row if isinstance(row, int) else pl.multiple_of(row, 16)
        lane = lane if isinstance(lane, int) else pl.multiple_of(lane, 128)
        return full.at[pl.ds(row, rows), pl.ds(lane, lanes)]

    def gather_start(self, s, full, base, send, recv):
        mine = self.spot(s + 1, full, base)
        self.copy = remote(mine, mine, send, recv, self.who[s])
        self.copy.start()

    def gather_finish(self):
        self.copy.wait()


G_KINDS = ("l", "l", "r", "r", "r", "f")
D_KINDS = ("r", "r", "r", "r", "r", "f")
K_KINDS = ("r", "r", "r", "f", "f", "f")
ANY_SPEC = pl.BlockSpec(memory_space=pl.ANY)
G_SHAPES = halves(896, 512, G_KINDS)
D_SHAPES = halves(512, 896, D_KINDS)
K_SHAPES = halves(128, 896, K_KINDS)
BF, F32 = jnp.bfloat16, jnp.float32
VMEM_SPEC = pl.BlockSpec(memory_space=pltpu.VMEM)
SMEM_SPEC = pl.BlockSpec(memory_space=pltpu.SMEM)
BLOCK = jax.ShapeDtypeStruct((64, 8, 896), BF)
DMA = pltpu.SemaphoreType.DMA


def params(cid, limit=VMEM_LIMIT):
    return pltpu.CompilerParams(collective_id=cid, has_side_effects=True, vmem_limit_bytes=limit)


class Mail:
    LOW = 512

    def __init__(self, buf, mids, out, spot, send, recv, dp, t):
        self.buf, self.mids, self.out = buf, mids, out
        self.me = (dp // 8, dp % 8)
        self.spot = spot
        self.send, self.recv, self.dp, self.t = send, recv, dp, t
        self.lanes = (pl.ds(0, self.LOW), pl.ds(self.LOW, 896 - self.LOW))

    def first(self):
        self.copies = [[], []]
        for j in range(1, 8):
            for f in range(2):
                to = (self.me[f] + j) % 8
                src = self.buf.at[to, :, :, self.lanes[f]] if f == 0 else self.buf.at[:, to, :, self.lanes[f]]
                c = remote(src, self.mids[f].at[self.spot[f]], self.send.at[0, f, j], self.recv.at[0, f, j],
                           around(self.dp, self.t, f, j))
                c.start()
                self.copies[f].append(c)
        for f in range(2):
            me = self.me[f]
            own = self.buf[me, :, :, self.lanes[f]] if f == 0 else self.buf[:, me, :, self.lanes[f]]
            self.mids[f][self.spot[f]] = own

    def second(self):
        for f in range(2):
            for c in self.copies[f]:
                c.wait()
        self.copies = []
        for j in range(1, 8):
            for f in range(2):
                g = 1 - f
                to = (self.me[g] + j) % 8
                dst = self.out.at[:, self.spot[1], :, self.lanes[f]] if f == 0 else self.out.at[self.spot[0], :, :, self.lanes[f]]
                c = remote(self.mids[f].at[:, to], dst, self.send.at[1, f, j], self.recv.at[1, f, j],
                           around(self.dp, self.t, g, j))
                c.start()
                self.copies.append(c)
        for f in range(2):
            own = self.mids[f][:, self.me[1 - f]]
            if f == 0:
                self.out[:, self.spot[1], :, self.lanes[f]] = own
            else:
                self.out[self.spot[0], :, :, self.lanes[f]] = own

    def last(self):
        for c in self.copies:
            c.wait()


MAIL = jax.ShapeDtypeStruct((8, 8, 8, 896), BF)
MAIL_SCRATCH = [
    pltpu.VMEM((8, 8, 8, 896), BF), pltpu.VMEM((8, 8, 8, 512), BF), pltpu.VMEM((8, 8, 8, 384), BF),
    DMA((2, 2, 8)), DMA((2, 2, 8)),
]


def sort_out(order, rows, buf, dp, t):
    for a in range(8):
        for b in range(8):
            buf[a, b] = rows[order[group_of(a * 8 + b, t)]]


def mm(a, b):
    return jnp.dot(a, b, preferred_element_type=F32)


def mm_t(a, b):
    return lax.dot_general(a, b, (((1,), (1,)), ((), ())), preferred_element_type=F32)


def t_mm(a, b):
    return lax.dot_general(a, b, (((0,), (0,)), ((), ())), preferred_element_type=F32)


def rope_table():
    places = np.arange(512, dtype=np.float32)
    frequency = np.power(np.float32(rope_base), -np.arange(32, dtype=np.float32) * np.float32(2.0 / HD)).astype(np.float32)
    angles = (places[:, None] * frequency[None, :]).astype(np.float64)
    cos, sin = np.cos(angles), np.sin(angles)
    return np.concatenate([cos, cos, sin, sin], axis=1).astype(np.float32)


def first_half(shape):
    return lax.broadcasted_iota(jnp.int32, shape, 1) % 64 < 32


def spread(table):
    other = pltpu.roll(table, 64, 1)
    low = lax.broadcasted_iota(jnp.int32, table.shape, 1) < 64
    cos, sin = jnp.where(low, table, other), jnp.where(low, other, table)
    return cos, jnp.where(first_half(table.shape), -sin, sin)


def turn(x, cos, sin):
    swapped = jnp.where(first_half(x.shape), pltpu.roll(x, 96, 1), pltpu.roll(x, 32, 1))
    return x * cos + swapped * sin


def one_head(pair, side):
    low = lax.broadcasted_iota(jnp.int32, pair.shape, 1) < 64
    return jnp.where(low if side == 0 else jnp.logical_not(low), pair, jnp.zeros_like(pair))


def fill_mask(mask, length):
    for b in range(2):
        rows = lax.broadcasted_iota(jnp.int32, (256, 512), 0) + b * 256
        cols = lax.broadcasted_iota(jnp.int32, (256, 512), 1)
        mask[pl.ds(b * 256, 256), :] = jnp.where((cols <= rows) & (cols < length), 0.0, -1e30)


class Swap:
    def __init__(self, x, got, send, recv, dp, t):
        self.who = partner("tn", dp, t)
        self.x, self.got, self.send, self.recv = x, got, send, recv
        self.copies = [None] * 4

    def start(self, i):
        rows = pl.ds(i * 128, 128)
        self.copies[i] = remote(self.x.at[rows], self.got.at[rows], self.send.at[i], self.recv.at[i], self.who)
        self.copies[i].start()

    def take(self, i):
        self.copies[i].wait()
        rows = pl.ds(i * 128, 128)
        return self.x[rows, :].astype(F32) + self.got[rows, :].astype(F32)


def meet_kernel(
    order, lengths, tok, cot, wq, wk, wv, wo, vecs, table,
    normed, q_o, k_o, v_o, lse_o, mixed, residual, normed_two, gy, squares, stream,
    sides, mask, x, got, tok_in, cot_in, send, recv, buf, mid0, mid1, c_send, c_recv, t_buf, t_mid0, t_mid1, t_send, t_recv,
):
    dp, t = coords()
    swap = Swap(x, got, send, recv, dp, t)
    mail = Mail(buf, (mid0, mid1), cot_in, (dp // 8, dp % 8), c_send, c_recv, dp, t)
    greet(neighbours(dp, t) + [swap.who])
    length = lengths[group_of(dp, t)]
    sort_out(order, tok, t_buf, dp, t)
    tokens = Mail(t_buf, (t_mid0, t_mid1), tok_in, (dp // 8, dp % 8), t_send, t_recv, dp, t)
    met(15)
    tokens.first()
    sort_out(order, cot, buf, dp, t)
    fill_mask(mask, length)
    cos, sin = spread(table[...])
    tokens.second()
    tokens.last()
    mail.first()
    for i in range(4):
        at = pl.ds(i * 128, 128)
        row = tok_in[pl.ds(i * 2, 2)].astype(F32).reshape(128, 896)
        stream[at, :] = row.astype(BF)
        inverse = lax.rsqrt(jnp.mean(row * row, axis=-1, keepdims=True) + epsilon)
        normed[at, :] = (row * inverse * vecs[0:1, :]).astype(BF)
    k = mm_t(normed[...], wk[...]) + vecs[2:3, 448:512]
    v = mm_t(normed[...], wv[...]) + vecs[2:3, 512:576]
    k2 = turn(jnp.concatenate([k, k], axis=1), cos, sin)
    k_o[...] = (k2.astype(BF).astype(F32) * 0.125).astype(BF)
    v_o[...] = jnp.concatenate([v, v], axis=1).astype(BF)
    for side in range(2):
        sides[side] = one_head(k_o[...], side)
        sides[2 + side] = one_head(v_o[...], side)
    for p in range(4):
        w = 128 if p < 3 else 64
        lanes = pl.ds(128 * p, w)
        q = mm_t(normed[...], wq[lanes, :]) + vecs[2:3, lanes]
        if w < 128:
            q = jnp.concatenate([q, jnp.zeros((512, 64), F32)], axis=1)
        q_o[:, pl.ds(128 * p, 128)] = turn(q, cos, sin).astype(BF)
    for b in range(2):
        rows, keys = pl.ds(256 * b, 256), pl.ds(0, 256 * (b + 1))
        lse_o[rows, :] = jnp.zeros((256, 128), F32)

        def heads(p, both):
            lanes = pl.ds(pl.multiple_of(128 * p, 128), 128)
            pair = q_o[rows, lanes]
            total = jnp.zeros((256, 128), F32)
            for side in range(2 if both else 1):
                score = mm_t(pair, sides[side, keys, :]) + mask[rows, keys]
                top = jnp.max(score, axis=-1, keepdims=True)
                expo = jnp.exp(score - top)
                mass = jnp.sum(expo, axis=-1, keepdims=True)
                probs = (expo * (1.0 / mass)).astype(BF)
                total = total + mm(probs, sides[2 + side, keys, :])
                here = lax.broadcasted_iota(jnp.int32, (256, 128), 1) == 2 * p + side
                lse_o[rows, :] = jnp.where(here, top + jnp.log(mass), lse_o[rows, :])
            mixed[rows, lanes] = total.astype(BF)

        def body(p, carry):
            heads(p, True)
            return carry

        lax.fori_loop(0, 3, body, 0)
        heads(3, False)
        x[rows, :] = mm(mixed[rows, pl.ds(0, 448)], wo[...]).astype(BF)
        swap.start(2 * b)
        swap.start(2 * b + 1)
        if b == 0:
            mail.second()
    total = jnp.zeros((8, 896), F32)
    for i in range(4):
        at = pl.ds(i * 128, 128)
        valid = lax.broadcasted_iota(jnp.int32, (128, 896), 0) + i * 128 < length
        attention = swap.take(i)
        res = stream[at, :].astype(F32) + attention
        residual[at, :] = res
        inverse = lax.rsqrt(jnp.mean(res * res, axis=-1, keepdims=True) + epsilon)
        normed_two[at, :] = (res * inverse * vecs[1:2, :]).astype(BF)
        kept = jnp.where(valid, attention, 0.0)
        total = total + jnp.sum((kept * kept).reshape(16, 8, 896), axis=0)
    squares[...] = total
    mail.last()
    for i in range(4):
        at = pl.ds(i * 128, 128)
        valid = lax.broadcasted_iota(jnp.int32, (128, 896), 0) + i * 128 < length
        gy[at, :] = jnp.where(valid, cot_in[pl.ds(i * 2, 2)].astype(F32).reshape(128, 896), 0.0).astype(BF)


def meet(*operands):
    rows = jax.ShapeDtypeStruct((512, 896), BF)
    wide_rows = jax.ShapeDtypeStruct((512, 512), BF)
    pair = jax.ShapeDtypeStruct((512, 128), BF)
    return pl.pallas_call(
        meet_kernel,
        out_shape=(
            rows, wide_rows, pair, pair, jax.ShapeDtypeStruct((512, 128), F32), wide_rows,
            jax.ShapeDtypeStruct((512, 896), F32), rows, rows, jax.ShapeDtypeStruct((8, 896), F32), rows,
        ),
        in_specs=[SMEM_SPEC] * 2 + [VMEM_SPEC] * 8,
        out_specs=(VMEM_SPEC,) * 11,
        scratch_shapes=[
            pltpu.VMEM((4, 512, 128), BF),
            pltpu.VMEM((512, 512), F32),
            pltpu.VMEM((512, 896), BF),
            pltpu.VMEM((512, 896), BF),
            pltpu.VMEM((8, 8, 8, 896), BF),
            pltpu.VMEM((8, 8, 8, 896), BF),
            DMA((4,)), DMA((4,)), *MAIL_SCRATCH, *MAIL_SCRATCH,
        ],
        compiler_params=params(2),
        name="meet",
    )(*operands)


class Message:
    def __init__(self, link, size):
        self.link, self.size, self.lands = link, size, None


class Plan:
    LATENCY = 2.2
    RATE = {"core": 600e3, "tn": 46e3}

    def __init__(self):
        self.tasks = []

    def add(self, act, cost, after=(), needs=(), sends=(), rank=5):
        task = dict(act=act, cost=cost, after=list(after), needs=list(needs), sends=list(sends), rank=rank, done=False)
        self.tasks.append(task)
        return task

    def run(self):
        now, free = 0.0, {}
        left = list(self.tasks)
        while left:
            open_ = [x for x in left if all(y["done"] for y in x["after"]) and all(m.lands is not None for m in x["needs"])]
            at = {id(x): max([now] + [m.lands for m in x["needs"]]) for x in open_}
            ready = [x for x in open_ if at[id(x)] <= now]
            task = min(ready, key=lambda x: x["rank"]) if ready else min(open_, key=lambda x: at[id(x)])
            now = at[id(task)] + task["cost"]
            task["act"]()
            task["done"] = True
            left.remove(task)
            for m in task["sends"]:
                links = LINKS if m.link == "all" else (m.link,)
                for link in links:
                    begin = max(now, free.get(link, 0.0))
                    free[link] = begin + m.size / len(links) / self.RATE.get(link, 46e3)
                m.lands = max(free[link] for link in links) + self.LATENCY
        return now


def follow(plan, c, first, last, begin, rank, up=False):
    def go(s):
        c.start(s, c.bufs[s - 1], c.gots[s], c.send.at[s], c.recv.at[s])

    def back(s):
        c.gather_start(s, c.full, c.base, c.send.at[6 + s], c.recv.at[6 + s])

    def size(s):
        return 2.0 * c.shapes[s + 1][0] * c.shapes[s + 1][1]

    if first > last and not up:
        return begin
    message = Message(c.dims[first], size(first))
    task = plan.add(functools.partial(go, first), 0.1, begin, sends=[message], rank=rank)
    for k in range(first, last + 1):
        def step(k=k):
            c.finish(k, c.bufs[k])
            if k < last:
                go(k + 1)
            elif up:
                c.spot(6, c.full, c.base)[...] = c.bufs[5][...]
                back(c.last)

        after = None
        if k < last:
            after = Message(c.dims[k + 1], size(k + 1))
        elif up:
            after = Message(c.dims[c.last], size(c.last))
        task = plan.add(step, 0.1 + size(k) / 2e6, [task], [message], [after] if after else [], rank)
        message = after
    if not up:
        return [task]
    for k in range(c.last, -1, -1):
        def step(k=k):
            c.gather_finish()
            if k > 0:
                back(k - 1)

        after = Message(c.dims[k - 1], size(k - 1)) if k > 0 else None
        task = plan.add(step, 0.1, [task], [message], [after] if after else [], rank)
        message = after
    return [task]


EARLY = 2
STAGE = [4, 4, 4, 4, 4, 4, 2, 2, 2, 3, 2, 1, 1, 1, 1]


def kind_of(n):
    p, j = n // 3, n % 3
    return (p, j, 896, 512, G_KINDS) if j < 2 else (p, j, 512, 896, D_KINDS)


def stage_shape(n, s):
    _, _, rows, lanes, kinds = kind_of(n)
    return ([(rows, lanes)] + halves(rows, lanes, kinds))[s + 1]


def tile(p):
    return pl.ds(512 * p, 512 if p < 4 else 384)


def wide_kernel(*refs):
    normed, gy, w_gate, w_up, w_down, gn_out, mlp_out = refs[:7]
    parts, refs = refs[7:22], refs[22:]
    gn_total, mlp_total, gn, got, hid, gg, gu, gate_w, up_w, down_w, x_send, x_recv, send, recv, local = refs[:15]
    refs = list(refs[15:])
    dp, t = coords()
    swap = Swap(gn, got, x_send, x_recv, dp, t)
    greet([swap.who] + [partner(d, dp, t) for d in ("core",) + LINKS])
    chains = []
    for n in range(15):
        p, j, rows, lanes, kinds = kind_of(n)
        c = Chain(rows, lanes, kinds, n, dp, t)
        c.source = refs.pop(0)
        c.gots = [refs.pop(0) for _ in range(STAGE[n] + 1)]
        c.bufs = c.gots[:-1] + [parts[n]] + [c.source]
        c.send, c.recv = send.at[n], recv.at[n]
        chains.append(c)
    loads = []

    def load(p):
        at, w, b = tile(p), 512 if p < 4 else 384, p % 2
        copies = [
            pltpu.make_async_copy(w_gate.at[:, at], gate_w.at[b, :, pl.ds(0, w)], local.at[p, 0]),
            pltpu.make_async_copy(w_up.at[:, at], up_w.at[b, :, pl.ds(0, w)], local.at[p, 1]),
            pltpu.make_async_copy(w_down.at[at, :], down_w.at[b, pl.ds(0, w), :], local.at[p, 2]),
        ]
        for c in copies:
            c.start()
        loads.append(copies)

    def layer(p):
        at, w, b = tile(p), 512 if p < 4 else 384, p % 2
        for c in loads[p]:
            c.wait()
        wg, wu, wd = gate_w.at[b, :, pl.ds(0, w)], up_w.at[b, :, pl.ds(0, w)], down_w.at[b, pl.ds(0, w), :]
        gate = mm(normed[...], wg[...])
        up = mm(normed[...], wu[...])
        back = mm_t(gy[...], wd[...])
        sig = 1.0 / (1.0 + jnp.exp(-gate))
        silu = gate * sig
        hid[:, at] = (silu * up).astype(BF)
        gu[:, at] = (back * silu).astype(BF)
        gg[:, at] = (back * up * sig * (1.0 + gate * (1.0 - sig))).astype(BF)
        mlp = mm(hid[:, at], wd[...])
        grad = mm_t(gg[:, at], wg[...]) + mm_t(gu[:, at], wu[...])
        if p == 0:
            mlp_total[...] = mlp
            gn_total[...] = grad
        elif p < 4:
            mlp_total[...] += mlp
            gn_total[...] += grad
        else:
            mlp_out[...] = (mlp_total[...] + mlp).astype(BF)
            gn[...] = (gn_total[...] + grad).astype(BF)
        if p + 2 < 5:
            load(p + 2)

    def weight(n):
        p, j = n // 3, n % 3
        w, dst = 512 if p < 4 else 384, chains[n].source
        if j < 2:
            dst[:, pl.ds(0, w)] = t_mm(normed[...], (gg, gu)[j][:, tile(p)]).astype(BF)
            if w < 512:
                dst[:, pl.ds(w, 512 - w)] = jnp.zeros((896, 512 - w), BF)
        else:
            dst[pl.ds(0, w), :] = t_mm(hid[:, tile(p)], gy[...]).astype(BF)
            if w < 512:
                dst[pl.ds(w, 512 - w), :] = jnp.zeros((512 - w, 896), BF)

    load(0)
    load(1)
    plan = Plan()
    meeting = plan.add(lambda: met(7), 0.3, rank=6)
    layers, done = [], []
    for p in range(5):
        layers.append(plan.add(functools.partial(layer, p), 3.4 if p < 4 else 2.6, layers[-1:], rank=5))
        if p == 0:
            layers.append(meeting)
            meeting["after"] = layers[:1]
        if p < EARLY:
            layers += [plan.add(functools.partial(weight, 3 * p + j), 0.55, layers[-1:], rank=4) for j in range(3)]
            done += layers[-3:]
    returned = [Message("tn", 128 * 896 * 2.0) for _ in range(4)]
    sent = plan.add(lambda: [swap.start(i) for i in range(4)], 0.2, layers[-1:] + [meeting], sends=returned, rank=0)
    for n in range(3 * EARLY, 15):
        done.append(plan.add(functools.partial(weight, n), 0.55 if n < 12 else 0.4, [sent], rank=5))
    for n, c in enumerate(chains):
        follow(plan, c, 0, STAGE[n], [done[n], meeting], 2)

    def take(i):
        gn_out[pl.ds(i * 128, 128), :] = swap.take(i)

    for i in range(4):
        plan.add(functools.partial(take, i), 0.2, [sent], returned[i : i + 1], rank=3)
    plan.run()


def wide(*operands):
    room = []
    for n in range(15):
        room += [pltpu.VMEM(stage_shape(n, s), BF) for s in range(-1, STAGE[n] + 1)]
    return pl.pallas_call(
        wide_kernel,
        out_shape=(
            jax.ShapeDtypeStruct((512, 896), F32),
            jax.ShapeDtypeStruct((512, 896), BF),
            *[jax.ShapeDtypeStruct(stage_shape(n, STAGE[n]), BF) for n in range(15)],
        ),
        in_specs=[VMEM_SPEC] * 2 + [ANY_SPEC] * 3,
        out_specs=(VMEM_SPEC,) * 17,
        scratch_shapes=[
            pltpu.VMEM((512, 896), F32),
            pltpu.VMEM((512, 896), F32),
            pltpu.VMEM((512, 896), BF),
            pltpu.VMEM((512, 896), BF),
            pltpu.VMEM((512, 2432), BF),
            pltpu.VMEM((512, 2432), BF),
            pltpu.VMEM((512, 2432), BF),
            pltpu.VMEM((2, 896, 512), BF),
            pltpu.VMEM((2, 896, 512), BF),
            pltpu.VMEM((2, 512, 896), BF),
            DMA((4,)), DMA((4,)), DMA((15, 12)), DMA((15, 12)), DMA((5, 3)),
            *room,
        ],
        compiler_params=params(3),
        name="wide",
    )(*operands)


LATE_TURN = [0, 1, 2, 3, 4, 0, 1, 2, 3]


def finish_kernel(*refs):
    lengths, parts_in, refs = refs[0], refs[1:16], refs[16:]
    (normed, q_in, k_in, v_in, lse, mixed, mlp, residual, gn2, gy, stream,
     wq, wk, wv, wo, vecs, table, squares) = refs[:18]
    gate_f, up_f, down_f, query_f, kv_f, out_f, small_o, res_o, gtok_o = refs[18:27]
    (mlp_got, gn, gn_got, sides, mask, ga, gm, gq, gk_t, gv_t, grad_res,
     small_buf, small_got) = refs[27:40]
    x_send, x_recv, send, recv, s_send, s_recv = refs[40:46]
    r_buf, r_mid0, r_mid1, r_send, r_recv, t_buf, t_mid0, t_mid1, t_send, t_recv = refs[46:56]
    refs = list(refs[56:])
    dp, t = coords()
    spot = (dp // 8 + t * (1 - 2 * (dp // 8 % 2)), dp % 8)
    length = lengths[group_of(dp, t)]
    swap_gn = Swap(gn, gn_got, x_send.at[0], x_recv.at[0], dp, t)
    swap_mlp = Swap(mlp, mlp_got, x_send.at[1], x_recv.at[1], dp, t)
    mail_res = Mail(r_buf, (r_mid0, r_mid1), res_o, spot, r_send, r_recv, dp, t)
    mail_tok = Mail(t_buf, (t_mid0, t_mid1), gtok_o, spot, t_send, t_recv, dp, t)
    across = (partner("x", *partner("core", dp, t)))
    greet(neighbours(dp, t) + [swap_gn.who, across])
    plan = Plan()
    chains = []
    for n in range(15):
        p, j, rows, lanes, kinds = kind_of(n)
        c = Chain(rows, lanes, kinds, n, dp, t)
        c.gots = [None] * (STAGE[n] + 1) + [refs.pop(0) for _ in range(STAGE[n] + 1, 6)]
        c.bufs = list(c.gots)
        c.bufs[STAGE[n]] = parts_in[n]
        c.send, c.recv = send.at[n], recv.at[n]
        c.full, c.base = (gate_f, up_f, down_f)[j], (0, 512 * p) if j < 2 else (512 * p, 0)
        chains.append(c)
    late, late_whole = [], []
    for i in range(9):
        c = Chain(128, 896, K_KINDS, LATE_TURN[i], dp, t)
        if i % 4 == 0:
            whole = refs.pop(0)
        c.source = whole.at[pl.ds(128 * (i % 4), 128), :] if i < 8 else whole
        c.gots = [refs.pop(0) for _ in range(6)]
        c.bufs = c.gots + [c.source]
        c.send, c.recv = send.at[15 + i], recv.at[15 + i]
        c.full, c.base = (query_f, out_f, kv_f)[i // 4], (128 * (i % 4), 0)
        late.append(c)
        if i % 4 == 0:
            late_whole.append(whole)
    q_src, o_src, k_src = late_whole
    meeting = plan.add(lambda: met(16), 0.5, rank=0)
    for n, c in enumerate(chains):
        follow(plan, c, STAGE[n] + 1, 5, [meeting], 4, True)
    swapped = [Message("tn", 128 * 896 * 2.0) for _ in range(4)]
    sent = plan.add(lambda: [swap_mlp.start(j) for j in range(4)], 0.2, [meeting], sends=swapped, rank=3)

    def norm_two(i):
        at = pl.ds(i * 128, 128)
        res, grad = residual[at, :], gn2[at, :]
        inverse = lax.rsqrt(jnp.mean(res * res, axis=-1, keepdims=True) + epsilon)
        unit = res * inverse
        total = jnp.sum((grad * unit).reshape(16, 8, 896), axis=0)
        scaled = grad * vecs[1:2, :]
        mean = jnp.mean(scaled * unit, axis=-1, keepdims=True)
        final = gy[at, :].astype(F32) + inverse * (scaled - unit * mean)
        grad_res[at, :] = final
        ga[at, :] = final.astype(BF)
        if i == 0:
            small_buf[0] = jnp.zeros((8, 896), F32)
        small_buf[0, 1:2, :] += jnp.sum(total, axis=0, keepdims=True)

    normed_back = [plan.add(functools.partial(norm_two, i), 0.6, rank=5) for i in range(4)]
    meeting["after"] = normed_back[:1]

    def prepare():
        fill_mask(mask, length)
        for side in range(2):
            sides[side] = one_head(k_in[...], side)
            sides[2 + side] = one_head(v_in[...], side)
        gk_t[...] = jnp.zeros((64, 512), F32)
        gv_t[...] = jnp.zeros((64, 512), F32)

    prepared = plan.add(prepare, 0.6, rank=5)

    def out_back():
        gm[:, pl.ds(384, 128)] = jnp.zeros((512, 128), BF)
        gm[:, pl.ds(0, 448)] = mm_t(ga[...], wo[...]).astype(BF)

    mixed_back = plan.add(out_back, 0.8, normed_back, rank=5)

    def heads(b, p):
        rows, keys = pl.ds(256 * b, 256), pl.ds(0, 256 * (b + 1))
        lanes = pl.ds(128 * p, 128)
        cos, sin = spread(table[rows, :])
        pair, pair_gm = q_in[rows, lanes], gm[rows, lanes]
        pair_t, pair_gm_t = pair.T, pair_gm.T
        grad = jnp.zeros((256, 128), F32)
        for side in range(2 if p < 3 else 1):
            h = 2 * p + side
            score = mm_t(pair, sides[side, keys, :]) + mask[rows, keys]
            probs = jnp.exp(score - lse[rows, h : h + 1])
            grad_probs = mm_t(pair_gm, sides[2 + side, keys, :])
            inner = jnp.sum(probs * grad_probs, axis=-1, keepdims=True)
            grad_scores = (probs * (grad_probs - inner)).astype(BF)
            grad = grad + mm(grad_scores, sides[side, keys, :])
            half = slice(64 * side, 64 * side + 64)
            gk_t[:, keys] += mm(pair_t[half, :], grad_scores)
            gv_t[:, keys] += mm(pair_gm_t[half, :], probs.astype(BF))
        gq[rows, lanes] = turn(grad, cos, -sin).astype(BF)

    key_grads = [None, None]

    def norm_part(b):
        rows = pl.ds(256 * b, 256)
        flat = table[rows, :].T
        cos_t, sin_t = flat[0:32], flat[64:96]
        one, two = gk_t[0:32, rows] * 0.125, gk_t[32:64, rows] * 0.125
        whole = jnp.concatenate([one * cos_t + two * sin_t, two * cos_t - one * sin_t, gv_t[:, rows]], axis=0).astype(BF)
        gkv = whole.T
        key_grads[b] = (whole, jnp.sum(gkv.astype(F32), axis=0, keepdims=True))
        part = mm(gq[rows, pl.ds(0, 448)], wq[...]) + mm(gkv[:, 0:64], wk[...]) + mm(gkv[:, 64:128], wv[...])
        gn[rows, :] = part.astype(BF)
        swap_gn.start(2 * b)
        swap_gn.start(2 * b + 1)

    returned = [Message("tn", 128 * 896 * 2.0) for _ in range(4)]
    before, parts = [prepared, mixed_back], [None, None]
    for b in (1, 0):
        before = [plan.add(functools.partial(heads, b, p), (1.0 + b) * (1.0 if p < 3 else 0.5), before, rank=5) for p in range(4)][-1:]
        parts[b] = plan.add(functools.partial(norm_part, b), 1.0, before + [meeting], sends=returned[2 * b : 2 * b + 2], rank=5)
        before = [parts[b]]

    def make_kv():
        whole = jnp.concatenate([key_grads[0][0], key_grads[1][0]], axis=1)
        k_src[...] = mm(whole, normed[...]).astype(BF)
        small_buf[0, 2:3, 0:448] = jnp.sum(gq[:, pl.ds(0, 448)].astype(F32), axis=0, keepdims=True)
        small_buf[0, 2:3, 512:640] = key_grads[0][1] + key_grads[1][1]
        small_buf[0, 3:4, :] = jnp.sum(squares[...], axis=0, keepdims=True)

    def make_q():
        q_src[...] = t_mm(gq[...], normed[...]).astype(BF)

    def make_o():
        o_src[...] = t_mm(mixed[...], ga[...]).astype(BF)

    made_q = plan.add(make_q, 0.8, [parts[0]], rank=5)
    made_kv = plan.add(make_kv, 0.6, [parts[0]], rank=5)
    made_o = plan.add(make_o, 0.8, [mixed_back], rank=4.5)
    for i, c in enumerate(late):
        follow(plan, c, 0, 5, [(made_q, made_o, made_kv)[i // 4], meeting], 2, True)

    def output(i):
        at = pl.ds(i * 128, 128)
        valid = lax.broadcasted_iota(jnp.int32, (128, 896), 0) + i * 128 < length
        branch = jnp.where(valid, swap_mlp.take(i), 0.0)
        result = jnp.where(valid, residual[at, :] + branch, 0.0)
        r_buf[pl.ds(i * 2, 2)] = result.reshape(2, 8, 8, 896).astype(BF)
        for row, x in ((4, result), (5, branch)):
            some = jnp.sum((x * x).reshape(16, 8, 896), axis=0)
            small_buf[0, row : row + 1, :] += jnp.sum(some, axis=0, keepdims=True)

    outputs = [plan.add(functools.partial(output, i), 0.5, [sent] + normed_back, swapped[i : i + 1], rank=6) for i in range(4)]

    def post(mail, ready, rank):
        one, two = Message("all", 2 * 458752.0), Message("all", 2 * 458752.0)
        a = plan.add(mail.first, 0.8, ready, sends=[one], rank=rank)
        b = plan.add(mail.second, 0.9, [a], [one], [two], rank)
        plan.add(mail.last, 0.2, [b], [two], rank=rank)

    post(mail_res, outputs + [meeting], 6)

    def norm_one(i):
        at = pl.ds(i * 128, 128)
        grad = swap_gn.take(i)
        row = stream[at, :].astype(F32)
        inverse = lax.rsqrt(jnp.mean(row * row, axis=-1, keepdims=True) + epsilon)
        unit = row * inverse
        total = jnp.sum((grad * unit).reshape(16, 8, 896), axis=0)
        scaled = grad * vecs[0:1, :]
        mean = jnp.mean(scaled * unit, axis=-1, keepdims=True)
        final = grad_res[at, :] + inverse * (scaled - unit * mean)
        t_buf[pl.ds(i * 2, 2)] = final.reshape(2, 8, 8, 896).astype(BF)
        small_buf[0, 0:1, :] += jnp.sum(total, axis=0, keepdims=True)

    finals = [plan.add(functools.partial(norm_one, i), 0.6, [parts[i // 2]], returned[i : i + 1], rank=1) for i in range(4)]
    post(mail_tok, finals, 0)

    def quartet(s):
        if s == 0:
            return [partner("core", dp, t), partner("x", dp, t), across]
        one, two = ("ya", "yb") if s == 1 else ("za", "zb")
        return [partner(one, dp, t), partner(two, dp, t), partner(one, *partner(two, dp, t))]

    posted = {}

    def share(s):
        posted[s] = [
            remote(small_buf.at[s], small_got.at[3 * s + i], s_send.at[3 * s + i], s_recv.at[3 * s + i], who)
            for i, who in enumerate(quartet(s))
        ]
        for c in posted[s]:
            c.start()

    def collect(s):
        for c in posted[s]:
            c.wait()
        small_buf[s + 1] = (small_buf[s] + small_got[3 * s]) + (small_got[3 * s + 1] + small_got[3 * s + 2])
        if s < 2:
            share(s + 1)
        else:
            small_o[...] = small_buf[3]

    message = Message("x", 28672.0)
    task = plan.add(functools.partial(share, 0), 0.2, finals + outputs + [made_kv], sends=[message], rank=1)
    for s in range(3):
        after = Message(("ya", "za", "za")[s], 28672.0)
        task = plan.add(functools.partial(collect, s), 0.2, [task], [message], [after] if s < 2 else [], rank=1)
        message = after
    plan.run()


def finish(*operands):
    wide_out = pltpu.VMEM((896, 2560), BF), pltpu.VMEM((896, 2560), BF), pltpu.VMEM((2560, 896), BF)
    room = []
    for n in range(15):
        room += [pltpu.VMEM(stage_shape(n, s), BF) for s in range(STAGE[n] + 1, 6)]
    for i in range(9):
        if i % 4 == 0:
            room.append(pltpu.VMEM((512 if i < 8 else 128, 896), BF))
        room += [pltpu.VMEM(x, BF) for x in K_SHAPES]
    return pl.pallas_call(
        finish_kernel,
        out_shape=(
            *wide_out,
            pltpu.VMEM((512, 896), BF),
            pltpu.VMEM((128, 896), BF),
            pltpu.VMEM((512, 896), BF),
            pltpu.VMEM((8, 896), F32),
            pltpu.VMEM((8, 8, 8, 896), BF),
            pltpu.VMEM((8, 8, 8, 896), BF),
        ),
        in_specs=[SMEM_SPEC] + [VMEM_SPEC] * 33,
        out_specs=(VMEM_SPEC,) * 9,
        scratch_shapes=[
            pltpu.VMEM((512, 896), BF),
            pltpu.VMEM((512, 896), BF),
            pltpu.VMEM((512, 896), BF),
            pltpu.VMEM((4, 512, 128), BF),
            pltpu.VMEM((512, 512), F32),
            pltpu.VMEM((512, 896), BF),
            pltpu.VMEM((512, 512), BF),
            pltpu.VMEM((512, 512), BF),
            pltpu.VMEM((64, 512), F32),
            pltpu.VMEM((64, 512), F32),
            pltpu.VMEM((512, 896), F32),
            pltpu.VMEM((4, 8, 896), F32),
            pltpu.VMEM((9, 8, 896), F32),
            DMA((2, 4)), DMA((2, 4)), DMA((24, 12)), DMA((24, 12)), DMA((9,)), DMA((9,)),
            *MAIL_SCRATCH, *MAIL_SCRATCH, *room,
        ],
        compiler_params=params(4, 45 << 20),
        name="finish",
    )(*operands)


def unpack_kernel(
    order, lengths, gate, up, down, query, kv, out_w, small, res, gtok,
    gate_o, up_o, down_o, query_o, key_o, value_o, out_o, res_o, gtok_o, gain1_o, gain2_o, bq_o, bk_o, bv_o, rms_o,
    where_from,
):
    i = pl.program_id(0)

    @pl.when(i == 0)
    def _():
        def note(g, carry):
            where_from[order[g]] = g
            return carry + lengths[g]

        count = lax.fori_loop(0, 64, note, 0).astype(F32) * 896.0
        rms = jnp.sqrt(jnp.sum(small[...], axis=-1, keepdims=True) / count)
        lane = lax.broadcasted_iota(jnp.int32, (1, 128), 1)
        line = jnp.where(lane == 0, rms[4:5], jnp.where(lane == 1, rms[3:4], rms[5:6]))
        gain1_o[...] = small[0, :]
        gain2_o[...] = small[1, :]
        bq_o[...] = small[2, 0:448]
        pair = small[2:3, 512:640]
        bk_o[...] = pair[0, 0:64]
        bv_o[...] = pltpu.roll(pair, 64, 1)[0, 0:64]
        rms_o[...] = line[0, 0:3]
        key_o[...] = kv[pl.ds(0, 64), :].astype(F32)
        value_o[...] = kv[pl.ds(64, 64), :].astype(F32)

    rows = pl.ds(pl.multiple_of(i * 64, 64), 64)
    gate_o[...] = gate[rows, pl.ds(0, 2432)].astype(F32)
    up_o[...] = up[rows, pl.ds(0, 2432)].astype(F32)
    down_o[...] = down[pl.ds(pl.multiple_of(i * 176, 16), 176), :].astype(F32)

    @pl.when(i < 7)
    def _():
        query_o[...] = query[rows, :].astype(F32)
        out_o[...] = out_w[rows, :].astype(F32)

    @pl.when(i < 8)
    def _():
        for j in range(8):
            slot = where_from[jnp.minimum(i, 7) * 8 + j]
            res_o[j] = res[slot]
            gtok_o[j] = gtok[slot]


def unpack(*operands):
    rows = lambda i: (i, 0)
    some = lambda i: (jnp.minimum(i, 6), 0)
    return pl.pallas_call(
        unpack_kernel,
        grid=(14,),
        out_shape=(
            jax.ShapeDtypeStruct((896, 2432), F32),
            jax.ShapeDtypeStruct((896, 2432), F32),
            jax.ShapeDtypeStruct((2432, 896), F32),
            jax.ShapeDtypeStruct((448, 896), F32),
            jax.ShapeDtypeStruct((64, 896), F32),
            jax.ShapeDtypeStruct((64, 896), F32),
            jax.ShapeDtypeStruct((448, 896), F32),
            BLOCK,
            BLOCK,
            *[jax.ShapeDtypeStruct((n,), F32) for n in (896, 896, 448, 64, 64, 3)],
        ),
        in_specs=[SMEM_SPEC] * 2 + [VMEM_SPEC] * 9,
        out_specs=(
            pl.BlockSpec((64, 2432), rows),
            pl.BlockSpec((64, 2432), rows),
            pl.BlockSpec((176, 896), rows),
            pl.BlockSpec((64, 896), some),
            pl.BlockSpec((64, 896), lambda i: (0, 0)),
            pl.BlockSpec((64, 896), lambda i: (0, 0)),
            pl.BlockSpec((64, 896), some),
            pl.BlockSpec((8, 8, 896), lambda i: (jnp.minimum(i, 7), 0, 0)),
            pl.BlockSpec((8, 8, 896), lambda i: (jnp.minimum(i, 7), 0, 0)),
            *[VMEM_SPEC] * 6,
        ),
        scratch_shapes=[pltpu.SMEM((64,), jnp.int32)],
        compiler_params=pltpu.CompilerParams(vmem_limit_bytes=16 << 20),
        name="unpack",
    )(*operands[:2], *[pltpu.with_memory_space_constraint(x, pltpu.VMEM) for x in operands[2:]])


def on_device(
    tokens,
    cotangent,
    lengths,
    deal_order,
    gain_attn,
    w_query,
    b_query,
    w_key,
    b_key,
    w_value,
    b_value,
    w_out,
    gain_mlp,
    w_gate,
    w_up,
    w_down,
):
    table = jnp.asarray(rope_table())
    biases = jnp.concatenate([b_query, b_key, b_value, jnp.zeros((320,), BF)])
    blank = jnp.zeros((896,), BF)
    vecs = jnp.stack([gain_attn, gain_mlp, biases] + [blank] * 5).astype(F32)
    normed, q, k, v, lse, mixed, residual, normed_two, gy, squares, stream = meet(
        deal_order, lengths, tokens, cotangent, w_query.T, w_key.T, w_value.T, w_out, vecs, table
    )
    gn2, mlp, *sums = wide(normed_two, gy, w_gate, w_up, w_down)
    gate, up, down, query, kv, out_w, small, sent_res, sent_tok = finish(
        lengths, *sums, normed, q, k, v, lse, mixed, mlp, residual, gn2, gy, stream,
        w_query.T, w_key.T, w_value.T, w_out, vecs, table, squares,
    )
    (
        gate, up, down, query, key, value, out_w, layer_out, grad_tokens,
        gain_one, gain_two, bias_query, bias_key, bias_value, rms_values,
    ) = unpack(
        deal_order, lengths, gate, up, down, query, kv, out_w, small,
        sent_res.reshape(64, 8, 896), sent_tok.reshape(64, 8, 896),
    )
    return (
        layer_out,
        grad_tokens,
        gain_one,
        query.T,
        bias_query,
        key.T,
        bias_key,
        value.T,
        bias_value,
        out_w,
        gain_two,
        gate,
        up,
        down,
        rms_values,
    )


def solution(mesh):
    in_specs = (
        P(None, "dp", None),
        P(None, "dp", None),
        P(),
        P(),
        P(),
        P(None, "tensor"),
        P("tensor"),
        P(None, "tensor"),
        P("tensor"),
        P(None, "tensor"),
        P("tensor"),
        P("tensor", None),
        P(),
        P(None, "tensor"),
        P(None, "tensor"),
        P("tensor", None),
    )
    out_specs = (
        P(None, "dp", None),
        P(None, "dp", None),
        P(),
        P(None, "tensor"),
        P("tensor"),
        P(None, "tensor"),
        P("tensor"),
        P(None, "tensor"),
        P("tensor"),
        P("tensor", None),
        P(),
        P(None, "tensor"),
        P(None, "tensor"),
        P("tensor", None),
        P(),
    )
    return jax.shard_map(
        on_device, mesh=mesh, in_specs=in_specs, out_specs=out_specs, check_vma=False
    )
```

```python
import functools
import math

import jax
import jax.numpy as jnp
import numpy as np
from jax import lax
from jax.experimental import pallas as pl
from jax.experimental.pallas import tpu as pltpu
from jax.sharding import PartitionSpec as P

MESH = pl.DeviceIdType.MESH
HD = 64
epsilon = 1e-06
rope_base = 1000000.0
VMEM_LIMIT = 60 << 20
LINKS = ("x", "ya", "za", "yb", "zb")


def flip(dp):
    return dp + 8 - 16 * ((dp // 8) % 2)


def group_of(dp, t):
    return dp + t * (flip(dp) - dp)


def coords():
    return lax.axis_index("dp"), lax.axis_index("tensor")


def partner(dim, dp, t):
    y, xl, z, c = dp // 16, (dp // 8) % 2, (dp // 2) % 4, dp % 2
    if dim == "core":
        c = 1 - c
    if dim == "x":
        xl = 1 - xl
    if dim == "ya":
        y = y + 1 - 2 * (y % 2)
    if dim == "yb":
        y = 3 - y
    if dim == "za":
        z = z + 1 - 2 * (z % 2)
    if dim == "zb":
        z = 3 - z
    if dim == "tn":
        xl, t = 1 - xl, 1 - t
    return (((y * 2 + xl) * 4 + z) * 2 + c, t)


def bit(dim, dp):
    y, xl, z, c = dp // 16, (dp // 8) % 2, (dp // 2) % 4, dp % 2
    return {
        "core": c,
        "x": xl,
        "ya": ((y + 1) // 2) % 2,
        "yb": y // 2,
        "za": ((z + 1) // 2) % 2,
        "zb": z // 2,
    }[dim]


def greet(partners):
    barrier = pltpu.get_barrier_semaphore()
    for who in partners:
        pl.semaphore_signal(barrier, inc=1, device_id=who, device_id_type=MESH)


def around(dp, t, axis, j):
    a, b = dp // 8, dp % 8
    return (((a + j) % 8 * 8 + b) if axis == 0 else a * 8 + (b + j) % 8, t)


def neighbours(dp, t):
    return [around(dp, t, axis, j) for axis in range(2) for j in range(1, 8)]


def met(n):
    pl.semaphore_wait(pltpu.get_barrier_semaphore(), n)


def remote(src, dst, send, recv, who):
    return pltpu.make_async_remote_copy(
        src_ref=src, dst_ref=dst, send_sem=send, recv_sem=recv, device_id=who, device_id_type=MESH
    )


def put_sum(dst, src, row, lane, other, rows, lanes):
    step = 16
    while step * 2 * lanes <= 32768 and rows % (step * 2) == 0:
        step *= 2

    def body(i, carry):
        here = pl.ds(pl.multiple_of(i * step, 16), step)
        there = pl.ds(pl.multiple_of(row + i * step, 16), step)
        lane_at = lane if isinstance(lane, int) else pl.multiple_of(lane, 128)
        dst[here, :] = src[there, pl.ds(lane_at, lanes)] + other[here, :]
        return carry

    lax.fori_loop(0, rows // step, body, 0)


def halves(rows, lanes, kinds):
    out = []
    for kind in kinds:
        if kind == "r":
            rows //= 2
        elif kind == "l":
            lanes //= 2
        out.append((rows, lanes))
    return out


class Chain:
    def __init__(self, rows, lanes, kinds, turn, dp, t):
        self.kinds = kinds
        self.dims = ("core",) + tuple(LINKS[(turn + i) % 5] for i in range(5))
        self.who = [partner(d, dp, t) for d in self.dims]
        self.bits = [bit(d, dp) for d in self.dims]
        self.shapes = [(rows, lanes)] + halves(rows, lanes, kinds)
        self.last = max(i for i, kind in enumerate(kinds) if kind != "f")
        self.corner = [(0, 0)]
        for s, kind in enumerate(kinds):
            row, lane = self.corner[-1]
            rows, lanes = self.shapes[s + 1]
            b = self.bits[s]
            self.corner.append((row + (b * rows if kind == "r" else 0), lane + (b * lanes if kind == "l" else 0)))

    def start(self, s, src, got, send, recv):
        rows, lanes = self.shapes[s + 1]
        give, self.keep = (0, 0), (0, 0)
        b = self.bits[s]
        if self.kinds[s] == "r":
            give, self.keep = (pl.multiple_of((1 - b) * rows, 16), 0), (b * rows, 0)
        elif self.kinds[s] == "l":
            give, self.keep = (0, pl.multiple_of((1 - b) * lanes, 128)), (0, b * lanes)
        self.src, self.got = src, got
        self.copy = remote(src.at[pl.ds(give[0], rows), pl.ds(give[1], lanes)], got, send, recv, self.who[s])
        self.copy.start()

    def finish(self, s, dst):
        self.copy.wait()
        rows, lanes = self.shapes[s + 1]
        put_sum(dst, self.src, self.keep[0], self.keep[1], self.got, rows, lanes)

    def spot(self, s, full, base):
        rows, lanes = self.shapes[s]
        row, lane = self.corner[s]
        row, lane = row + base[0], lane + base[1]
        row = row if isinstance(row, int) else pl.multiple_of(row, 16)
        lane = lane if isinstance(lane, int) else pl.multiple_of(lane, 128)
        return full.at[pl.ds(row, rows), pl.ds(lane, lanes)]

    def gather_start(self, s, full, base, send, recv):
        mine = self.spot(s + 1, full, base)
        self.copy = remote(mine, mine, send, recv, self.who[s])
        self.copy.start()

    def gather_finish(self):
        self.copy.wait()


G_KINDS = ("l", "l", "r", "r", "r", "f")
D_KINDS = ("r", "r", "r", "r", "r", "f")
K_KINDS = ("r", "r", "r", "f", "f", "f")
ANY_SPEC = pl.BlockSpec(memory_space=pl.ANY)
G_SHAPES = halves(896, 512, G_KINDS)
D_SHAPES = halves(512, 896, D_KINDS)
K_SHAPES = halves(128, 896, K_KINDS)
BF, F32 = jnp.bfloat16, jnp.float32
VMEM_SPEC = pl.BlockSpec(memory_space=pltpu.VMEM)
SMEM_SPEC = pl.BlockSpec(memory_space=pltpu.SMEM)
BLOCK = jax.ShapeDtypeStruct((64, 8, 896), BF)
DMA = pltpu.SemaphoreType.DMA


def params(cid, limit=VMEM_LIMIT):
    return pltpu.CompilerParams(collective_id=cid, has_side_effects=True, vmem_limit_bytes=limit)


class Mail:
    LOW = 512

    def __init__(self, buf, mids, out, spot, send, recv, dp, t):
        self.buf, self.mids, self.out = buf, mids, out
        self.me = (dp // 8, dp % 8)
        self.spot = spot
        self.send, self.recv, self.dp, self.t = send, recv, dp, t
        self.lanes = (pl.ds(0, self.LOW), pl.ds(self.LOW, 896 - self.LOW))

    def first(self):
        self.copies = [[], []]
        for j in range(1, 8):
            for f in range(2):
                to = (self.me[f] + j) % 8
                src = self.buf.at[to, :, :, self.lanes[f]] if f == 0 else self.buf.at[:, to, :, self.lanes[f]]
                c = remote(src, self.mids[f].at[self.spot[f]], self.send.at[0, f, j], self.recv.at[0, f, j],
                           around(self.dp, self.t, f, j))
                c.start()
                self.copies[f].append(c)
        for f in range(2):
            me = self.me[f]
            own = self.buf[me, :, :, self.lanes[f]] if f == 0 else self.buf[:, me, :, self.lanes[f]]
            self.mids[f][self.spot[f]] = own

    def second(self):
        for f in range(2):
            for c in self.copies[f]:
                c.wait()
        self.copies = []
        for j in range(1, 8):
            for f in range(2):
                g = 1 - f
                to = (self.me[g] + j) % 8
                dst = self.out.at[:, self.spot[1], :, self.lanes[f]] if f == 0 else self.out.at[self.spot[0], :, :, self.lanes[f]]
                c = remote(self.mids[f].at[:, to], dst, self.send.at[1, f, j], self.recv.at[1, f, j],
                           around(self.dp, self.t, g, j))
                c.start()
                self.copies.append(c)
        for f in range(2):
            own = self.mids[f][:, self.me[1 - f]]
            if f == 0:
                self.out[:, self.spot[1], :, self.lanes[f]] = own
            else:
                self.out[self.spot[0], :, :, self.lanes[f]] = own

    def last(self):
        for c in self.copies:
            c.wait()


MAIL = jax.ShapeDtypeStruct((8, 8, 8, 896), BF)
MAIL_SCRATCH = [
    pltpu.VMEM((8, 8, 8, 896), BF), pltpu.VMEM((8, 8, 8, 512), BF), pltpu.VMEM((8, 8, 8, 384), BF),
    DMA((2, 2, 8)), DMA((2, 2, 8)),
]


def sort_out(order, rows, buf, dp, t):
    for a in range(8):
        for b in range(8):
            buf[a, b] = rows[order[group_of(a * 8 + b, t)]]


def mm(a, b):
    return jnp.dot(a, b, preferred_element_type=F32)


def mm_t(a, b):
    return lax.dot_general(a, b, (((1,), (1,)), ((), ())), preferred_element_type=F32)


def t_mm(a, b):
    return lax.dot_general(a, b, (((0,), (0,)), ((), ())), preferred_element_type=F32)


def rope_table():
    places = np.arange(512, dtype=np.float32)
    frequency = np.power(np.float32(rope_base), -np.arange(32, dtype=np.float32) * np.float32(2.0 / HD)).astype(np.float32)
    angles = (places[:, None] * frequency[None, :]).astype(np.float64)
    cos, sin = np.cos(angles), np.sin(angles)
    return np.concatenate([cos, cos, sin, sin], axis=1).astype(np.float32)


def first_half(shape):
    return lax.broadcasted_iota(jnp.int32, shape, 1) % 64 < 32


def spread(table):
    other = pltpu.roll(table, 64, 1)
    low = lax.broadcasted_iota(jnp.int32, table.shape, 1) < 64
    cos, sin = jnp.where(low, table, other), jnp.where(low, other, table)
    return cos, jnp.where(first_half(table.shape), -sin, sin)


def turn(x, cos, sin):
    swapped = jnp.where(first_half(x.shape), pltpu.roll(x, 96, 1), pltpu.roll(x, 32, 1))
    return x * cos + swapped * sin


def one_head(pair, side):
    low = lax.broadcasted_iota(jnp.int32, pair.shape, 1) < 64
    return jnp.where(low if side == 0 else jnp.logical_not(low), pair, jnp.zeros_like(pair))


def fill_mask(mask, length):
    for b in range(2):
        rows = lax.broadcasted_iota(jnp.int32, (256, 512), 0) + b * 256
        cols = lax.broadcasted_iota(jnp.int32, (256, 512), 1)
        mask[pl.ds(b * 256, 256), :] = jnp.where((cols <= rows) & (cols < length), 0.0, -1e30)


class Swap:
    def __init__(self, x, got, send, recv, dp, t):
        self.who = partner("tn", dp, t)
        self.x, self.got, self.send, self.recv = x, got, send, recv
        self.copies = [None] * 4

    def start(self, i):
        rows = pl.ds(i * 128, 128)
        self.copies[i] = remote(self.x.at[rows], self.got.at[rows], self.send.at[i], self.recv.at[i], self.who)
        self.copies[i].start()

    def take(self, i):
        self.copies[i].wait()
        rows = pl.ds(i * 128, 128)
        return self.x[rows, :].astype(F32) + self.got[rows, :].astype(F32)


def meet_kernel(
    order, lengths, tok, cot, wq, wk, wv, wo, vecs, table,
    normed, q_o, k_o, v_o, lse_o, mixed, residual, normed_two, gy, squares, stream,
    sides, mask, x, got, tok_in, cot_in, send, recv, buf, mid0, mid1, c_send, c_recv, t_buf, t_mid0, t_mid1, t_send, t_recv,
):
    dp, t = coords()
    swap = Swap(x, got, send, recv, dp, t)
    mail = Mail(buf, (mid0, mid1), cot_in, (dp // 8, dp % 8), c_send, c_recv, dp, t)
    greet(neighbours(dp, t) + [swap.who])
    length = lengths[group_of(dp, t)]
    sort_out(order, tok, t_buf, dp, t)
    tokens = Mail(t_buf, (t_mid0, t_mid1), tok_in, (dp // 8, dp % 8), t_send, t_recv, dp, t)
    met(15)
    tokens.first()
    sort_out(order, cot, buf, dp, t)
    fill_mask(mask, length)
    cos, sin = spread(table[...])
    tokens.second()
    tokens.last()
    mail.first()
    for i in range(4):
        at = pl.ds(i * 128, 128)
        row = tok_in[pl.ds(i * 2, 2)].astype(F32).reshape(128, 896)
        stream[at, :] = row.astype(BF)
        inverse = lax.rsqrt(jnp.mean(row * row, axis=-1, keepdims=True) + epsilon)
        normed[at, :] = (row * inverse * vecs[0:1, :]).astype(BF)
    k = mm_t(normed[...], wk[...]) + vecs[2:3, 448:512]
    v = mm_t(normed[...], wv[...]) + vecs[2:3, 512:576]
    k2 = turn(jnp.concatenate([k, k], axis=1), cos, sin)
    k_o[...] = (k2.astype(BF).astype(F32) * 0.125).astype(BF)
    v_o[...] = jnp.concatenate([v, v], axis=1).astype(BF)
    for side in range(2):
        sides[side] = one_head(k_o[...], side)
        sides[2 + side] = one_head(v_o[...], side)
    for p in range(4):
        w = 128 if p < 3 else 64
        lanes = pl.ds(128 * p, w)
        q = mm_t(normed[...], wq[lanes, :]) + vecs[2:3, lanes]
        if w < 128:
            q = jnp.concatenate([q, jnp.zeros((512, 64), F32)], axis=1)
        q_o[:, pl.ds(128 * p, 128)] = turn(q, cos, sin).astype(BF)
    for b in range(2):
        rows, keys = pl.ds(256 * b, 256), pl.ds(0, 256 * (b + 1))
        lse_o[rows, :] = jnp.zeros((256, 128), F32)

        def heads(p, both):
            lanes = pl.ds(pl.multiple_of(128 * p, 128), 128)
            pair = q_o[rows, lanes]
            total = jnp.zeros((256, 128), F32)
            for side in range(2 if both else 1):
                score = mm_t(pair, sides[side, keys, :]) + mask[rows, keys]
                top = jnp.max(score, axis=-1, keepdims=True)
                expo = jnp.exp(score - top)
                mass = jnp.sum(expo, axis=-1, keepdims=True)
                probs = (expo * (1.0 / mass)).astype(BF)
                total = total + mm(probs, sides[2 + side, keys, :])
                here = lax.broadcasted_iota(jnp.int32, (256, 128), 1) == 2 * p + side
                lse_o[rows, :] = jnp.where(here, top + jnp.log(mass), lse_o[rows, :])
            mixed[rows, lanes] = total.astype(BF)

        def body(p, carry):
            heads(p, True)
            return carry

        lax.fori_loop(0, 3, body, 0)
        heads(3, False)
        x[rows, :] = mm(mixed[rows, pl.ds(0, 448)], wo[...]).astype(BF)
        swap.start(2 * b)
        swap.start(2 * b + 1)
        if b == 0:
            mail.second()
    total = jnp.zeros((8, 896), F32)
    for i in range(4):
        at = pl.ds(i * 128, 128)
        valid = lax.broadcasted_iota(jnp.int32, (128, 896), 0) + i * 128 < length
        attention = swap.take(i)
        res = stream[at, :].astype(F32) + attention
        residual[at, :] = res
        inverse = lax.rsqrt(jnp.mean(res * res, axis=-1, keepdims=True) + epsilon)
        normed_two[at, :] = (res * inverse * vecs[1:2, :]).astype(BF)
        kept = jnp.where(valid, attention, 0.0)
        total = total + jnp.sum((kept * kept).reshape(16, 8, 896), axis=0)
    squares[...] = total
    mail.last()
    for i in range(4):
        at = pl.ds(i * 128, 128)
        valid = lax.broadcasted_iota(jnp.int32, (128, 896), 0) + i * 128 < length
        gy[at, :] = jnp.where(valid, cot_in[pl.ds(i * 2, 2)].astype(F32).reshape(128, 896), 0.0).astype(BF)


def meet(*operands):
    rows = jax.ShapeDtypeStruct((512, 896), BF)
    wide_rows = jax.ShapeDtypeStruct((512, 512), BF)
    pair = jax.ShapeDtypeStruct((512, 128), BF)
    return pl.pallas_call(
        meet_kernel,
        out_shape=(
            rows, wide_rows, pair, pair, jax.ShapeDtypeStruct((512, 128), F32), wide_rows,
            jax.ShapeDtypeStruct((512, 896), F32), rows, rows, jax.ShapeDtypeStruct((8, 896), F32), rows,
        ),
        in_specs=[SMEM_SPEC] * 2 + [VMEM_SPEC] * 8,
        out_specs=(VMEM_SPEC,) * 11,
        scratch_shapes=[
            pltpu.VMEM((4, 512, 128), BF),
            pltpu.VMEM((512, 512), F32),
            pltpu.VMEM((512, 896), BF),
            pltpu.VMEM((512, 896), BF),
            pltpu.VMEM((8, 8, 8, 896), BF),
            pltpu.VMEM((8, 8, 8, 896), BF),
            DMA((4,)), DMA((4,)), *MAIL_SCRATCH, *MAIL_SCRATCH,
        ],
        compiler_params=params(2),
        name="meet",
    )(*operands)


class Message:
    def __init__(self, link, size):
        self.link, self.size, self.lands = link, size, None


class Plan:
    LATENCY = 3.2
    RATE = {"core": 500e3, "tn": 43e3}

    def __init__(self):
        self.tasks = []

    def add(self, act, cost, after=(), needs=(), sends=(), rank=5):
        task = dict(act=act, cost=cost, after=list(after), needs=list(needs), sends=list(sends), rank=rank, done=False)
        self.tasks.append(task)
        return task

    def run(self):
        now, free = 0.0, {}
        left = list(self.tasks)
        while left:
            open_ = [x for x in left if all(y["done"] for y in x["after"]) and all(m.lands is not None for m in x["needs"])]
            at = {id(x): max([now] + [m.lands for m in x["needs"]]) for x in open_}
            ready = [x for x in open_ if at[id(x)] <= now]
            task = min(ready, key=lambda x: x["rank"]) if ready else min(open_, key=lambda x: at[id(x)])
            now = at[id(task)] + task["cost"]
            task["act"]()
            task["done"] = True
            left.remove(task)
            for m in task["sends"]:
                links = LINKS if m.link == "all" else (m.link,)
                for link in links:
                    begin = max(now, free.get(link, 0.0))
                    free[link] = begin + m.size / len(links) / self.RATE.get(link, 40e3)
                m.lands = max(free[link] for link in links) + self.LATENCY
        return now


def follow(plan, c, first, last, begin, rank, up=False):
    def go(s):
        c.start(s, c.bufs[s - 1], c.gots[s], c.send.at[s], c.recv.at[s])

    def back(s):
        c.gather_start(s, c.full, c.base, c.send.at[6 + s], c.recv.at[6 + s])

    def size(s):
        return 2.0 * c.shapes[s + 1][0] * c.shapes[s + 1][1]

    if first > last and not up:
        return begin
    message = Message(c.dims[first], size(first))
    task = plan.add(functools.partial(go, first), 0.1, begin, sends=[message], rank=rank)
    for k in range(first, last + 1):
        def step(k=k):
            c.finish(k, c.bufs[k])
            if k < last:
                go(k + 1)
            elif up:
                c.spot(6, c.full, c.base)[...] = c.bufs[5][...]
                back(c.last)

        after = None
        if k < last:
            after = Message(c.dims[k + 1], size(k + 1))
        elif up:
            after = Message(c.dims[c.last], size(c.last))
        task = plan.add(step, 0.1 + size(k) / 2e6, [task], [message], [after] if after else [], rank)
        message = after
    if not up:
        return [task]
    for k in range(c.last, -1, -1):
        def step(k=k):
            c.gather_finish()
            if k > 0:
                back(k - 1)

        after = Message(c.dims[k - 1], size(k - 1)) if k > 0 else None
        task = plan.add(step, 0.1, [task], [message], [after] if after else [], rank)
        message = after
    return [task]


EARLY = 3
STAGE = [4, 4, 3, 4, 4, 4, 4, 3, 2, 2, 2, 1, 1, 1, 1]


TURN = [2, 4, 1, 3, 0, 0, 1, 2, 3, 4, 0, 3, 4, 2, 1]


def kind_of(n):
    p, j = n // 3, n % 3
    return (p, j, 896, 512, G_KINDS) if j < 2 else (p, j, 512, 896, D_KINDS)


def stage_shape(n, s):
    _, _, rows, lanes, kinds = kind_of(n)
    return ([(rows, lanes)] + halves(rows, lanes, kinds))[s + 1]


def tile(p):
    return pl.ds(512 * p, 512 if p < 4 else 384)


def wide_kernel(*refs):
    normed, gy, w_gate, w_up, w_down, gn_out, mlp_out = refs[:7]
    parts, refs = refs[7:22], refs[22:]
    gn_total, mlp_total, gn, got, hid, gg, gu, gate_w, up_w, down_w, x_send, x_recv, send, recv, local = refs[:15]
    refs = list(refs[15:])
    dp, t = coords()
    swap = Swap(gn, got, x_send, x_recv, dp, t)
    greet([swap.who] + [partner(d, dp, t) for d in ("core",) + LINKS])
    chains = []
    for n in range(15):
        p, j, rows, lanes, kinds = kind_of(n)
        c = Chain(rows, lanes, kinds, TURN[n], dp, t)
        c.source = refs.pop(0)
        c.gots = [refs.pop(0) for _ in range(STAGE[n] + 1)]
        c.bufs = c.gots[:-1] + [parts[n]] + [c.source]
        c.send, c.recv = send.at[n], recv.at[n]
        chains.append(c)
    loads = []

    def load(p):
        at, w, b = tile(p), 512 if p < 4 else 384, p % 2
        copies = [
            pltpu.make_async_copy(w_gate.at[:, at], gate_w.at[b, :, pl.ds(0, w)], local.at[p, 0]),
            pltpu.make_async_copy(w_up.at[:, at], up_w.at[b, :, pl.ds(0, w)], local.at[p, 1]),
            pltpu.make_async_copy(w_down.at[at, :], down_w.at[b, pl.ds(0, w), :], local.at[p, 2]),
        ]
        for c in copies:
            c.start()
        loads.append(copies)

    def layer(p):
        at, w, b = tile(p), 512 if p < 4 else 384, p % 2
        for c in loads[p]:
            c.wait()
        wg, wu, wd = gate_w.at[b, :, pl.ds(0, w)], up_w.at[b, :, pl.ds(0, w)], down_w.at[b, pl.ds(0, w), :]
        gate = mm(normed[...], wg[...])
        up = mm(normed[...], wu[...])
        back = mm_t(gy[...], wd[...])
        sig = 1.0 / (1.0 + jnp.exp(-gate))
        silu = gate * sig
        hid[:, at] = (silu * up).astype(BF)
        gu[:, at] = (back * silu).astype(BF)
        gg[:, at] = (back * up * sig * (1.0 + gate * (1.0 - sig))).astype(BF)
        mlp = mm(hid[:, at], wd[...])
        grad = mm_t(gg[:, at], wg[...]) + mm_t(gu[:, at], wu[...])
        if p == 0:
            mlp_total[...] = mlp
            gn_total[...] = grad
        elif p < 4:
            mlp_total[...] += mlp
            gn_total[...] += grad
        else:
            mlp_out[...] = (mlp_total[...] + mlp).astype(BF)
            gn[...] = (gn_total[...] + grad).astype(BF)
        if p + 2 < 5:
            load(p + 2)

    def weight(n):
        p, j = n // 3, n % 3
        w, dst = 512 if p < 4 else 384, chains[n].source
        if j < 2:
            dst[:, pl.ds(0, w)] = t_mm(normed[...], (gg, gu)[j][:, tile(p)]).astype(BF)
            if w < 512:
                dst[:, pl.ds(w, 512 - w)] = jnp.zeros((896, 512 - w), BF)
        else:
            dst[pl.ds(0, w), :] = t_mm(hid[:, tile(p)], gy[...]).astype(BF)
            if w < 512:
                dst[pl.ds(w, 512 - w), :] = jnp.zeros((512 - w, 896), BF)

    load(0)
    load(1)
    plan = Plan()
    meeting = plan.add(lambda: met(7), 0.3, rank=6)
    layers, done = [], []
    for p in range(5):
        layers.append(plan.add(functools.partial(layer, p), 3.4 if p < 4 else 2.6, layers[-1:], rank=5))
        if p == 0:
            layers.append(meeting)
            meeting["after"] = layers[:1]
        if p < EARLY:
            layers += [plan.add(functools.partial(weight, 3 * p + j), 0.55, layers[-1:], rank=4) for j in range(3)]
            done += layers[-3:]
    returned = [Message("tn", 128 * 896 * 2.0) for _ in range(4)]
    sent = plan.add(lambda: [swap.start(i) for i in range(4)], 0.2, layers[-1:] + [meeting], sends=returned, rank=0)
    for n in range(3 * EARLY, 15):
        done.append(plan.add(functools.partial(weight, n), 0.55 if n < 12 else 0.4, [sent], rank=5))
    for n, c in enumerate(chains):
        follow(plan, c, 0, STAGE[n], [done[n], meeting], 2)

    def take(i):
        gn_out[pl.ds(i * 128, 128), :] = swap.take(i)

    for i in range(4):
        plan.add(functools.partial(take, i), 0.2, [sent], returned[i : i + 1], rank=3)
    plan.run()


def wide(*operands):
    room = []
    for n in range(15):
        room += [pltpu.VMEM(stage_shape(n, s), BF) for s in range(-1, STAGE[n] + 1)]
    return pl.pallas_call(
        wide_kernel,
        out_shape=(
            pltpu.VMEM((512, 896), F32),
            pltpu.VMEM((512, 896), BF),
            *[pltpu.VMEM(stage_shape(n, STAGE[n]), BF) for n in range(15)],
        ),
        in_specs=[VMEM_SPEC] * 2 + [ANY_SPEC] * 3,
        out_specs=(VMEM_SPEC,) * 17,
        scratch_shapes=[
            pltpu.VMEM((512, 896), F32),
            pltpu.VMEM((512, 896), F32),
            pltpu.VMEM((512, 896), BF),
            pltpu.VMEM((512, 896), BF),
            pltpu.VMEM((512, 2432), BF),
            pltpu.VMEM((512, 2432), BF),
            pltpu.VMEM((512, 2432), BF),
            pltpu.VMEM((2, 896, 512), BF),
            pltpu.VMEM((2, 896, 512), BF),
            pltpu.VMEM((2, 512, 896), BF),
            DMA((4,)), DMA((4,)), DMA((15, 12)), DMA((15, 12)), DMA((5, 3)),
            *room,
        ],
        compiler_params=params(3, 52 << 20),
        name="wide",
    )(*operands)


FROM_WIDE = set(range(1, 16)) | {22, 24}


def in_vmem(x):
    return pltpu.with_memory_space_constraint(x, pltpu.VMEM)


LATE_TURN = [2, 2, 0, 2, 2, 3, 3, 0, 3]
RANK = [4.4, 4, 4, 4, 4, 5.5, 4.2, 4, 4.4, 4.6, 4.4, 4.2, 4.4, 4.4, 4.6]
LATE_RANK = [2, 1, 3, 2, 4.5, 4.5, 4.5, 1, 3]
MAIL_RANK = [3, 0]


def finish_kernel(*refs):
    lengths, parts_in, refs = refs[0], refs[1:16], refs[16:]
    (normed, q_in, k_in, v_in, lse, mixed, mlp, residual, gn2, gy, stream,
     wq, wk, wv, wo, vecs, table, squares) = refs[:18]
    gate_f, up_f, down_f, query_f, kv_f, out_f, small_o, res_o, gtok_o = refs[18:27]
    (mlp_got, gn, gn_got, sides, mask, ga, gm, gq, gk_t, gv_t, grad_res,
     small_buf, small_got) = refs[27:40]
    x_send, x_recv, send, recv, s_send, s_recv = refs[40:46]
    r_buf, r_mid0, r_mid1, r_send, r_recv, t_buf, t_mid0, t_mid1, t_send, t_recv = refs[46:56]
    refs = list(refs[56:])
    dp, t = coords()
    spot = (dp // 8 + t * (1 - 2 * (dp // 8 % 2)), dp % 8)
    length = lengths[group_of(dp, t)]
    swap_gn = Swap(gn, gn_got, x_send.at[0], x_recv.at[0], dp, t)
    swap_mlp = Swap(mlp, mlp_got, x_send.at[1], x_recv.at[1], dp, t)
    mail_res = Mail(r_buf, (r_mid0, r_mid1), res_o, spot, r_send, r_recv, dp, t)
    mail_tok = Mail(t_buf, (t_mid0, t_mid1), gtok_o, spot, t_send, t_recv, dp, t)
    across = (partner("x", *partner("core", dp, t)))
    greet(neighbours(dp, t) + [swap_gn.who, across])
    plan = Plan()
    chains = []
    for n in range(15):
        p, j, rows, lanes, kinds = kind_of(n)
        c = Chain(rows, lanes, kinds, TURN[n], dp, t)
        c.gots = [None] * (STAGE[n] + 1) + [refs.pop(0) for _ in range(STAGE[n] + 1, 6)]
        c.bufs = list(c.gots)
        c.bufs[STAGE[n]] = parts_in[n]
        c.send, c.recv = send.at[n], recv.at[n]
        c.full, c.base = (gate_f, up_f, down_f)[j], (0, 512 * p) if j < 2 else (512 * p, 0)
        chains.append(c)
    late, late_whole = [], []
    for i in range(9):
        c = Chain(128, 896, K_KINDS, LATE_TURN[i], dp, t)
        if i % 4 == 0:
            whole = refs.pop(0)
        c.source = whole.at[pl.ds(128 * (i % 4), 128), :] if i < 8 else whole
        c.gots = [refs.pop(0) for _ in range(6)]
        c.bufs = c.gots + [c.source]
        c.send, c.recv = send.at[15 + i], recv.at[15 + i]
        c.full, c.base = (query_f, out_f, kv_f)[i // 4], (128 * (i % 4), 0)
        late.append(c)
        if i % 4 == 0:
            late_whole.append(whole)
    q_src, o_src, k_src = late_whole
    meeting = plan.add(lambda: met(16), 0.5, rank=0)
    for n, c in enumerate(chains):
        follow(plan, c, STAGE[n] + 1, 5, [meeting], RANK[n], True)
    swapped = [Message("tn", 128 * 896 * 2.0) for _ in range(4)]
    sent = plan.add(lambda: [swap_mlp.start(j) for j in range(4)], 0.2, [meeting], sends=swapped, rank=3)

    def norm_two(i):
        at = pl.ds(i * 128, 128)
        res, grad = residual[at, :], gn2[at, :]
        inverse = lax.rsqrt(jnp.mean(res * res, axis=-1, keepdims=True) + epsilon)
        unit = res * inverse
        total = jnp.sum((grad * unit).reshape(16, 8, 896), axis=0)
        scaled = grad * vecs[1:2, :]
        mean = jnp.mean(scaled * unit, axis=-1, keepdims=True)
        final = gy[at, :].astype(F32) + inverse * (scaled - unit * mean)
        grad_res[at, :] = final
        ga[at, :] = final.astype(BF)
        if i == 0:
            small_buf[0] = jnp.zeros((8, 896), F32)
        small_buf[0, 1:2, :] += jnp.sum(total, axis=0, keepdims=True)

    normed_back = [plan.add(functools.partial(norm_two, i), 0.6, rank=5) for i in range(4)]
    meeting["after"] = normed_back[:1]

    def prepare():
        fill_mask(mask, length)
        for side in range(2):
            sides[side] = one_head(k_in[...], side)
            sides[2 + side] = one_head(v_in[...], side)
        gk_t[...] = jnp.zeros((64, 512), F32)
        gv_t[...] = jnp.zeros((64, 512), F32)

    prepared = plan.add(prepare, 0.6, rank=5)

    def out_back():
        gm[:, pl.ds(384, 128)] = jnp.zeros((512, 128), BF)
        gm[:, pl.ds(0, 448)] = mm_t(ga[...], wo[...]).astype(BF)

    mixed_back = plan.add(out_back, 0.8, normed_back, rank=5)

    def heads(b, p):
        rows, keys = pl.ds(256 * b, 256), pl.ds(0, 256 * (b + 1))
        lanes = pl.ds(128 * p, 128)
        cos, sin = spread(table[rows, :])
        pair, pair_gm = q_in[rows, lanes], gm[rows, lanes]
        pair_t, pair_gm_t = pair.T, pair_gm.T
        grad = jnp.zeros((256, 128), F32)
        for side in range(2 if p < 3 else 1):
            h = 2 * p + side
            score = mm_t(pair, sides[side, keys, :]) + mask[rows, keys]
            probs = jnp.exp(score - lse[rows, h : h + 1])
            grad_probs = mm_t(pair_gm, sides[2 + side, keys, :])
            inner = jnp.sum(probs * grad_probs, axis=-1, keepdims=True)
            grad_scores = (probs * (grad_probs - inner)).astype(BF)
            grad = grad + mm(grad_scores, sides[side, keys, :])
            half = slice(64 * side, 64 * side + 64)
            gk_t[:, keys] += mm(pair_t[half, :], grad_scores)
            gv_t[:, keys] += mm(pair_gm_t[half, :], probs.astype(BF))
        gq[rows, lanes] = turn(grad, cos, -sin).astype(BF)

    key_grads = [None, None]

    def norm_part(b):
        rows = pl.ds(256 * b, 256)
        flat = table[rows, :].T
        cos_t, sin_t = flat[0:32], flat[64:96]
        one, two = gk_t[0:32, rows] * 0.125, gk_t[32:64, rows] * 0.125
        whole = jnp.concatenate([one * cos_t + two * sin_t, two * cos_t - one * sin_t, gv_t[:, rows]], axis=0).astype(BF)
        gkv = whole.T
        key_grads[b] = (whole, jnp.sum(gkv.astype(F32), axis=0, keepdims=True))
        part = mm(gq[rows, pl.ds(0, 448)], wq[...]) + mm(gkv[:, 0:64], wk[...]) + mm(gkv[:, 64:128], wv[...])
        gn[rows, :] = part.astype(BF)
        swap_gn.start(2 * b)
        swap_gn.start(2 * b + 1)

    returned = [Message("tn", 128 * 896 * 2.0) for _ in range(4)]
    before, parts = [prepared, mixed_back], [None, None]
    for b in (1, 0):
        before = [plan.add(functools.partial(heads, b, p), (1.0 + b) * (1.0 if p < 3 else 0.5), before, rank=5) for p in range(4)][-1:]
        parts[b] = plan.add(functools.partial(norm_part, b), 1.0, before + [meeting], sends=returned[2 * b : 2 * b + 2], rank=5)
        before = [parts[b]]

    def make_kv():
        whole = jnp.concatenate([key_grads[0][0], key_grads[1][0]], axis=1)
        k_src[...] = mm(whole, normed[...]).astype(BF)
        small_buf[0, 2:3, 0:448] = jnp.sum(gq[:, pl.ds(0, 448)].astype(F32), axis=0, keepdims=True)
        small_buf[0, 2:3, 512:640] = key_grads[0][1] + key_grads[1][1]
        small_buf[0, 3:4, :] = jnp.sum(squares[...], axis=0, keepdims=True)

    def make_q():
        q_src[...] = t_mm(gq[...], normed[...]).astype(BF)

    def make_o():
        o_src[...] = t_mm(mixed[...], ga[...]).astype(BF)

    made_q = plan.add(make_q, 0.8, [parts[0]], rank=5)
    made_kv = plan.add(make_kv, 0.6, [parts[0]], rank=5)
    made_o = plan.add(make_o, 0.8, [mixed_back], rank=4.5)
    for i, c in enumerate(late):
        follow(plan, c, 0, 5, [(made_q, made_o, made_kv)[i // 4], meeting], LATE_RANK[i], True)

    def output(i):
        at = pl.ds(i * 128, 128)
        valid = lax.broadcasted_iota(jnp.int32, (128, 896), 0) + i * 128 < length
        branch = jnp.where(valid, swap_mlp.take(i), 0.0)
        result = jnp.where(valid, residual[at, :] + branch, 0.0)
        r_buf[pl.ds(i * 2, 2)] = result.reshape(2, 8, 8, 896).astype(BF)
        for row, x in ((4, result), (5, branch)):
            some = jnp.sum((x * x).reshape(16, 8, 896), axis=0)
            small_buf[0, row : row + 1, :] += jnp.sum(some, axis=0, keepdims=True)

    outputs = [plan.add(functools.partial(output, i), 0.5, [sent] + normed_back, swapped[i : i + 1], rank=6) for i in range(4)]

    def post(mail, ready, rank):
        one, two = Message("all", 2 * 458752.0), Message("all", 2 * 458752.0)
        a = plan.add(mail.first, 0.8, ready, sends=[one], rank=rank)
        b = plan.add(mail.second, 0.9, [a], [one], [two], rank)
        plan.add(mail.last, 0.2, [b], [two], rank=rank)

    post(mail_res, outputs + [meeting], MAIL_RANK[0])

    def norm_one(i):
        at = pl.ds(i * 128, 128)
        grad = swap_gn.take(i)
        row = stream[at, :].astype(F32)
        inverse = lax.rsqrt(jnp.mean(row * row, axis=-1, keepdims=True) + epsilon)
        unit = row * inverse
        total = jnp.sum((grad * unit).reshape(16, 8, 896), axis=0)
        scaled = grad * vecs[0:1, :]
        mean = jnp.mean(scaled * unit, axis=-1, keepdims=True)
        final = grad_res[at, :] + inverse * (scaled - unit * mean)
        t_buf[pl.ds(i * 2, 2)] = final.reshape(2, 8, 8, 896).astype(BF)
        small_buf[0, 0:1, :] += jnp.sum(total, axis=0, keepdims=True)

    finals = [plan.add(functools.partial(norm_one, i), 0.6, [parts[i // 2]], returned[i : i + 1], rank=1) for i in range(4)]
    post(mail_tok, finals, MAIL_RANK[1])

    def quartet(s):
        if s == 0:
            return [partner("core", dp, t), partner("x", dp, t), across]
        one, two = ("ya", "yb") if s == 1 else ("za", "zb")
        return [partner(one, dp, t), partner(two, dp, t), partner(one, *partner(two, dp, t))]

    posted = {}

    def share(s):
        posted[s] = [
            remote(small_buf.at[s], small_got.at[3 * s + i], s_send.at[3 * s + i], s_recv.at[3 * s + i], who)
            for i, who in enumerate(quartet(s))
        ]
        for c in posted[s]:
            c.start()

    def collect(s):
        for c in posted[s]:
            c.wait()
        small_buf[s + 1] = (small_buf[s] + small_got[3 * s]) + (small_got[3 * s + 1] + small_got[3 * s + 2])
        if s < 2:
            share(s + 1)
        else:
            small_o[...] = small_buf[3]

    message = Message("x", 28672.0)
    task = plan.add(functools.partial(share, 0), 0.2, finals + outputs + [made_kv], sends=[message], rank=1)
    for s in range(3):
        after = Message(("ya", "za", "za")[s], 28672.0)
        task = plan.add(functools.partial(collect, s), 0.2, [task], [message], [after] if s < 2 else [], rank=1)
        message = after
    plan.run()


def finish(*operands):
    wide_out = pltpu.VMEM((896, 2560), BF), pltpu.VMEM((896, 2560), BF), pltpu.VMEM((2560, 896), BF)
    room = []
    for n in range(15):
        room += [pltpu.VMEM(stage_shape(n, s), BF) for s in range(STAGE[n] + 1, 6)]
    for i in range(9):
        if i % 4 == 0:
            room.append(pltpu.VMEM((512 if i < 8 else 128, 896), BF))
        room += [pltpu.VMEM(x, BF) for x in K_SHAPES]
    return pl.pallas_call(
        finish_kernel,
        out_shape=(
            *wide_out,
            pltpu.VMEM((512, 896), BF),
            pltpu.VMEM((128, 896), BF),
            pltpu.VMEM((512, 896), BF),
            pltpu.VMEM((8, 896), F32),
            pltpu.VMEM((8, 8, 8, 896), BF),
            pltpu.VMEM((8, 8, 8, 896), BF),
        ),
        in_specs=[SMEM_SPEC] + [VMEM_SPEC] * 33,
        out_specs=(VMEM_SPEC,) * 9,
        scratch_shapes=[
            pltpu.VMEM((512, 896), BF),
            pltpu.VMEM((512, 896), BF),
            pltpu.VMEM((512, 896), BF),
            pltpu.VMEM((4, 512, 128), BF),
            pltpu.VMEM((512, 512), F32),
            pltpu.VMEM((512, 896), BF),
            pltpu.VMEM((512, 512), BF),
            pltpu.VMEM((512, 512), BF),
            pltpu.VMEM((64, 512), F32),
            pltpu.VMEM((64, 512), F32),
            pltpu.VMEM((512, 896), F32),
            pltpu.VMEM((4, 8, 896), F32),
            pltpu.VMEM((9, 8, 896), F32),
            DMA((2, 4)), DMA((2, 4)), DMA((24, 12)), DMA((24, 12)), DMA((9,)), DMA((9,)),
            *MAIL_SCRATCH, *MAIL_SCRATCH, *room,
        ],
        compiler_params=params(4, 38 << 20),
        name="finish",
    )(*[in_vmem(x) if i in FROM_WIDE else x for i, x in enumerate(operands)])


def unpack_kernel(
    order, lengths, gate, up, down, query, kv, out_w, small, res, gtok,
    gate_o, up_o, down_o, query_o, key_o, value_o, out_o, res_o, gtok_o, gain1_o, gain2_o, bq_o, bk_o, bv_o, rms_o,
    where_from,
):
    i = pl.program_id(0)

    @pl.when(i == 0)
    def _():
        def note(g, carry):
            where_from[order[g]] = g
            return carry + lengths[g]

        count = lax.fori_loop(0, 64, note, 0).astype(F32) * 896.0
        rms = jnp.sqrt(jnp.sum(small[...], axis=-1, keepdims=True) / count)
        lane = lax.broadcasted_iota(jnp.int32, (1, 128), 1)
        line = jnp.where(lane == 0, rms[4:5], jnp.where(lane == 1, rms[3:4], rms[5:6]))
        gain1_o[...] = small[0, :]
        gain2_o[...] = small[1, :]
        bq_o[...] = small[2, 0:448]
        pair = small[2:3, 512:640]
        bk_o[...] = pair[0, 0:64]
        bv_o[...] = pltpu.roll(pair, 64, 1)[0, 0:64]
        rms_o[...] = line[0, 0:3]
        key_o[...] = kv[pl.ds(0, 64), :].astype(F32)
        value_o[...] = kv[pl.ds(64, 64), :].astype(F32)

    rows = pl.ds(pl.multiple_of(i * 64, 64), 64)
    gate_o[...] = gate[rows, pl.ds(0, 2432)].astype(F32)
    up_o[...] = up[rows, pl.ds(0, 2432)].astype(F32)
    down_o[...] = down[pl.ds(pl.multiple_of(i * 176, 16), 176), :].astype(F32)

    @pl.when(i < 7)
    def _():
        query_o[...] = query[rows, :].astype(F32)
        out_o[...] = out_w[rows, :].astype(F32)

    @pl.when(i < 8)
    def _():
        for j in range(8):
            slot = where_from[jnp.minimum(i, 7) * 8 + j]
            res_o[j] = res[slot]
            gtok_o[j] = gtok[slot]


def unpack(*operands):
    rows = lambda i: (i, 0)
    some = lambda i: (jnp.minimum(i, 6), 0)
    return pl.pallas_call(
        unpack_kernel,
        grid=(14,),
        out_shape=(
            jax.ShapeDtypeStruct((896, 2432), F32),
            jax.ShapeDtypeStruct((896, 2432), F32),
            jax.ShapeDtypeStruct((2432, 896), F32),
            jax.ShapeDtypeStruct((448, 896), F32),
            jax.ShapeDtypeStruct((64, 896), F32),
            jax.ShapeDtypeStruct((64, 896), F32),
            jax.ShapeDtypeStruct((448, 896), F32),
            BLOCK,
            BLOCK,
            *[jax.ShapeDtypeStruct((n,), F32) for n in (896, 896, 448, 64, 64, 3)],
        ),
        in_specs=[SMEM_SPEC] * 2 + [VMEM_SPEC] * 9,
        out_specs=(
            pl.BlockSpec((64, 2432), rows),
            pl.BlockSpec((64, 2432), rows),
            pl.BlockSpec((176, 896), rows),
            pl.BlockSpec((64, 896), some),
            pl.BlockSpec((64, 896), lambda i: (0, 0)),
            pl.BlockSpec((64, 896), lambda i: (0, 0)),
            pl.BlockSpec((64, 896), some),
            pl.BlockSpec((8, 8, 896), lambda i: (jnp.minimum(i, 7), 0, 0)),
            pl.BlockSpec((8, 8, 896), lambda i: (jnp.minimum(i, 7), 0, 0)),
            *[VMEM_SPEC] * 6,
        ),
        scratch_shapes=[pltpu.SMEM((64,), jnp.int32)],
        compiler_params=pltpu.CompilerParams(vmem_limit_bytes=16 << 20),
        name="unpack",
    )(*operands[:2], *[pltpu.with_memory_space_constraint(x, pltpu.VMEM) for x in operands[2:]])


def on_device(
    tokens,
    cotangent,
    lengths,
    deal_order,
    gain_attn,
    w_query,
    b_query,
    w_key,
    b_key,
    w_value,
    b_value,
    w_out,
    gain_mlp,
    w_gate,
    w_up,
    w_down,
):
    table = jnp.asarray(rope_table())
    biases = jnp.concatenate([b_query, b_key, b_value, jnp.zeros((320,), BF)])
    blank = jnp.zeros((896,), BF)
    vecs = jnp.stack([gain_attn, gain_mlp, biases] + [blank] * 5).astype(F32)
    normed, q, k, v, lse, mixed, residual, normed_two, gy, squares, stream = meet(
        deal_order, lengths, tokens, cotangent, w_query.T, w_key.T, w_value.T, w_out, vecs, table
    )
    gn2, mlp, *sums = wide(normed_two, gy, w_gate, w_up, w_down)
    gate, up, down, query, kv, out_w, small, sent_res, sent_tok = finish(
        lengths, *sums, normed, q, k, v, lse, mixed, mlp, residual, gn2, gy, stream,
        w_query.T, w_key.T, w_value.T, w_out, vecs, table, squares,
    )
    (
        gate, up, down, query, key, value, out_w, layer_out, grad_tokens,
        gain_one, gain_two, bias_query, bias_key, bias_value, rms_values,
    ) = unpack(
        deal_order, lengths, gate, up, down, query, kv, out_w, small,
        sent_res.reshape(64, 8, 896), sent_tok.reshape(64, 8, 896),
    )
    return (
        layer_out,
        grad_tokens,
        gain_one,
        query.T,
        bias_query,
        key.T,
        bias_key,
        value.T,
        bias_value,
        out_w,
        gain_two,
        gate,
        up,
        down,
        rms_values,
    )


def solution(mesh):
    in_specs = (
        P(None, "dp", None),
        P(None, "dp", None),
        P(),
        P(),
        P(),
        P(None, "tensor"),
        P("tensor"),
        P(None, "tensor"),
        P("tensor"),
        P(None, "tensor"),
        P("tensor"),
        P("tensor", None),
        P(),
        P(None, "tensor"),
        P(None, "tensor"),
        P("tensor", None),
    )
    out_specs = (
        P(None, "dp", None),
        P(None, "dp", None),
        P(),
        P(None, "tensor"),
        P("tensor"),
        P(None, "tensor"),
        P("tensor"),
        P(None, "tensor"),
        P("tensor"),
        P("tensor", None),
        P(),
        P(None, "tensor"),
        P(None, "tensor"),
        P("tensor", None),
        P(),
    )
    return jax.shard_map(
        on_device, mesh=mesh, in_specs=in_specs, out_specs=out_specs, check_vma=False
    )
```

```python
import functools
import math

import jax
import jax.numpy as jnp
import numpy as np
from jax import lax
from jax.experimental import pallas as pl
from jax.experimental.pallas import tpu as pltpu
from jax.sharding import PartitionSpec as P

MESH = pl.DeviceIdType.MESH
HD = 64
epsilon = 1e-06
rope_base = 1000000.0
VMEM_LIMIT = 60 << 20
LINKS = ("x", "ya", "za", "yb", "zb")


def flip(dp):
    return dp + 8 - 16 * ((dp // 8) % 2)


def group_of(dp, t):
    return dp + t * (flip(dp) - dp)


def coords():
    return lax.axis_index("dp"), lax.axis_index("tensor")


def partner(dim, dp, t):
    y, xl, z, c = dp // 16, (dp // 8) % 2, (dp // 2) % 4, dp % 2
    if dim == "core":
        c = 1 - c
    if dim == "x":
        xl = 1 - xl
    if dim == "ya":
        y = y + 1 - 2 * (y % 2)
    if dim == "yb":
        y = 3 - y
    if dim == "za":
        z = z + 1 - 2 * (z % 2)
    if dim == "zb":
        z = 3 - z
    if dim == "tn":
        xl, t = 1 - xl, 1 - t
    return (((y * 2 + xl) * 4 + z) * 2 + c, t)


def bit(dim, dp):
    y, xl, z, c = dp // 16, (dp // 8) % 2, (dp // 2) % 4, dp % 2
    return {
        "core": c,
        "x": xl,
        "ya": ((y + 1) // 2) % 2,
        "yb": y // 2,
        "za": ((z + 1) // 2) % 2,
        "zb": z // 2,
    }[dim]


def greet(partners):
    barrier = pltpu.get_barrier_semaphore()
    for who in partners:
        pl.semaphore_signal(barrier, inc=1, device_id=who, device_id_type=MESH)


def around(dp, t, axis, j):
    a, b = dp // 8, dp % 8
    return (((a + j) % 8 * 8 + b) if axis == 0 else a * 8 + (b + j) % 8, t)


def neighbours(dp, t):
    return [around(dp, t, axis, j) for axis in range(2) for j in range(1, 8)]


def met(n):
    pl.semaphore_wait(pltpu.get_barrier_semaphore(), n)


def remote(src, dst, send, recv, who):
    return pltpu.make_async_remote_copy(
        src_ref=src, dst_ref=dst, send_sem=send, recv_sem=recv, device_id=who, device_id_type=MESH
    )


def put_sum(dst, src, row, lane, other, rows, lanes):
    step = 16
    while step * 2 * lanes <= 32768 and rows % (step * 2) == 0:
        step *= 2

    def body(i, carry):
        here = pl.ds(pl.multiple_of(i * step, 16), step)
        there = pl.ds(pl.multiple_of(row + i * step, 16), step)
        lane_at = lane if isinstance(lane, int) else pl.multiple_of(lane, 128)
        dst[here, :] = src[there, pl.ds(lane_at, lanes)] + other[here, :]
        return carry

    lax.fori_loop(0, rows // step, body, 0)


def halves(rows, lanes, kinds):
    out = []
    for kind in kinds:
        if kind == "r":
            rows //= 2
        elif kind == "l":
            lanes //= 2
        out.append((rows, lanes))
    return out


class Chain:
    def __init__(self, rows, lanes, kinds, turn, dp, t):
        self.kinds = kinds
        self.dims = ("core",) + tuple(LINKS[(turn + i) % 5] for i in range(5))
        self.who = [partner(d, dp, t) for d in self.dims]
        self.bits = [bit(d, dp) for d in self.dims]
        self.shapes = [(rows, lanes)] + halves(rows, lanes, kinds)
        self.last = max(i for i, kind in enumerate(kinds) if kind != "f")
        self.corner = [(0, 0)]
        for s, kind in enumerate(kinds):
            row, lane = self.corner[-1]
            rows, lanes = self.shapes[s + 1]
            b = self.bits[s]
            self.corner.append((row + (b * rows if kind == "r" else 0), lane + (b * lanes if kind == "l" else 0)))

    def start(self, s, src, got, send, recv):
        rows, lanes = self.shapes[s + 1]
        give, self.keep = (0, 0), (0, 0)
        b = self.bits[s]
        if self.kinds[s] == "r":
            give, self.keep = (pl.multiple_of((1 - b) * rows, 16), 0), (b * rows, 0)
        elif self.kinds[s] == "l":
            give, self.keep = (0, pl.multiple_of((1 - b) * lanes, 128)), (0, b * lanes)
        self.src, self.got = src, got
        self.copy = remote(src.at[pl.ds(give[0], rows), pl.ds(give[1], lanes)], got, send, recv, self.who[s])
        self.copy.start()

    def finish(self, s, dst):
        self.copy.wait()
        rows, lanes = self.shapes[s + 1]
        put_sum(dst, self.src, self.keep[0], self.keep[1], self.got, rows, lanes)

    def spot(self, s, full, base):
        rows, lanes = self.shapes[s]
        row, lane = self.corner[s]
        row, lane = row + base[0], lane + base[1]
        row = row if isinstance(row, int) else pl.multiple_of(row, 16)
        lane = lane if isinstance(lane, int) else pl.multiple_of(lane, 128)
        return full.at[pl.ds(row, rows), pl.ds(lane, lanes)]

    def gather_start(self, s, full, base, send, recv):
        mine = self.spot(s + 1, full, base)
        self.copy = remote(mine, mine, send, recv, self.who[s])
        self.copy.start()

    def gather_finish(self):
        self.copy.wait()


G_KINDS = ("l", "l", "r", "r", "r", "f")
D_KINDS = ("r", "r", "r", "r", "r", "f")
K_KINDS = ("r", "r", "r", "f", "f", "f")
ANY_SPEC = pl.BlockSpec(memory_space=pl.ANY)
G_SHAPES = halves(896, 512, G_KINDS)
D_SHAPES = halves(512, 896, D_KINDS)
K_SHAPES = halves(128, 896, K_KINDS)
BF, F32 = jnp.bfloat16, jnp.float32
VMEM_SPEC = pl.BlockSpec(memory_space=pltpu.VMEM)
SMEM_SPEC = pl.BlockSpec(memory_space=pltpu.SMEM)
BLOCK = jax.ShapeDtypeStruct((64, 8, 896), BF)
DMA = pltpu.SemaphoreType.DMA


def params(cid, limit=VMEM_LIMIT):
    return pltpu.CompilerParams(collective_id=cid, has_side_effects=True, vmem_limit_bytes=limit)


class Mail:
    LOW = 512

    def __init__(self, buf, mids, out, spot, send, recv, dp, t):
        self.buf, self.mids, self.out = buf, mids, out
        self.me = (dp // 8, dp % 8)
        self.spot = spot
        self.send, self.recv, self.dp, self.t = send, recv, dp, t
        self.lanes = (pl.ds(0, self.LOW), pl.ds(self.LOW, 896 - self.LOW))

    def first(self):
        self.copies = [[], []]
        for j in range(1, 8):
            for f in range(2):
                to = (self.me[f] + j) % 8
                src = self.buf.at[to, :, :, self.lanes[f]] if f == 0 else self.buf.at[:, to, :, self.lanes[f]]
                c = remote(src, self.mids[f].at[self.spot[f]], self.send.at[0, f, j], self.recv.at[0, f, j],
                           around(self.dp, self.t, f, j))
                c.start()
                self.copies[f].append(c)
        for f in range(2):
            me = self.me[f]
            own = self.buf[me, :, :, self.lanes[f]] if f == 0 else self.buf[:, me, :, self.lanes[f]]
            self.mids[f][self.spot[f]] = own

    def second(self):
        for f in range(2):
            for c in self.copies[f]:
                c.wait()
        self.copies = []
        for j in range(1, 8):
            for f in range(2):
                g = 1 - f
                to = (self.me[g] + j) % 8
                dst = self.out.at[:, self.spot[1], :, self.lanes[f]] if f == 0 else self.out.at[self.spot[0], :, :, self.lanes[f]]
                c = remote(self.mids[f].at[:, to], dst, self.send.at[1, f, j], self.recv.at[1, f, j],
                           around(self.dp, self.t, g, j))
                c.start()
                self.copies.append(c)
        for f in range(2):
            own = self.mids[f][:, self.me[1 - f]]
            if f == 0:
                self.out[:, self.spot[1], :, self.lanes[f]] = own
            else:
                self.out[self.spot[0], :, :, self.lanes[f]] = own

    def last(self):
        for c in self.copies:
            c.wait()


MAIL = jax.ShapeDtypeStruct((8, 8, 8, 896), BF)
MAIL_SCRATCH = [
    pltpu.VMEM((8, 8, 8, 896), BF), pltpu.VMEM((8, 8, 8, 512), BF), pltpu.VMEM((8, 8, 8, 384), BF),
    DMA((2, 2, 8)), DMA((2, 2, 8)),
]


def sort_out(order, rows, buf, dp, t):
    for a in range(8):
        for b in range(8):
            buf[a, b] = rows[order[group_of(a * 8 + b, t)]]


def mm(a, b):
    return jnp.dot(a, b, preferred_element_type=F32)


def mm_t(a, b):
    return lax.dot_general(a, b, (((1,), (1,)), ((), ())), preferred_element_type=F32)


def t_mm(a, b):
    return lax.dot_general(a, b, (((0,), (0,)), ((), ())), preferred_element_type=F32)


def rope_table():
    places = np.arange(512, dtype=np.float32)
    frequency = np.power(np.float32(rope_base), -np.arange(32, dtype=np.float32) * np.float32(2.0 / HD)).astype(np.float32)
    angles = (places[:, None] * frequency[None, :]).astype(np.float64)
    cos, sin = np.cos(angles), np.sin(angles)
    return np.concatenate([cos, cos, sin, sin], axis=1).astype(np.float32)


def first_half(shape):
    return lax.broadcasted_iota(jnp.int32, shape, 1) % 64 < 32


def spread(table):
    other = pltpu.roll(table, 64, 1)
    low = lax.broadcasted_iota(jnp.int32, table.shape, 1) < 64
    cos, sin = jnp.where(low, table, other), jnp.where(low, other, table)
    return cos, jnp.where(first_half(table.shape), -sin, sin)


def turn(x, cos, sin):
    swapped = jnp.where(first_half(x.shape), pltpu.roll(x, 96, 1), pltpu.roll(x, 32, 1))
    return x * cos + swapped * sin


def one_head(pair, side):
    low = lax.broadcasted_iota(jnp.int32, pair.shape, 1) < 64
    return jnp.where(low if side == 0 else jnp.logical_not(low), pair, jnp.zeros_like(pair))


def fill_mask(mask, length):
    for b in range(2):
        rows = lax.broadcasted_iota(jnp.int32, (256, 512), 0) + b * 256
        cols = lax.broadcasted_iota(jnp.int32, (256, 512), 1)
        mask[pl.ds(b * 256, 256), :] = jnp.where((cols <= rows) & (cols < length), 0.0, -1e30)


class Swap:
    def __init__(self, x, got, send, recv, dp, t):
        self.who = partner("tn", dp, t)
        self.x, self.got, self.send, self.recv = x, got, send, recv
        self.copies = [None] * 4

    def start(self, i):
        rows = pl.ds(i * 128, 128)
        self.copies[i] = remote(self.x.at[rows], self.got.at[rows], self.send.at[i], self.recv.at[i], self.who)
        self.copies[i].start()

    def take(self, i):
        self.copies[i].wait()
        rows = pl.ds(i * 128, 128)
        return self.x[rows, :].astype(F32) + self.got[rows, :].astype(F32)


def meet_kernel(
    order, lengths, tok, cot, wq, wk, wv, wo, vecs, table,
    normed, q_o, k_o, v_o, lse_o, mixed, residual, normed_two, gy, squares, stream,
    sides, mask, x, got, tok_in, cot_in, send, recv, buf, mid0, mid1, c_send, c_recv, t_buf, t_mid0, t_mid1, t_send, t_recv,
):
    dp, t = coords()
    swap = Swap(x, got, send, recv, dp, t)
    mail = Mail(buf, (mid0, mid1), cot_in, (dp // 8, dp % 8), c_send, c_recv, dp, t)
    greet(neighbours(dp, t) + [swap.who])
    length = lengths[group_of(dp, t)]
    sort_out(order, tok, t_buf, dp, t)
    tokens = Mail(t_buf, (t_mid0, t_mid1), tok_in, (dp // 8, dp % 8), t_send, t_recv, dp, t)
    met(15)
    tokens.first()
    sort_out(order, cot, buf, dp, t)
    fill_mask(mask, length)
    tokens.second()
    tokens.last()
    mail.first()
    for b in range(4):
        rows, keys = pl.ds(128 * b, 128), pl.ds(0, 128 * (b + 1))
        row = tok_in[pl.ds(b * 2, 2)].astype(F32).reshape(128, 896)
        stream[rows, :] = row.astype(BF)
        inverse = lax.rsqrt(jnp.mean(row * row, axis=-1, keepdims=True) + epsilon)
        unit = (row * inverse * vecs[0:1, :]).astype(BF)
        normed[rows, :] = unit
        cos, sin = spread(table[rows, :])
        k = mm_t(unit, wk[...]) + vecs[2:3, 448:512]
        v = mm_t(unit, wv[...]) + vecs[2:3, 512:576]
        k2 = turn(jnp.concatenate([k, k], axis=1), cos, sin)
        k2 = (k2.astype(BF).astype(F32) * 0.125).astype(BF)
        v2 = jnp.concatenate([v, v], axis=1).astype(BF)
        k_o[rows, :] = k2
        v_o[rows, :] = v2
        for side in range(2):
            sides[side, rows, :] = one_head(k2, side)
            sides[2 + side, rows, :] = one_head(v2, side)
        q = mm_t(unit, wq[...]) + vecs[2:3, 0:448]
        q = jnp.concatenate([q, jnp.zeros((128, 64), F32)], axis=1)
        for p in range(4):
            q_o[rows, pl.ds(128 * p, 128)] = turn(q[:, 128 * p : 128 * p + 128], cos, sin).astype(BF)
        lse_o[rows, :] = jnp.zeros((128, 128), F32)

        def heads(p, both):
            lanes = pl.ds(pl.multiple_of(128 * p, 128), 128)
            pair = q_o[rows, lanes]
            total = jnp.zeros((128, 128), F32)
            for side in range(2 if both else 1):
                score = mm_t(pair, sides[side, keys, :]) + mask[rows, keys]
                top = jnp.max(score, axis=-1, keepdims=True)
                expo = jnp.exp(score - top)
                mass = jnp.sum(expo, axis=-1, keepdims=True)
                probs = (expo * (1.0 / mass)).astype(BF)
                total = total + mm(probs, sides[2 + side, keys, :])
                here = lax.broadcasted_iota(jnp.int32, (128, 128), 1) == 2 * p + side
                lse_o[rows, :] = jnp.where(here, top + jnp.log(mass), lse_o[rows, :])
            mixed[rows, lanes] = total.astype(BF)

        for p in range(4):
            heads(p, p < 3)
        x[rows, :] = mm(mixed[rows, pl.ds(0, 448)], wo[...]).astype(BF)
        swap.start(b)
        if b == 1:
            mail.second()
    total = jnp.zeros((8, 896), F32)
    for i in range(4):
        at = pl.ds(i * 128, 128)
        valid = lax.broadcasted_iota(jnp.int32, (128, 896), 0) + i * 128 < length
        attention = swap.take(i)
        res = stream[at, :].astype(F32) + attention
        residual[at, :] = res
        inverse = lax.rsqrt(jnp.mean(res * res, axis=-1, keepdims=True) + epsilon)
        normed_two[at, :] = (res * inverse * vecs[1:2, :]).astype(BF)
        kept = jnp.where(valid, attention, 0.0)
        total = total + jnp.sum((kept * kept).reshape(16, 8, 896), axis=0)
    squares[...] = total
    mail.last()
    for i in range(4):
        at = pl.ds(i * 128, 128)
        valid = lax.broadcasted_iota(jnp.int32, (128, 896), 0) + i * 128 < length
        gy[at, :] = jnp.where(valid, cot_in[pl.ds(i * 2, 2)].astype(F32).reshape(128, 896), 0.0).astype(BF)


def meet(*operands):
    rows = jax.ShapeDtypeStruct((512, 896), BF)
    wide_rows = jax.ShapeDtypeStruct((512, 512), BF)
    pair = jax.ShapeDtypeStruct((512, 128), BF)
    return pl.pallas_call(
        meet_kernel,
        out_shape=(
            rows, wide_rows, pair, pair, jax.ShapeDtypeStruct((512, 128), F32), wide_rows,
            jax.ShapeDtypeStruct((512, 896), F32), rows, rows, jax.ShapeDtypeStruct((8, 896), F32), rows,
        ),
        in_specs=[SMEM_SPEC] * 2 + [VMEM_SPEC] * 8,
        out_specs=(VMEM_SPEC,) * 11,
        scratch_shapes=[
            pltpu.VMEM((4, 512, 128), BF),
            pltpu.VMEM((512, 512), F32),
            pltpu.VMEM((512, 896), BF),
            pltpu.VMEM((512, 896), BF),
            pltpu.VMEM((8, 8, 8, 896), BF),
            pltpu.VMEM((8, 8, 8, 896), BF),
            DMA((4,)), DMA((4,)), *MAIL_SCRATCH, *MAIL_SCRATCH,
        ],
        compiler_params=params(2),
        name="meet",
    )(*operands)


class Message:
    def __init__(self, link, size):
        self.link, self.size, self.lands = link, size, None


class Plan:
    LATENCY = 3.2
    RATE = {"core": 500e3, "tn": 43e3}

    def __init__(self):
        self.tasks = []

    def add(self, act, cost, after=(), needs=(), sends=(), rank=5):
        task = dict(act=act, cost=cost, after=list(after), needs=list(needs), sends=list(sends), rank=rank, done=False)
        self.tasks.append(task)
        return task

    def run(self):
        now, free = 0.0, {}
        left = list(self.tasks)
        while left:
            open_ = [x for x in left if all(y["done"] for y in x["after"]) and all(m.lands is not None for m in x["needs"])]
            at = {id(x): max([now] + [m.lands for m in x["needs"]]) for x in open_}
            ready = [x for x in open_ if at[id(x)] <= now]
            task = min(ready, key=lambda x: x["rank"]) if ready else min(open_, key=lambda x: at[id(x)])
            now = at[id(task)] + task["cost"]
            task["act"]()
            task["done"] = True
            left.remove(task)
            for m in task["sends"]:
                links = LINKS if m.link == "all" else (m.link,)
                for link in links:
                    begin = max(now, free.get(link, 0.0))
                    free[link] = begin + m.size / len(links) / self.RATE.get(link, 40e3)
                m.lands = max(free[link] for link in links) + self.LATENCY
        return now


def follow(plan, c, first, last, begin, rank, up=False):
    def go(s):
        c.start(s, c.bufs[s - 1], c.gots[s], c.send.at[s], c.recv.at[s])

    def back(s):
        c.gather_start(s, c.full, c.base, c.send.at[6 + s], c.recv.at[6 + s])

    def size(s):
        return 2.0 * c.shapes[s + 1][0] * c.shapes[s + 1][1]

    if first > last and not up:
        return begin
    message = Message(c.dims[first], size(first))
    task = plan.add(functools.partial(go, first), 0.1, begin, sends=[message], rank=rank)
    for k in range(first, last + 1):
        def step(k=k):
            c.finish(k, c.bufs[k])
            if k < last:
                go(k + 1)
            elif up:
                c.spot(6, c.full, c.base)[...] = c.bufs[5][...]
                back(c.last)

        after = None
        if k < last:
            after = Message(c.dims[k + 1], size(k + 1))
        elif up:
            after = Message(c.dims[c.last], size(c.last))
        task = plan.add(step, 0.1 + size(k) / 2e6, [task], [message], [after] if after else [], rank)
        message = after
    if not up:
        return [task]
    for k in range(c.last, -1, -1):
        def step(k=k):
            c.gather_finish()
            if k > 0:
                back(k - 1)

        after = Message(c.dims[k - 1], size(k - 1)) if k > 0 else None
        task = plan.add(step, 0.1, [task], [message], [after] if after else [], rank)
        message = after
    return [task]


EARLY = 3
STAGE = [4, 4, 3, 4, 4, 4, 4, 3, 2, 2, 2, 1, 1, 1, 1]


TURN = [2, 4, 1, 0, 3, 0, 1, 2, 3, 4, 0, 3, 4, 2, 1]


def kind_of(n):
    p, j = n // 3, n % 3
    return (p, j, 896, 512, G_KINDS) if j < 2 else (p, j, 512, 896, D_KINDS)


def stage_shape(n, s):
    _, _, rows, lanes, kinds = kind_of(n)
    return ([(rows, lanes)] + halves(rows, lanes, kinds))[s + 1]


def tile(p):
    return pl.ds(512 * p, 512 if p < 4 else 384)


def wide_kernel(*refs):
    normed, gy, w_gate, w_up, w_down, gn_out, mlp_out = refs[:7]
    parts, refs = refs[7:22], refs[22:]
    gn_total, mlp_total, gn, got, hid, gg, gu, gate_w, up_w, down_w, x_send, x_recv, send, recv, local = refs[:15]
    refs = list(refs[15:])
    dp, t = coords()
    swap = Swap(gn, got, x_send, x_recv, dp, t)
    greet([swap.who] + [partner(d, dp, t) for d in ("core",) + LINKS])
    chains = []
    for n in range(15):
        p, j, rows, lanes, kinds = kind_of(n)
        c = Chain(rows, lanes, kinds, TURN[n], dp, t)
        c.source = refs.pop(0)
        c.gots = [refs.pop(0) for _ in range(STAGE[n] + 1)]
        c.bufs = c.gots[:-1] + [parts[n]] + [c.source]
        c.send, c.recv = send.at[n], recv.at[n]
        chains.append(c)
    loads = []

    def load(p):
        at, w, b = tile(p), 512 if p < 4 else 384, p % 2
        copies = [
            pltpu.make_async_copy(w_gate.at[:, at], gate_w.at[b, :, pl.ds(0, w)], local.at[p, 0]),
            pltpu.make_async_copy(w_up.at[:, at], up_w.at[b, :, pl.ds(0, w)], local.at[p, 1]),
            pltpu.make_async_copy(w_down.at[at, :], down_w.at[b, pl.ds(0, w), :], local.at[p, 2]),
        ]
        for c in copies:
            c.start()
        loads.append(copies)

    def layer(p):
        at, w, b = tile(p), 512 if p < 4 else 384, p % 2
        for c in loads[p]:
            c.wait()
        wg, wu, wd = gate_w.at[b, :, pl.ds(0, w)], up_w.at[b, :, pl.ds(0, w)], down_w.at[b, pl.ds(0, w), :]
        gate = mm(normed[...], wg[...])
        up = mm(normed[...], wu[...])
        back = mm_t(gy[...], wd[...])
        sig = 1.0 / (1.0 + jnp.exp(-gate))
        silu = gate * sig
        hid[:, at] = (silu * up).astype(BF)
        gu[:, at] = (back * silu).astype(BF)
        gg[:, at] = (back * up * sig * (1.0 + gate * (1.0 - sig))).astype(BF)
        mlp = mm(hid[:, at], wd[...])
        grad = mm_t(gg[:, at], wg[...]) + mm_t(gu[:, at], wu[...])
        if p == 0:
            mlp_total[...] = mlp
            gn_total[...] = grad
        elif p < 4:
            mlp_total[...] += mlp
            gn_total[...] += grad
        else:
            mlp_out[...] = (mlp_total[...] + mlp).astype(BF)
            gn[...] = (gn_total[...] + grad).astype(BF)
        if p + 2 < 5:
            load(p + 2)

    def weight(n):
        p, j = n // 3, n % 3
        w, dst = 512 if p < 4 else 384, chains[n].source
        if j < 2:
            dst[:, pl.ds(0, w)] = t_mm(normed[...], (gg, gu)[j][:, tile(p)]).astype(BF)
            if w < 512:
                dst[:, pl.ds(w, 512 - w)] = jnp.zeros((896, 512 - w), BF)
        else:
            dst[pl.ds(0, w), :] = t_mm(hid[:, tile(p)], gy[...]).astype(BF)
            if w < 512:
                dst[pl.ds(w, 512 - w), :] = jnp.zeros((512 - w, 896), BF)

    load(0)
    load(1)
    plan = Plan()
    meeting = plan.add(lambda: met(7), 0.3, rank=6)
    layers, done = [], []
    for p in range(5):
        layers.append(plan.add(functools.partial(layer, p), 3.4 if p < 4 else 2.6, layers[-1:], rank=5))
        if p == 0:
            layers.append(meeting)
            meeting["after"] = layers[:1]
        if p < EARLY:
            layers += [plan.add(functools.partial(weight, 3 * p + j), 0.55, layers[-1:], rank=4) for j in range(3)]
            done += layers[-3:]
    returned = [Message("tn", 128 * 896 * 2.0) for _ in range(4)]
    sent = plan.add(lambda: [swap.start(i) for i in range(4)], 0.2, layers[-1:] + [meeting], sends=returned, rank=0)
    for n in range(3 * EARLY, 15):
        done.append(plan.add(functools.partial(weight, n), 0.55 if n < 12 else 0.4, [sent], rank=5))
    for n, c in enumerate(chains):
        follow(plan, c, 0, STAGE[n], [done[n], meeting], 2)

    def take(i):
        gn_out[pl.ds(i * 128, 128), :] = swap.take(i)

    for i in range(4):
        plan.add(functools.partial(take, i), 0.2, [sent], returned[i : i + 1], rank=3)
    plan.run()


def wide(*operands):
    room = []
    for n in range(15):
        room += [pltpu.VMEM(stage_shape(n, s), BF) for s in range(-1, STAGE[n] + 1)]
    return pl.pallas_call(
        wide_kernel,
        out_shape=(
            pltpu.VMEM((512, 896), F32),
            pltpu.VMEM((512, 896), BF),
            *[pltpu.VMEM(stage_shape(n, STAGE[n]), BF) for n in range(15)],
        ),
        in_specs=[VMEM_SPEC] * 2 + [ANY_SPEC] * 3,
        out_specs=(VMEM_SPEC,) * 17,
        scratch_shapes=[
            pltpu.VMEM((512, 896), F32),
            pltpu.VMEM((512, 896), F32),
            pltpu.VMEM((512, 896), BF),
            pltpu.VMEM((512, 896), BF),
            pltpu.VMEM((512, 2432), BF),
            pltpu.VMEM((512, 2432), BF),
            pltpu.VMEM((512, 2432), BF),
            pltpu.VMEM((2, 896, 512), BF),
            pltpu.VMEM((2, 896, 512), BF),
            pltpu.VMEM((2, 512, 896), BF),
            DMA((4,)), DMA((4,)), DMA((15, 12)), DMA((15, 12)), DMA((5, 3)),
            *room,
        ],
        compiler_params=params(3, 52 << 20),
        name="wide",
    )(*operands)


FROM_WIDE = set(range(1, 16)) | {22, 24}


def in_vmem(x):
    return pltpu.with_memory_space_constraint(x, pltpu.VMEM)


LATE_TURN = [4, 1, 0, 3, 1, 3, 3, 1, 3]
RANK = [4.6, 4, 4, 3.5, 3.5, 6.5, 3.5, 4, 4.2, 3.5, 4.2, 4, 4.2, 4.4, 4.6]
LATE_RANK = [2, 2, 1, 4.1, 1, 4.1, 2, 1, 3]
MAIL_RANK = [3, 0]
SWAP_LATE = 3


def finish_kernel(*refs):
    lengths, parts_in, refs = refs[0], refs[1:16], refs[16:]
    (normed, q_in, k_in, v_in, lse, mixed, mlp, residual, gn2, gy, stream,
     wq, wk, wv, wo, vecs, table, squares) = refs[:18]
    gate_f, up_f, down_f, query_f, kv_f, out_f, small_o, res_o, gtok_o = refs[18:27]
    (mlp_got, gn, gn_got, sides, mask, ga, gm, gq, gk_t, gv_t, grad_res,
     small_buf, small_got) = refs[27:40]
    x_send, x_recv, send, recv, s_send, s_recv = refs[40:46]
    r_buf, r_mid0, r_mid1, r_send, r_recv, t_buf, t_mid0, t_mid1, t_send, t_recv = refs[46:56]
    refs = list(refs[56:])
    dp, t = coords()
    spot = (dp // 8 + t * (1 - 2 * (dp // 8 % 2)), dp % 8)
    length = lengths[group_of(dp, t)]
    swap_gn = Swap(gn, gn_got, x_send.at[0], x_recv.at[0], dp, t)
    swap_mlp = Swap(mlp, mlp_got, x_send.at[1], x_recv.at[1], dp, t)
    mail_res = Mail(r_buf, (r_mid0, r_mid1), res_o, spot, r_send, r_recv, dp, t)
    mail_tok = Mail(t_buf, (t_mid0, t_mid1), gtok_o, spot, t_send, t_recv, dp, t)
    across = (partner("x", *partner("core", dp, t)))
    greet(neighbours(dp, t) + [swap_gn.who, across])
    plan = Plan()
    chains = []
    for n in range(15):
        p, j, rows, lanes, kinds = kind_of(n)
        c = Chain(rows, lanes, kinds, TURN[n], dp, t)
        c.gots = [None] * (STAGE[n] + 1) + [refs.pop(0) for _ in range(STAGE[n] + 1, 6)]
        c.bufs = list(c.gots)
        c.bufs[STAGE[n]] = parts_in[n]
        c.send, c.recv = send.at[n], recv.at[n]
        c.full, c.base = (gate_f, up_f, down_f)[j], (0, 512 * p) if j < 2 else (512 * p, 0)
        chains.append(c)
    late, late_whole = [], []
    for i in range(9):
        c = Chain(128, 896, K_KINDS, LATE_TURN[i], dp, t)
        if i % 4 == 0:
            whole = refs.pop(0)
        c.source = whole.at[pl.ds(128 * (i % 4), 128), :] if i < 8 else whole
        c.gots = [refs.pop(0) for _ in range(6)]
        c.bufs = c.gots + [c.source]
        c.send, c.recv = send.at[15 + i], recv.at[15 + i]
        c.full, c.base = (query_f, out_f, kv_f)[i // 4], (128 * (i % 4), 0)
        late.append(c)
        if i % 4 == 0:
            late_whole.append(whole)
    q_src, o_src, k_src = late_whole
    meeting = plan.add(lambda: met(16), 0.5, rank=0)
    for n, c in enumerate(chains):
        follow(plan, c, STAGE[n] + 1, 5, [meeting], RANK[n], True)
    swapped = [Message("tn", 128 * 896 * 2.0) for _ in range(4)]
    sent = [plan.add(functools.partial(swap_mlp.start, j), 0.1, [meeting], sends=swapped[j : j + 1], rank=3) for j in range(4)]

    def norm_two(i):
        at = pl.ds(i * 128, 128)
        res, grad = residual[at, :], gn2[at, :]
        inverse = lax.rsqrt(jnp.mean(res * res, axis=-1, keepdims=True) + epsilon)
        unit = res * inverse
        total = jnp.sum((grad * unit).reshape(16, 8, 896), axis=0)
        scaled = grad * vecs[1:2, :]
        mean = jnp.mean(scaled * unit, axis=-1, keepdims=True)
        final = gy[at, :].astype(F32) + inverse * (scaled - unit * mean)
        grad_res[at, :] = final
        ga[at, :] = final.astype(BF)
        if i == 0:
            small_buf[0] = jnp.zeros((8, 896), F32)
        small_buf[0, 1:2, :] += jnp.sum(total, axis=0, keepdims=True)

    normed_back = [plan.add(functools.partial(norm_two, i), 0.6, rank=5) for i in range(4)]
    meeting["after"] = normed_back[:1]

    def prepare():
        fill_mask(mask, length)
        for side in range(2):
            sides[side] = one_head(k_in[...], side)
            sides[2 + side] = one_head(v_in[...], side)
        gk_t[...] = jnp.zeros((64, 512), F32)
        gv_t[...] = jnp.zeros((64, 512), F32)

    prepared = plan.add(prepare, 0.6, rank=5)

    def out_back():
        gm[:, pl.ds(384, 128)] = jnp.zeros((512, 128), BF)
        gm[:, pl.ds(0, 448)] = mm_t(ga[...], wo[...]).astype(BF)

    mixed_back = plan.add(out_back, 0.8, normed_back, rank=5)

    def heads(b, p):
        rows, keys = pl.ds(256 * b, 256), pl.ds(0, 256 * (b + 1))
        lanes = pl.ds(128 * p, 128)
        cos, sin = spread(table[rows, :])
        pair, pair_gm = q_in[rows, lanes], gm[rows, lanes]
        pair_t, pair_gm_t = pair.T, pair_gm.T
        grad = jnp.zeros((256, 128), F32)
        for side in range(2 if p < 3 else 1):
            h = 2 * p + side
            score = mm_t(pair, sides[side, keys, :]) + mask[rows, keys]
            probs = jnp.exp(score - lse[rows, h : h + 1])
            grad_probs = mm_t(pair_gm, sides[2 + side, keys, :])
            inner = jnp.sum(probs * grad_probs, axis=-1, keepdims=True)
            grad_scores = (probs * (grad_probs - inner)).astype(BF)
            grad = grad + mm(grad_scores, sides[side, keys, :])
            half = slice(64 * side, 64 * side + 64)
            gk_t[:, keys] += mm(pair_t[half, :], grad_scores)
            gv_t[:, keys] += mm(pair_gm_t[half, :], probs.astype(BF))
        gq[rows, lanes] = turn(grad, cos, -sin).astype(BF)

    key_grads = [None, None]

    def norm_part(b):
        rows = pl.ds(256 * b, 256)
        flat = table[rows, :].T
        cos_t, sin_t = flat[0:32], flat[64:96]
        one, two = gk_t[0:32, rows] * 0.125, gk_t[32:64, rows] * 0.125
        whole = jnp.concatenate([one * cos_t + two * sin_t, two * cos_t - one * sin_t, gv_t[:, rows]], axis=0).astype(BF)
        gkv = whole.T
        key_grads[b] = (whole, jnp.sum(gkv.astype(F32), axis=0, keepdims=True))
        part = mm(gq[rows, pl.ds(0, 448)], wq[...]) + mm(gkv[:, 0:64], wk[...]) + mm(gkv[:, 64:128], wv[...])
        gn[rows, :] = part.astype(BF)
        swap_gn.start(2 * b)
        swap_gn.start(2 * b + 1)

    returned = [Message("tn", 128 * 896 * 2.0) for _ in range(4)]
    before, parts = [prepared, mixed_back], [None, None]
    for b in (1, 0):
        before = [plan.add(functools.partial(heads, b, p), (1.0 + b) * (1.0 if p < 3 else 0.5), before, rank=5) for p in range(4)][-1:]
        parts[b] = plan.add(functools.partial(norm_part, b), 1.0, before + [meeting], sends=returned[2 * b : 2 * b + 2], rank=5)
        before = [parts[b]]

    for j in range(4 - SWAP_LATE, 4):
        sent[j]["after"] = [parts[0]]

    def make_kv():
        whole = jnp.concatenate([key_grads[0][0], key_grads[1][0]], axis=1)
        k_src[...] = mm(whole, normed[...]).astype(BF)
        small_buf[0, 2:3, 0:448] = jnp.sum(gq[:, pl.ds(0, 448)].astype(F32), axis=0, keepdims=True)
        small_buf[0, 2:3, 512:640] = key_grads[0][1] + key_grads[1][1]
        small_buf[0, 3:4, :] = jnp.sum(squares[...], axis=0, keepdims=True)

    def make_q():
        q_src[...] = t_mm(gq[...], normed[...]).astype(BF)

    def make_o():
        o_src[...] = t_mm(mixed[...], ga[...]).astype(BF)

    made_q = plan.add(make_q, 0.8, [parts[0]], rank=5)
    made_kv = plan.add(make_kv, 0.6, [parts[0]], rank=5)
    made_o = plan.add(make_o, 0.8, [mixed_back], rank=4.5)
    for i, c in enumerate(late):
        follow(plan, c, 0, 5, [(made_q, made_o, made_kv)[i // 4], meeting], LATE_RANK[i], True)

    def output(i):
        at = pl.ds(i * 128, 128)
        valid = lax.broadcasted_iota(jnp.int32, (128, 896), 0) + i * 128 < length
        branch = jnp.where(valid, swap_mlp.take(i), 0.0)
        result = jnp.where(valid, residual[at, :] + branch, 0.0)
        r_buf[pl.ds(i * 2, 2)] = result.reshape(2, 8, 8, 896).astype(BF)
        for row, x in ((4, result), (5, branch)):
            some = jnp.sum((x * x).reshape(16, 8, 896), axis=0)
            small_buf[0, row : row + 1, :] += jnp.sum(some, axis=0, keepdims=True)

    outputs = [plan.add(functools.partial(output, i), 0.5, [sent[i]] + normed_back, swapped[i : i + 1], rank=6) for i in range(4)]

    def post(mail, ready, rank):
        one, two = Message("all", 2 * 458752.0), Message("all", 2 * 458752.0)
        a = plan.add(mail.first, 0.8, ready, sends=[one], rank=rank)
        b = plan.add(mail.second, 0.9, [a], [one], [two], rank)
        plan.add(mail.last, 0.2, [b], [two], rank=rank)

    post(mail_res, outputs + [meeting], MAIL_RANK[0])

    def norm_one(i):
        at = pl.ds(i * 128, 128)
        grad = swap_gn.take(i)
        row = stream[at, :].astype(F32)
        inverse = lax.rsqrt(jnp.mean(row * row, axis=-1, keepdims=True) + epsilon)
        unit = row * inverse
        total = jnp.sum((grad * unit).reshape(16, 8, 896), axis=0)
        scaled = grad * vecs[0:1, :]
        mean = jnp.mean(scaled * unit, axis=-1, keepdims=True)
        final = grad_res[at, :] + inverse * (scaled - unit * mean)
        t_buf[pl.ds(i * 2, 2)] = final.reshape(2, 8, 8, 896).astype(BF)
        small_buf[0, 0:1, :] += jnp.sum(total, axis=0, keepdims=True)

    finals = [plan.add(functools.partial(norm_one, i), 0.6, [parts[i // 2]], returned[i : i + 1], rank=1) for i in range(4)]
    post(mail_tok, finals, MAIL_RANK[1])

    def quartet(s):
        if s == 0:
            return [partner("core", dp, t), partner("x", dp, t), across]
        one, two = ("ya", "yb") if s == 1 else ("za", "zb")
        return [partner(one, dp, t), partner(two, dp, t), partner(one, *partner(two, dp, t))]

    posted = {}

    def share(s):
        posted[s] = [
            remote(small_buf.at[s], small_got.at[3 * s + i], s_send.at[3 * s + i], s_recv.at[3 * s + i], who)
            for i, who in enumerate(quartet(s))
        ]
        for c in posted[s]:
            c.start()

    def collect(s):
        for c in posted[s]:
            c.wait()
        small_buf[s + 1] = (small_buf[s] + small_got[3 * s]) + (small_got[3 * s + 1] + small_got[3 * s + 2])
        if s < 2:
            share(s + 1)
        else:
            small_o[...] = small_buf[3]

    message = Message("x", 28672.0)
    task = plan.add(functools.partial(share, 0), 0.2, finals + outputs + [made_kv], sends=[message], rank=1)
    for s in range(3):
        after = Message(("ya", "za", "za")[s], 28672.0)
        task = plan.add(functools.partial(collect, s), 0.2, [task], [message], [after] if s < 2 else [], rank=1)
        message = after
    plan.run()


def finish(*operands):
    wide_out = pltpu.VMEM((896, 2560), BF), pltpu.VMEM((896, 2560), BF), pltpu.VMEM((2560, 896), BF)
    room = []
    for n in range(15):
        room += [pltpu.VMEM(stage_shape(n, s), BF) for s in range(STAGE[n] + 1, 6)]
    for i in range(9):
        if i % 4 == 0:
            room.append(pltpu.VMEM((512 if i < 8 else 128, 896), BF))
        room += [pltpu.VMEM(x, BF) for x in K_SHAPES]
    return pl.pallas_call(
        finish_kernel,
        out_shape=(
            *wide_out,
            pltpu.VMEM((512, 896), BF),
            pltpu.VMEM((128, 896), BF),
            pltpu.VMEM((512, 896), BF),
            pltpu.VMEM((8, 896), F32),
            pltpu.VMEM((8, 8, 8, 896), BF),
            pltpu.VMEM((8, 8, 8, 896), BF),
        ),
        in_specs=[SMEM_SPEC] + [VMEM_SPEC] * 33,
        out_specs=(VMEM_SPEC,) * 9,
        scratch_shapes=[
            pltpu.VMEM((512, 896), BF),
            pltpu.VMEM((512, 896), BF),
            pltpu.VMEM((512, 896), BF),
            pltpu.VMEM((4, 512, 128), BF),
            pltpu.VMEM((512, 512), F32),
            pltpu.VMEM((512, 896), BF),
            pltpu.VMEM((512, 512), BF),
            pltpu.VMEM((512, 512), BF),
            pltpu.VMEM((64, 512), F32),
            pltpu.VMEM((64, 512), F32),
            pltpu.VMEM((512, 896), F32),
            pltpu.VMEM((4, 8, 896), F32),
            pltpu.VMEM((9, 8, 896), F32),
            DMA((2, 4)), DMA((2, 4)), DMA((24, 12)), DMA((24, 12)), DMA((9,)), DMA((9,)),
            *MAIL_SCRATCH, *MAIL_SCRATCH, *room,
        ],
        compiler_params=params(4, 38 << 20),
        name="finish",
    )(*[in_vmem(x) if i in FROM_WIDE else x for i, x in enumerate(operands)])


def unpack_kernel(
    order, lengths, gate, up, down, query, kv, out_w, small, res, gtok,
    gate_o, up_o, down_o, query_o, key_o, value_o, out_o, res_o, gtok_o, gain1_o, gain2_o, bq_o, bk_o, bv_o, rms_o,
    where_from,
):
    i = pl.program_id(0)

    @pl.when(i == 0)
    def _():
        def note(g, carry):
            where_from[order[g]] = g
            return carry + lengths[g]

        count = lax.fori_loop(0, 64, note, 0).astype(F32) * 896.0
        rms = jnp.sqrt(jnp.sum(small[...], axis=-1, keepdims=True) / count)
        lane = lax.broadcasted_iota(jnp.int32, (1, 128), 1)
        line = jnp.where(lane == 0, rms[4:5], jnp.where(lane == 1, rms[3:4], rms[5:6]))
        gain1_o[...] = small[0, :]
        gain2_o[...] = small[1, :]
        bq_o[...] = small[2, 0:448]
        pair = small[2:3, 512:640]
        bk_o[...] = pair[0, 0:64]
        bv_o[...] = pltpu.roll(pair, 64, 1)[0, 0:64]
        rms_o[...] = line[0, 0:3]
        key_o[...] = kv[pl.ds(0, 64), :].astype(F32)
        value_o[...] = kv[pl.ds(64, 64), :].astype(F32)

    rows = pl.ds(pl.multiple_of(i * 64, 64), 64)
    gate_o[...] = gate[rows, pl.ds(0, 2432)].astype(F32)
    up_o[...] = up[rows, pl.ds(0, 2432)].astype(F32)
    down_o[...] = down[pl.ds(pl.multiple_of(i * 176, 16), 176), :].astype(F32)

    @pl.when(i < 7)
    def _():
        query_o[...] = query[rows, :].astype(F32)
        out_o[...] = out_w[rows, :].astype(F32)

    @pl.when(i < 8)
    def _():
        for j in range(8):
            slot = where_from[jnp.minimum(i, 7) * 8 + j]
            res_o[j] = res[slot]
            gtok_o[j] = gtok[slot]


def unpack(*operands):
    rows = lambda i: (i, 0)
    some = lambda i: (jnp.minimum(i, 6), 0)
    return pl.pallas_call(
        unpack_kernel,
        grid=(14,),
        out_shape=(
            jax.ShapeDtypeStruct((896, 2432), F32),
            jax.ShapeDtypeStruct((896, 2432), F32),
            jax.ShapeDtypeStruct((2432, 896), F32),
            jax.ShapeDtypeStruct((448, 896), F32),
            jax.ShapeDtypeStruct((64, 896), F32),
            jax.ShapeDtypeStruct((64, 896), F32),
            jax.ShapeDtypeStruct((448, 896), F32),
            BLOCK,
            BLOCK,
            *[jax.ShapeDtypeStruct((n,), F32) for n in (896, 896, 448, 64, 64, 3)],
        ),
        in_specs=[SMEM_SPEC] * 2 + [VMEM_SPEC] * 9,
        out_specs=(
            pl.BlockSpec((64, 2432), rows),
            pl.BlockSpec((64, 2432), rows),
            pl.BlockSpec((176, 896), rows),
            pl.BlockSpec((64, 896), some),
            pl.BlockSpec((64, 896), lambda i: (0, 0)),
            pl.BlockSpec((64, 896), lambda i: (0, 0)),
            pl.BlockSpec((64, 896), some),
            pl.BlockSpec((8, 8, 896), lambda i: (jnp.minimum(i, 7), 0, 0)),
            pl.BlockSpec((8, 8, 896), lambda i: (jnp.minimum(i, 7), 0, 0)),
            *[VMEM_SPEC] * 6,
        ),
        scratch_shapes=[pltpu.SMEM((64,), jnp.int32)],
        compiler_params=pltpu.CompilerParams(vmem_limit_bytes=16 << 20),
        name="unpack",
    )(*operands[:2], *[pltpu.with_memory_space_constraint(x, pltpu.VMEM) for x in operands[2:]])


def on_device(
    tokens,
    cotangent,
    lengths,
    deal_order,
    gain_attn,
    w_query,
    b_query,
    w_key,
    b_key,
    w_value,
    b_value,
    w_out,
    gain_mlp,
    w_gate,
    w_up,
    w_down,
):
    table = jnp.asarray(rope_table())
    biases = jnp.concatenate([b_query, b_key, b_value, jnp.zeros((320,), BF)])
    blank = jnp.zeros((896,), BF)
    vecs = jnp.stack([gain_attn, gain_mlp, biases] + [blank] * 5).astype(F32)
    normed, q, k, v, lse, mixed, residual, normed_two, gy, squares, stream = meet(
        deal_order, lengths, tokens, cotangent, w_query.T, w_key.T, w_value.T, w_out, vecs, table
    )
    gn2, mlp, *sums = wide(normed_two, gy, w_gate, w_up, w_down)
    gate, up, down, query, kv, out_w, small, sent_res, sent_tok = finish(
        lengths, *sums, normed, q, k, v, lse, mixed, mlp, residual, gn2, gy, stream,
        w_query.T, w_key.T, w_value.T, w_out, vecs, table, squares,
    )
    (
        gate, up, down, query, key, value, out_w, layer_out, grad_tokens,
        gain_one, gain_two, bias_query, bias_key, bias_value, rms_values,
    ) = unpack(
        deal_order, lengths, gate, up, down, query, kv, out_w, small,
        sent_res.reshape(64, 8, 896), sent_tok.reshape(64, 8, 896),
    )
    return (
        layer_out,
        grad_tokens,
        gain_one,
        query.T,
        bias_query,
        key.T,
        bias_key,
        value.T,
        bias_value,
        out_w,
        gain_two,
        gate,
        up,
        down,
        rms_values,
    )


def solution(mesh):
    in_specs = (
        P(None, "dp", None),
        P(None, "dp", None),
        P(),
        P(),
        P(),
        P(None, "tensor"),
        P("tensor"),
        P(None, "tensor"),
        P("tensor"),
        P(None, "tensor"),
        P("tensor"),
        P("tensor", None),
        P(),
        P(None, "tensor"),
        P(None, "tensor"),
        P("tensor", None),
    )
    out_specs = (
        P(None, "dp", None),
        P(None, "dp", None),
        P(),
        P(None, "tensor"),
        P("tensor"),
        P(None, "tensor"),
        P("tensor"),
        P(None, "tensor"),
        P("tensor"),
        P("tensor", None),
        P(),
        P(None, "tensor"),
        P(None, "tensor"),
        P("tensor", None),
        P(),
    )
    return jax.shard_map(
        on_device, mesh=mesh, in_specs=in_specs, out_specs=out_specs, check_vma=False
    )
```

```python
import functools
import math

import jax
import jax.numpy as jnp
import numpy as np
from jax import lax
from jax.experimental import pallas as pl
from jax.experimental.pallas import tpu as pltpu
from jax.sharding import PartitionSpec as P

MESH = pl.DeviceIdType.MESH
HD = 64
epsilon = 1e-06
rope_base = 1000000.0
VMEM_LIMIT = 60 << 20
LINKS = ("x", "ya", "za", "yb", "zb")


def flip(dp):
    return dp + 8 - 16 * ((dp // 8) % 2)


def group_of(dp, t):
    return dp + t * (flip(dp) - dp)


def coords():
    return lax.axis_index("dp"), lax.axis_index("tensor")


def partner(dim, dp, t):
    y, xl, z, c = dp // 16, (dp // 8) % 2, (dp // 2) % 4, dp % 2
    if dim == "core":
        c = 1 - c
    if dim == "x":
        xl = 1 - xl
    if dim == "ya":
        y = y + 1 - 2 * (y % 2)
    if dim == "yb":
        y = 3 - y
    if dim == "za":
        z = z + 1 - 2 * (z % 2)
    if dim == "zb":
        z = 3 - z
    if dim == "tn":
        xl, t = 1 - xl, 1 - t
    return (((y * 2 + xl) * 4 + z) * 2 + c, t)


def bit(dim, dp):
    y, xl, z, c = dp // 16, (dp // 8) % 2, (dp // 2) % 4, dp % 2
    return {
        "core": c,
        "x": xl,
        "ya": ((y + 1) // 2) % 2,
        "yb": y // 2,
        "za": ((z + 1) // 2) % 2,
        "zb": z // 2,
    }[dim]


def greet(partners):
    barrier = pltpu.get_barrier_semaphore()
    for who in partners:
        pl.semaphore_signal(barrier, inc=1, device_id=who, device_id_type=MESH)


def around(dp, t, axis, j):
    a, b = dp // 8, dp % 8
    return (((a + j) % 8 * 8 + b) if axis == 0 else a * 8 + (b + j) % 8, t)


def neighbours(dp, t):
    return [around(dp, t, axis, j) for axis in range(2) for j in range(1, 8)]


def met(n):
    pl.semaphore_wait(pltpu.get_barrier_semaphore(), n)


def remote(src, dst, send, recv, who):
    return pltpu.make_async_remote_copy(
        src_ref=src, dst_ref=dst, send_sem=send, recv_sem=recv, device_id=who, device_id_type=MESH
    )


def put_sum(dst, src, row, lane, other, rows, lanes):
    step = 16
    while step * 2 * lanes <= 32768 and rows % (step * 2) == 0:
        step *= 2

    def body(i, carry):
        here = pl.ds(pl.multiple_of(i * step, 16), step)
        there = pl.ds(pl.multiple_of(row + i * step, 16), step)
        lane_at = lane if isinstance(lane, int) else pl.multiple_of(lane, 128)
        dst[here, :] = src[there, pl.ds(lane_at, lanes)] + other[here, :]
        return carry

    lax.fori_loop(0, rows // step, body, 0)


def halves(rows, lanes, kinds):
    out = []
    for kind in kinds:
        if kind == "r":
            rows //= 2
        elif kind == "l":
            lanes //= 2
        out.append((rows, lanes))
    return out


class Chain:
    def __init__(self, rows, lanes, kinds, turn, dp, t):
        self.kinds = kinds
        self.dims = ("core",) + tuple(LINKS[(turn + i) % 5] for i in range(5))
        self.who = [partner(d, dp, t) for d in self.dims]
        self.bits = [bit(d, dp) for d in self.dims]
        self.shapes = [(rows, lanes)] + halves(rows, lanes, kinds)
        self.last = max(i for i, kind in enumerate(kinds) if kind != "f")
        self.corner = [(0, 0)]
        for s, kind in enumerate(kinds):
            row, lane = self.corner[-1]
            rows, lanes = self.shapes[s + 1]
            b = self.bits[s]
            self.corner.append((row + (b * rows if kind == "r" else 0), lane + (b * lanes if kind == "l" else 0)))

    def start(self, s, src, got, send, recv):
        rows, lanes = self.shapes[s + 1]
        give, self.keep = (0, 0), (0, 0)
        b = self.bits[s]
        if self.kinds[s] == "r":
            give, self.keep = (pl.multiple_of((1 - b) * rows, 16), 0), (b * rows, 0)
        elif self.kinds[s] == "l":
            give, self.keep = (0, pl.multiple_of((1 - b) * lanes, 128)), (0, b * lanes)
        self.src, self.got = src, got
        self.copy = remote(src.at[pl.ds(give[0], rows), pl.ds(give[1], lanes)], got, send, recv, self.who[s])
        self.copy.start()

    def finish(self, s, dst):
        self.copy.wait()
        rows, lanes = self.shapes[s + 1]
        put_sum(dst, self.src, self.keep[0], self.keep[1], self.got, rows, lanes)

    def spot(self, s, full, base):
        rows, lanes = self.shapes[s]
        row, lane = self.corner[s]
        row, lane = row + base[0], lane + base[1]
        row = row if isinstance(row, int) else pl.multiple_of(row, 16)
        lane = lane if isinstance(lane, int) else pl.multiple_of(lane, 128)
        return full.at[pl.ds(row, rows), pl.ds(lane, lanes)]

    def gather_start(self, s, full, base, send, recv):
        mine = self.spot(s + 1, full, base)
        self.copy = remote(mine, mine, send, recv, self.who[s])
        self.copy.start()

    def gather_finish(self):
        self.copy.wait()


G_KINDS = ("l", "l", "r", "r", "r", "f")
D_KINDS = ("r", "r", "r", "r", "r", "f")
K_KINDS = ("r", "r", "r", "f", "f", "f")
ANY_SPEC = pl.BlockSpec(memory_space=pl.ANY)
G_SHAPES = halves(896, 512, G_KINDS)
D_SHAPES = halves(512, 896, D_KINDS)
K_SHAPES = halves(128, 896, K_KINDS)
BF, F32 = jnp.bfloat16, jnp.float32
VMEM_SPEC = pl.BlockSpec(memory_space=pltpu.VMEM)
SMEM_SPEC = pl.BlockSpec(memory_space=pltpu.SMEM)
BLOCK = jax.ShapeDtypeStruct((64, 8, 896), BF)
DMA = pltpu.SemaphoreType.DMA


def params(cid, limit=VMEM_LIMIT):
    return pltpu.CompilerParams(collective_id=cid, has_side_effects=True, vmem_limit_bytes=limit)


class Mail:
    LOW = 512

    def __init__(self, buf, mids, out, spot, send, recv, dp, t):
        self.buf, self.mids, self.out = buf, mids, out
        self.me = (dp // 8, dp % 8)
        self.spot = spot
        self.send, self.recv, self.dp, self.t = send, recv, dp, t
        self.lanes = (pl.ds(0, self.LOW), pl.ds(self.LOW, 896 - self.LOW))

    def first(self):
        self.copies = [[], []]
        for j in range(1, 8):
            for f in range(2):
                to = (self.me[f] + j) % 8
                src = self.buf.at[to, :, :, self.lanes[f]] if f == 0 else self.buf.at[:, to, :, self.lanes[f]]
                c = remote(src, self.mids[f].at[self.spot[f]], self.send.at[0, f, j], self.recv.at[0, f, j],
                           around(self.dp, self.t, f, j))
                c.start()
                self.copies[f].append(c)
        for f in range(2):
            me = self.me[f]
            own = self.buf[me, :, :, self.lanes[f]] if f == 0 else self.buf[:, me, :, self.lanes[f]]
            self.mids[f][self.spot[f]] = own

    def second(self):
        for f in range(2):
            for c in self.copies[f]:
                c.wait()
        self.copies = []
        for j in range(1, 8):
            for f in range(2):
                g = 1 - f
                to = (self.me[g] + j) % 8
                dst = self.out.at[:, self.spot[1], :, self.lanes[f]] if f == 0 else self.out.at[self.spot[0], :, :, self.lanes[f]]
                c = remote(self.mids[f].at[:, to], dst, self.send.at[1, f, j], self.recv.at[1, f, j],
                           around(self.dp, self.t, g, j))
                c.start()
                self.copies.append(c)
        for f in range(2):
            own = self.mids[f][:, self.me[1 - f]]
            if f == 0:
                self.out[:, self.spot[1], :, self.lanes[f]] = own
            else:
                self.out[self.spot[0], :, :, self.lanes[f]] = own

    def last(self):
        for c in self.copies:
            c.wait()


MAIL = jax.ShapeDtypeStruct((8, 8, 8, 896), BF)
MAIL_SCRATCH = [
    pltpu.VMEM((8, 8, 8, 896), BF), pltpu.VMEM((8, 8, 8, 512), BF), pltpu.VMEM((8, 8, 8, 384), BF),
    DMA((2, 2, 8)), DMA((2, 2, 8)),
]


def sort_out(order, rows, buf, dp, t):
    def go(a, carry):
        for b in range(8):
            buf[a, b] = rows[order[group_of(a * 8 + b, t)]]
        return carry

    lax.fori_loop(0, 8, go, 0)


def mm(a, b):
    return jnp.dot(a, b, preferred_element_type=F32)


def mm_t(a, b):
    return lax.dot_general(a, b, (((1,), (1,)), ((), ())), preferred_element_type=F32)


def t_mm(a, b):
    return lax.dot_general(a, b, (((0,), (0,)), ((), ())), preferred_element_type=F32)


def rope_table():
    places = np.arange(512, dtype=np.float32)
    frequency = np.power(np.float32(rope_base), -np.arange(32, dtype=np.float32) * np.float32(2.0 / HD)).astype(np.float32)
    angles = (places[:, None] * frequency[None, :]).astype(np.float64)
    cos, sin = np.cos(angles), np.sin(angles)
    return np.concatenate([cos, cos, sin, sin], axis=1).astype(np.float32)


def first_half(shape):
    return lax.broadcasted_iota(jnp.int32, shape, 1) % 64 < 32


def spread(table):
    other = pltpu.roll(table, 64, 1)
    low = lax.broadcasted_iota(jnp.int32, table.shape, 1) < 64
    cos, sin = jnp.where(low, table, other), jnp.where(low, other, table)
    return cos, jnp.where(first_half(table.shape), -sin, sin)


def turn(x, cos, sin):
    swapped = jnp.where(first_half(x.shape), pltpu.roll(x, 96, 1), pltpu.roll(x, 32, 1))
    return x * cos + swapped * sin


def one_head(pair, side):
    low = lax.broadcasted_iota(jnp.int32, pair.shape, 1) < 64
    return jnp.where(low if side == 0 else jnp.logical_not(low), pair, jnp.zeros_like(pair))


def fill_mask(mask, length):
    for b in range(2):
        rows = lax.broadcasted_iota(jnp.int32, (256, 512), 0) + b * 256
        cols = lax.broadcasted_iota(jnp.int32, (256, 512), 1)
        mask[pl.ds(b * 256, 256), :] = jnp.where((cols <= rows) & (cols < length), 0.0, -1e30)


class Swap:
    def __init__(self, x, got, send, recv, dp, t):
        self.who = partner("tn", dp, t)
        self.x, self.got, self.send, self.recv = x, got, send, recv
        self.copies = [None] * 4

    def start(self, i):
        rows = pl.ds(i * 128, 128)
        self.copies[i] = remote(self.x.at[rows], self.got.at[rows], self.send.at[i], self.recv.at[i], self.who)
        self.copies[i].start()

    def take(self, i):
        self.copies[i].wait()
        rows = pl.ds(i * 128, 128)
        return self.x[rows, :].astype(F32) + self.got[rows, :].astype(F32)


def meet_kernel(
    order, lengths, tok, cot, wq, wk, wv, wo, vecs, table,
    normed, q_o, k_o, v_o, lse_o, mixed, residual, normed_two, gy, squares, stream,
    sides, mask, x, got, tok_in, cot_in, send, recv, buf, mid0, mid1, c_send, c_recv, t_buf, t_mid0, t_mid1, t_send, t_recv,
):
    dp, t = coords()
    swap = Swap(x, got, send, recv, dp, t)
    mail = Mail(buf, (mid0, mid1), cot_in, (dp // 8, dp % 8), c_send, c_recv, dp, t)
    greet(neighbours(dp, t) + [swap.who])
    length = lengths[group_of(dp, t)]
    sort_out(order, tok, t_buf, dp, t)
    tokens = Mail(t_buf, (t_mid0, t_mid1), tok_in, (dp // 8, dp % 8), t_send, t_recv, dp, t)
    met(15)
    tokens.first()
    sort_out(order, cot, buf, dp, t)
    fill_mask(mask, length)
    tokens.second()
    tokens.last()
    mail.first()
    for b in range(4):
        rows, keys = pl.ds(128 * b, 128), pl.ds(0, 128 * (b + 1))
        row = tok_in[pl.ds(b * 2, 2)].astype(F32).reshape(128, 896)
        stream[rows, :] = row.astype(BF)
        inverse = lax.rsqrt(jnp.mean(row * row, axis=-1, keepdims=True) + epsilon)
        unit = (row * inverse * vecs[0:1, :]).astype(BF)
        normed[rows, :] = unit
        cos, sin = spread(table[rows, :])
        k = mm_t(unit, wk[...]) + vecs[2:3, 448:512]
        v = mm_t(unit, wv[...]) + vecs[2:3, 512:576]
        k2 = turn(jnp.concatenate([k, k], axis=1), cos, sin)
        k2 = (k2.astype(BF).astype(F32) * 0.125).astype(BF)
        v2 = jnp.concatenate([v, v], axis=1).astype(BF)
        k_o[rows, :] = k2
        v_o[rows, :] = v2
        for side in range(2):
            sides[side, rows, :] = one_head(k2, side)
            sides[2 + side, rows, :] = one_head(v2, side)
        q = mm_t(unit, wq[...]) + vecs[2:3, 0:448]
        q = jnp.concatenate([q, jnp.zeros((128, 64), F32)], axis=1)
        for p in range(4):
            q_o[rows, pl.ds(128 * p, 128)] = turn(q[:, 128 * p : 128 * p + 128], cos, sin).astype(BF)
        lse_o[rows, :] = jnp.zeros((128, 128), F32)

        def heads(p, both):
            lanes = pl.ds(pl.multiple_of(128 * p, 128), 128)
            pair = q_o[rows, lanes]
            total = jnp.zeros((128, 128), F32)
            for side in range(2 if both else 1):
                score = mm_t(pair, sides[side, keys, :]) + mask[rows, keys]
                top = jnp.max(score, axis=-1, keepdims=True)
                expo = jnp.exp(score - top)
                mass = jnp.sum(expo, axis=-1, keepdims=True)
                probs = (expo * (1.0 / mass)).astype(BF)
                total = total + mm(probs, sides[2 + side, keys, :])
                here = lax.broadcasted_iota(jnp.int32, (128, 128), 1) == 2 * p + side
                lse_o[rows, :] = jnp.where(here, top + jnp.log(mass), lse_o[rows, :])
            mixed[rows, lanes] = total.astype(BF)

        def body(p, carry):
            heads(p, True)
            return carry

        lax.fori_loop(0, 3, body, 0)
        heads(3, False)
        x[rows, :] = mm(mixed[rows, pl.ds(0, 448)], wo[...]).astype(BF)
        swap.start(b)
        if b == 1:
            mail.second()
    total = jnp.zeros((8, 896), F32)
    for i in range(4):
        at = pl.ds(i * 128, 128)
        valid = lax.broadcasted_iota(jnp.int32, (128, 896), 0) + i * 128 < length
        attention = swap.take(i)
        res = stream[at, :].astype(F32) + attention
        residual[at, :] = res
        inverse = lax.rsqrt(jnp.mean(res * res, axis=-1, keepdims=True) + epsilon)
        normed_two[at, :] = (res * inverse * vecs[1:2, :]).astype(BF)
        kept = jnp.where(valid, attention, 0.0)
        total = total + jnp.sum((kept * kept).reshape(16, 8, 896), axis=0)
    squares[...] = total
    mail.last()
    for i in range(4):
        at = pl.ds(i * 128, 128)
        valid = lax.broadcasted_iota(jnp.int32, (128, 896), 0) + i * 128 < length
        gy[at, :] = jnp.where(valid, cot_in[pl.ds(i * 2, 2)].astype(F32).reshape(128, 896), 0.0).astype(BF)


def meet(*operands):
    rows = jax.ShapeDtypeStruct((512, 896), BF)
    wide_rows = jax.ShapeDtypeStruct((512, 512), BF)
    pair = jax.ShapeDtypeStruct((512, 128), BF)
    return pl.pallas_call(
        meet_kernel,
        out_shape=(
            rows, wide_rows, pair, pair, jax.ShapeDtypeStruct((512, 128), F32), wide_rows,
            jax.ShapeDtypeStruct((512, 896), F32), rows, rows, jax.ShapeDtypeStruct((8, 896), F32), rows,
        ),
        in_specs=[SMEM_SPEC] * 2 + [VMEM_SPEC] * 8,
        out_specs=(VMEM_SPEC,) * 11,
        scratch_shapes=[
            pltpu.VMEM((4, 512, 128), BF),
            pltpu.VMEM((512, 512), F32),
            pltpu.VMEM((512, 896), BF),
            pltpu.VMEM((512, 896), BF),
            pltpu.VMEM((8, 8, 8, 896), BF),
            pltpu.VMEM((8, 8, 8, 896), BF),
            DMA((4,)), DMA((4,)), *MAIL_SCRATCH, *MAIL_SCRATCH,
        ],
        compiler_params=params(2),
        name="meet",
    )(*operands)


class Message:
    def __init__(self, link, size):
        self.link, self.size, self.lands = link, size, None


class Plan:
    LATENCY = 3.2
    RATE = {"core": 500e3, "tn": 43e3}

    def __init__(self):
        self.tasks = []

    def add(self, act, cost, after=(), needs=(), sends=(), rank=5):
        task = dict(act=act, cost=cost, after=list(after), needs=list(needs), sends=list(sends), rank=rank, done=False)
        self.tasks.append(task)
        return task

    def run(self):
        now, free = 0.0, {}
        left = list(self.tasks)
        while left:
            open_ = [x for x in left if all(y["done"] for y in x["after"]) and all(m.lands is not None for m in x["needs"])]
            at = {id(x): max([now] + [m.lands for m in x["needs"]]) for x in open_}
            ready = [x for x in open_ if at[id(x)] <= now]
            task = min(ready, key=lambda x: x["rank"]) if ready else min(open_, key=lambda x: at[id(x)])
            now = at[id(task)] + task["cost"]
            task["act"]()
            task["done"] = True
            left.remove(task)
            for m in task["sends"]:
                links = LINKS if m.link == "all" else (m.link,)
                for link in links:
                    begin = max(now, free.get(link, 0.0))
                    free[link] = begin + m.size / len(links) / self.RATE.get(link, 40e3)
                m.lands = max(free[link] for link in links) + self.LATENCY
        return now


def follow(plan, c, first, last, begin, rank, up=False):
    def go(s):
        c.start(s, c.bufs[s - 1], c.gots[s], c.send.at[s], c.recv.at[s])

    def back(s):
        c.gather_start(s, c.full, c.base, c.send.at[6 + s], c.recv.at[6 + s])

    def size(s):
        return 2.0 * c.shapes[s + 1][0] * c.shapes[s + 1][1]

    if first > last and not up:
        return begin
    message = Message(c.dims[first], size(first))
    task = plan.add(functools.partial(go, first), 0.1, begin, sends=[message], rank=rank)
    for k in range(first, last + 1):
        def step(k=k):
            c.finish(k, c.bufs[k])
            if k < last:
                go(k + 1)
            elif up:
                c.spot(6, c.full, c.base)[...] = c.bufs[5][...]
                back(c.last)

        after = None
        if k < last:
            after = Message(c.dims[k + 1], size(k + 1))
        elif up:
            after = Message(c.dims[c.last], size(c.last))
        task = plan.add(step, 0.1 + size(k) / 2e6, [task], [message], [after] if after else [], rank)
        message = after
    if not up:
        return [task]
    for k in range(c.last, -1, -1):
        def step(k=k):
            c.gather_finish()
            if k > 0:
                back(k - 1)

        after = Message(c.dims[k - 1], size(k - 1)) if k > 0 else None
        task = plan.add(step, 0.1, [task], [message], [after] if after else [], rank)
        message = after
    return [task]


EARLY = 3
STAGE = [4, 4, 3, 4, 4, 4, 4, 3, 2, 2, 2, 1, 1, 1, 1]


TURN = [2, 4, 1, 0, 3, 0, 1, 2, 3, 4, 0, 3, 4, 2, 1]


def kind_of(n):
    p, j = n // 3, n % 3
    return (p, j, 896, 512, G_KINDS) if j < 2 else (p, j, 512, 896, D_KINDS)


def stage_shape(n, s):
    _, _, rows, lanes, kinds = kind_of(n)
    return ([(rows, lanes)] + halves(rows, lanes, kinds))[s + 1]


def tile(p):
    return pl.ds(512 * p, 512 if p < 4 else 384)


def wide_kernel(*refs):
    normed, gy, w_gate, w_up, w_down, gn_out, mlp_out = refs[:7]
    parts, refs = refs[7:22], refs[22:]
    gn_total, mlp_total, gn, got, hid, gg, gu, gate_w, up_w, down_w, x_send, x_recv, send, recv, local = refs[:15]
    refs = list(refs[15:])
    dp, t = coords()
    swap = Swap(gn, got, x_send, x_recv, dp, t)
    greet([swap.who] + [partner(d, dp, t) for d in ("core",) + LINKS])
    chains = []
    for n in range(15):
        p, j, rows, lanes, kinds = kind_of(n)
        c = Chain(rows, lanes, kinds, TURN[n], dp, t)
        c.source = refs.pop(0)
        c.gots = [refs.pop(0) for _ in range(STAGE[n] + 1)]
        c.bufs = c.gots[:-1] + [parts[n]] + [c.source]
        c.send, c.recv = send.at[n], recv.at[n]
        chains.append(c)
    loads = []

    def load(p):
        at, w, b = tile(p), 512 if p < 4 else 384, p % 2
        copies = [
            pltpu.make_async_copy(w_gate.at[:, at], gate_w.at[b, :, pl.ds(0, w)], local.at[p, 0]),
            pltpu.make_async_copy(w_up.at[:, at], up_w.at[b, :, pl.ds(0, w)], local.at[p, 1]),
            pltpu.make_async_copy(w_down.at[at, :], down_w.at[b, pl.ds(0, w), :], local.at[p, 2]),
        ]
        for c in copies:
            c.start()
        loads.append(copies)

    def layer(p):
        at, w, b = tile(p), 512 if p < 4 else 384, p % 2
        for c in loads[p]:
            c.wait()
        wg, wu, wd = gate_w.at[b, :, pl.ds(0, w)], up_w.at[b, :, pl.ds(0, w)], down_w.at[b, pl.ds(0, w), :]
        gate = mm(normed[...], wg[...])
        up = mm(normed[...], wu[...])
        back = mm_t(gy[...], wd[...])
        sig = 1.0 / (1.0 + jnp.exp(-gate))
        silu = gate * sig
        hid[:, at] = (silu * up).astype(BF)
        gu[:, at] = (back * silu).astype(BF)
        gg[:, at] = (back * up * sig * (1.0 + gate * (1.0 - sig))).astype(BF)
        mlp = mm(hid[:, at], wd[...])
        grad = mm_t(gg[:, at], wg[...]) + mm_t(gu[:, at], wu[...])
        if p == 0:
            mlp_total[...] = mlp
            gn_total[...] = grad
        elif p < 4:
            mlp_total[...] += mlp
            gn_total[...] += grad
        else:
            mlp_out[...] = (mlp_total[...] + mlp).astype(BF)
            gn[...] = (gn_total[...] + grad).astype(BF)
        if p + 2 < 5:
            load(p + 2)

    def weight(n):
        p, j = n // 3, n % 3
        w, dst = 512 if p < 4 else 384, chains[n].source
        if j < 2:
            dst[:, pl.ds(0, w)] = t_mm(normed[...], (gg, gu)[j][:, tile(p)]).astype(BF)
            if w < 512:
                dst[:, pl.ds(w, 512 - w)] = jnp.zeros((896, 512 - w), BF)
        else:
            dst[pl.ds(0, w), :] = t_mm(hid[:, tile(p)], gy[...]).astype(BF)
            if w < 512:
                dst[pl.ds(w, 512 - w), :] = jnp.zeros((512 - w, 896), BF)

    load(0)
    load(1)
    plan = Plan()
    meeting = plan.add(lambda: met(7), 0.3, rank=6)
    layers, done = [], []
    for p in range(5):
        layers.append(plan.add(functools.partial(layer, p), 3.4 if p < 4 else 2.6, layers[-1:], rank=5))
        if p == 0:
            layers.append(meeting)
            meeting["after"] = layers[:1]
        if p < EARLY:
            layers += [plan.add(functools.partial(weight, 3 * p + j), 0.55, layers[-1:], rank=4) for j in range(3)]
            done += layers[-3:]
    returned = [Message("tn", 128 * 896 * 2.0) for _ in range(4)]
    sent = plan.add(lambda: [swap.start(i) for i in range(4)], 0.2, layers[-1:] + [meeting], sends=returned, rank=0)
    for n in range(3 * EARLY, 15):
        done.append(plan.add(functools.partial(weight, n), 0.55 if n < 12 else 0.4, [sent], rank=5))
    for n, c in enumerate(chains):
        follow(plan, c, 0, STAGE[n], [done[n], meeting], 2)

    def take(i):
        gn_out[pl.ds(i * 128, 128), :] = swap.take(i)

    for i in range(4):
        plan.add(functools.partial(take, i), 0.2, [sent], returned[i : i + 1], rank=3)
    plan.run()


def wide(*operands):
    room = []
    for n in range(15):
        room += [pltpu.VMEM(stage_shape(n, s), BF) for s in range(-1, STAGE[n] + 1)]
    return pl.pallas_call(
        wide_kernel,
        out_shape=(
            pltpu.VMEM((512, 896), F32),
            pltpu.VMEM((512, 896), BF),
            *[pltpu.VMEM(stage_shape(n, STAGE[n]), BF) for n in range(15)],
        ),
        in_specs=[VMEM_SPEC] * 2 + [ANY_SPEC] * 3,
        out_specs=(VMEM_SPEC,) * 17,
        scratch_shapes=[
            pltpu.VMEM((512, 896), F32),
            pltpu.VMEM((512, 896), F32),
            pltpu.VMEM((512, 896), BF),
            pltpu.VMEM((512, 896), BF),
            pltpu.VMEM((512, 2432), BF),
            pltpu.VMEM((512, 2432), BF),
            pltpu.VMEM((512, 2432), BF),
            pltpu.VMEM((2, 896, 512), BF),
            pltpu.VMEM((2, 896, 512), BF),
            pltpu.VMEM((2, 512, 896), BF),
            DMA((4,)), DMA((4,)), DMA((15, 12)), DMA((15, 12)), DMA((5, 3)),
            *room,
        ],
        compiler_params=params(3, 52 << 20),
        name="wide",
    )(*operands)


FROM_WIDE = set(range(1, 16)) | {22, 24}


def in_vmem(x):
    return pltpu.with_memory_space_constraint(x, pltpu.VMEM)


LATE_TURN = [4, 1, 0, 3, 1, 3, 3, 1, 3]
RANK = [4.6, 4, 4, 3.5, 3.5, 6.5, 3.5, 4, 4.2, 3.5, 4.2, 4, 4.2, 4.4, 4.6]
LATE_RANK = [2, 2, 1, 4.1, 1, 4.1, 2, 1, 3]
MAIL_RANK = [3, 0]
SWAP_LATE = 3


def finish_kernel(*refs):
    lengths, parts_in, refs = refs[0], refs[1:16], refs[16:]
    (normed, q_in, k_in, v_in, lse, mixed, mlp, residual, gn2, gy, stream,
     wq, wk, wv, wo, vecs, table, squares) = refs[:18]
    gate_f, up_f, down_f, query_f, kv_f, out_f, small_o, res_o, gtok_o = refs[18:27]
    (mlp_got, gn, gn_got, sides, mask, ga, gm, gq, gk_t, gv_t, grad_res,
     small_buf, small_got) = refs[27:40]
    x_send, x_recv, send, recv, s_send, s_recv = refs[40:46]
    r_buf, r_mid0, r_mid1, r_send, r_recv, t_buf, t_mid0, t_mid1, t_send, t_recv = refs[46:56]
    refs = list(refs[56:])
    dp, t = coords()
    spot = (dp // 8 + t * (1 - 2 * (dp // 8 % 2)), dp % 8)
    length = lengths[group_of(dp, t)]
    swap_gn = Swap(gn, gn_got, x_send.at[0], x_recv.at[0], dp, t)
    swap_mlp = Swap(mlp, mlp_got, x_send.at[1], x_recv.at[1], dp, t)
    mail_res = Mail(r_buf, (r_mid0, r_mid1), res_o, spot, r_send, r_recv, dp, t)
    mail_tok = Mail(t_buf, (t_mid0, t_mid1), gtok_o, spot, t_send, t_recv, dp, t)
    across = (partner("x", *partner("core", dp, t)))
    greet(neighbours(dp, t) + [swap_gn.who, across])
    plan = Plan()
    chains = []
    for n in range(15):
        p, j, rows, lanes, kinds = kind_of(n)
        c = Chain(rows, lanes, kinds, TURN[n], dp, t)
        c.gots = [None] * (STAGE[n] + 1) + [refs.pop(0) for _ in range(STAGE[n] + 1, 6)]
        c.bufs = list(c.gots)
        c.bufs[STAGE[n]] = parts_in[n]
        c.send, c.recv = send.at[n], recv.at[n]
        c.full, c.base = (gate_f, up_f, down_f)[j], (0, 512 * p) if j < 2 else (512 * p, 0)
        chains.append(c)
    late, late_whole = [], []
    for i in range(9):
        c = Chain(128, 896, K_KINDS, LATE_TURN[i], dp, t)
        if i % 4 == 0:
            whole = refs.pop(0)
        c.source = whole.at[pl.ds(128 * (i % 4), 128), :] if i < 8 else whole
        c.gots = [refs.pop(0) for _ in range(6)]
        c.bufs = c.gots + [c.source]
        c.send, c.recv = send.at[15 + i], recv.at[15 + i]
        c.full, c.base = (query_f, out_f, kv_f)[i // 4], (128 * (i % 4), 0)
        late.append(c)
        if i % 4 == 0:
            late_whole.append(whole)
    q_src, o_src, k_src = late_whole
    meeting = plan.add(lambda: met(16), 0.5, rank=0)
    for n, c in enumerate(chains):
        follow(plan, c, STAGE[n] + 1, 5, [meeting], RANK[n], True)
    swapped = [Message("tn", 128 * 896 * 2.0) for _ in range(4)]
    sent = [plan.add(functools.partial(swap_mlp.start, j), 0.1, [meeting], sends=swapped[j : j + 1], rank=3) for j in range(4)]

    def norm_two(i):
        at = pl.ds(i * 128, 128)
        res, grad = residual[at, :], gn2[at, :]
        inverse = lax.rsqrt(jnp.mean(res * res, axis=-1, keepdims=True) + epsilon)
        unit = res * inverse
        total = jnp.sum((grad * unit).reshape(16, 8, 896), axis=0)
        scaled = grad * vecs[1:2, :]
        mean = jnp.mean(scaled * unit, axis=-1, keepdims=True)
        final = gy[at, :].astype(F32) + inverse * (scaled - unit * mean)
        grad_res[at, :] = final
        ga[at, :] = final.astype(BF)
        if i == 0:
            small_buf[0] = jnp.zeros((8, 896), F32)
        small_buf[0, 1:2, :] += jnp.sum(total, axis=0, keepdims=True)

    normed_back = [plan.add(functools.partial(norm_two, i), 0.6, rank=5) for i in range(4)]
    meeting["after"] = normed_back[:1]

    def prepare():
        fill_mask(mask, length)
        for side in range(2):
            sides[side] = one_head(k_in[...], side)
            sides[2 + side] = one_head(v_in[...], side)
        gk_t[...] = jnp.zeros((64, 512), F32)
        gv_t[...] = jnp.zeros((64, 512), F32)

    prepared = plan.add(prepare, 0.6, rank=5)

    def out_back():
        gm[:, pl.ds(384, 128)] = jnp.zeros((512, 128), BF)
        gm[:, pl.ds(0, 448)] = mm_t(ga[...], wo[...]).astype(BF)

    mixed_back = plan.add(out_back, 0.8, normed_back, rank=5)

    def heads(b, p):
        rows, keys = pl.ds(256 * b, 256), pl.ds(0, 256 * (b + 1))
        lanes = pl.ds(128 * p, 128)
        cos, sin = spread(table[rows, :])
        pair, pair_gm = q_in[rows, lanes], gm[rows, lanes]
        pair_t, pair_gm_t = pair.T, pair_gm.T
        grad = jnp.zeros((256, 128), F32)
        for side in range(2 if p < 3 else 1):
            h = 2 * p + side
            score = mm_t(pair, sides[side, keys, :]) + mask[rows, keys]
            probs = jnp.exp(score - lse[rows, h : h + 1])
            grad_probs = mm_t(pair_gm, sides[2 + side, keys, :])
            inner = jnp.sum(probs * grad_probs, axis=-1, keepdims=True)
            grad_scores = (probs * (grad_probs - inner)).astype(BF)
            grad = grad + mm(grad_scores, sides[side, keys, :])
            half = slice(64 * side, 64 * side + 64)
            gk_t[:, keys] += mm(pair_t[half, :], grad_scores)
            gv_t[:, keys] += mm(pair_gm_t[half, :], probs.astype(BF))
        gq[rows, lanes] = turn(grad, cos, -sin).astype(BF)

    key_grads = [None, None]

    def norm_part(b):
        rows = pl.ds(256 * b, 256)
        flat = table[rows, :].T
        cos_t, sin_t = flat[0:32], flat[64:96]
        one, two = gk_t[0:32, rows] * 0.125, gk_t[32:64, rows] * 0.125
        whole = jnp.concatenate([one * cos_t + two * sin_t, two * cos_t - one * sin_t, gv_t[:, rows]], axis=0).astype(BF)
        gkv = whole.T
        key_grads[b] = (whole, jnp.sum(gkv.astype(F32), axis=0, keepdims=True))
        part = mm(gq[rows, pl.ds(0, 448)], wq[...]) + mm(gkv[:, 0:64], wk[...]) + mm(gkv[:, 64:128], wv[...])
        gn[rows, :] = part.astype(BF)
        swap_gn.start(2 * b)
        swap_gn.start(2 * b + 1)

    returned = [Message("tn", 128 * 896 * 2.0) for _ in range(4)]
    before, parts = [prepared, mixed_back], [None, None]
    for b in (1, 0):
        before = [plan.add(functools.partial(heads, b, p), (1.0 + b) * (1.0 if p < 3 else 0.5), before, rank=5) for p in range(4)][-1:]
        parts[b] = plan.add(functools.partial(norm_part, b), 1.0, before + [meeting], sends=returned[2 * b : 2 * b + 2], rank=5)
        before = [parts[b]]

    for j in range(4 - SWAP_LATE, 4):
        sent[j]["after"] = [parts[0]]

    def make_kv():
        whole = jnp.concatenate([key_grads[0][0], key_grads[1][0]], axis=1)
        k_src[...] = mm(whole, normed[...]).astype(BF)
        small_buf[0, 2:3, 0:448] = jnp.sum(gq[:, pl.ds(0, 448)].astype(F32), axis=0, keepdims=True)
        small_buf[0, 2:3, 512:640] = key_grads[0][1] + key_grads[1][1]
        small_buf[0, 3:4, :] = jnp.sum(squares[...], axis=0, keepdims=True)

    def make_q():
        q_src[...] = t_mm(gq[...], normed[...]).astype(BF)

    def make_o():
        o_src[...] = t_mm(mixed[...], ga[...]).astype(BF)

    made_q = plan.add(make_q, 0.8, [parts[0]], rank=5)
    made_kv = plan.add(make_kv, 0.6, [parts[0]], rank=5)
    made_o = plan.add(make_o, 0.8, [mixed_back], rank=4.5)
    for i, c in enumerate(late):
        follow(plan, c, 0, 5, [(made_q, made_o, made_kv)[i // 4], meeting], LATE_RANK[i], True)

    def output(i):
        at = pl.ds(i * 128, 128)
        valid = lax.broadcasted_iota(jnp.int32, (128, 896), 0) + i * 128 < length
        branch = jnp.where(valid, swap_mlp.take(i), 0.0)
        result = jnp.where(valid, residual[at, :] + branch, 0.0)
        r_buf[pl.ds(i * 2, 2)] = result.reshape(2, 8, 8, 896).astype(BF)
        for row, x in ((4, result), (5, branch)):
            some = jnp.sum((x * x).reshape(16, 8, 896), axis=0)
            small_buf[0, row : row + 1, :] += jnp.sum(some, axis=0, keepdims=True)

    outputs = [plan.add(functools.partial(output, i), 0.5, [sent[i]] + normed_back, swapped[i : i + 1], rank=6) for i in range(4)]

    def post(mail, ready, rank):
        one, two = Message("all", 2 * 458752.0), Message("all", 2 * 458752.0)
        a = plan.add(mail.first, 0.8, ready, sends=[one], rank=rank)
        b = plan.add(mail.second, 0.9, [a], [one], [two], rank)
        plan.add(mail.last, 0.2, [b], [two], rank=rank)

    post(mail_res, outputs + [meeting], MAIL_RANK[0])

    def norm_one(i):
        at = pl.ds(i * 128, 128)
        grad = swap_gn.take(i)
        row = stream[at, :].astype(F32)
        inverse = lax.rsqrt(jnp.mean(row * row, axis=-1, keepdims=True) + epsilon)
        unit = row * inverse
        total = jnp.sum((grad * unit).reshape(16, 8, 896), axis=0)
        scaled = grad * vecs[0:1, :]
        mean = jnp.mean(scaled * unit, axis=-1, keepdims=True)
        final = grad_res[at, :] + inverse * (scaled - unit * mean)
        t_buf[pl.ds(i * 2, 2)] = final.reshape(2, 8, 8, 896).astype(BF)
        small_buf[0, 0:1, :] += jnp.sum(total, axis=0, keepdims=True)

    finals = [plan.add(functools.partial(norm_one, i), 0.6, [parts[i // 2]], returned[i : i + 1], rank=1) for i in range(4)]
    post(mail_tok, finals, MAIL_RANK[1])

    def quartet(s):
        if s == 0:
            return [partner("core", dp, t), partner("x", dp, t), across]
        one, two = ("ya", "yb") if s == 1 else ("za", "zb")
        return [partner(one, dp, t), partner(two, dp, t), partner(one, *partner(two, dp, t))]

    posted = {}

    def share(s):
        posted[s] = [
            remote(small_buf.at[s], small_got.at[3 * s + i], s_send.at[3 * s + i], s_recv.at[3 * s + i], who)
            for i, who in enumerate(quartet(s))
        ]
        for c in posted[s]:
            c.start()

    def collect(s):
        for c in posted[s]:
            c.wait()
        small_buf[s + 1] = (small_buf[s] + small_got[3 * s]) + (small_got[3 * s + 1] + small_got[3 * s + 2])
        if s < 2:
            share(s + 1)
        else:
            small_o[...] = small_buf[3]

    message = Message("x", 28672.0)
    task = plan.add(functools.partial(share, 0), 0.2, finals + outputs + [made_kv], sends=[message], rank=1)
    for s in range(3):
        after = Message(("ya", "za", "za")[s], 28672.0)
        task = plan.add(functools.partial(collect, s), 0.2, [task], [message], [after] if s < 2 else [], rank=1)
        message = after
    plan.run()


def finish(*operands):
    wide_out = pltpu.VMEM((896, 2560), BF), pltpu.VMEM((896, 2560), BF), pltpu.VMEM((2560, 896), BF)
    room = []
    for n in range(15):
        room += [pltpu.VMEM(stage_shape(n, s), BF) for s in range(STAGE[n] + 1, 6)]
    for i in range(9):
        if i % 4 == 0:
            room.append(pltpu.VMEM((512 if i < 8 else 128, 896), BF))
        room += [pltpu.VMEM(x, BF) for x in K_SHAPES]
    return pl.pallas_call(
        finish_kernel,
        out_shape=(
            *wide_out,
            pltpu.VMEM((512, 896), BF),
            pltpu.VMEM((128, 896), BF),
            pltpu.VMEM((512, 896), BF),
            pltpu.VMEM((8, 896), F32),
            pltpu.VMEM((8, 8, 8, 896), BF),
            pltpu.VMEM((8, 8, 8, 896), BF),
        ),
        in_specs=[SMEM_SPEC] + [VMEM_SPEC] * 33,
        out_specs=(VMEM_SPEC,) * 9,
        scratch_shapes=[
            pltpu.VMEM((512, 896), BF),
            pltpu.VMEM((512, 896), BF),
            pltpu.VMEM((512, 896), BF),
            pltpu.VMEM((4, 512, 128), BF),
            pltpu.VMEM((512, 512), F32),
            pltpu.VMEM((512, 896), BF),
            pltpu.VMEM((512, 512), BF),
            pltpu.VMEM((512, 512), BF),
            pltpu.VMEM((64, 512), F32),
            pltpu.VMEM((64, 512), F32),
            pltpu.VMEM((512, 896), F32),
            pltpu.VMEM((4, 8, 896), F32),
            pltpu.VMEM((9, 8, 896), F32),
            DMA((2, 4)), DMA((2, 4)), DMA((24, 12)), DMA((24, 12)), DMA((9,)), DMA((9,)),
            *MAIL_SCRATCH, *MAIL_SCRATCH, *room,
        ],
        compiler_params=params(4, 38 << 20),
        name="finish",
    )(*[in_vmem(x) if i in FROM_WIDE else x for i, x in enumerate(operands)])


def unpack_kernel(
    order, lengths, gate, up, down, query, kv, out_w, small, res, gtok,
    gate_o, up_o, down_o, query_o, key_o, value_o, out_o, res_o, gtok_o, gain1_o, gain2_o, bq_o, bk_o, bv_o, rms_o,
    where_from,
):
    i = pl.program_id(0)

    @pl.when(i == 0)
    def _():
        def note(g, carry):
            where_from[order[g]] = g
            return carry + lengths[g]

        count = lax.fori_loop(0, 64, note, 0).astype(F32) * 896.0
        rms = jnp.sqrt(jnp.sum(small[...], axis=-1, keepdims=True) / count)
        lane = lax.broadcasted_iota(jnp.int32, (1, 128), 1)
        line = jnp.where(lane == 0, rms[4:5], jnp.where(lane == 1, rms[3:4], rms[5:6]))
        gain1_o[...] = small[0, :]
        gain2_o[...] = small[1, :]
        bq_o[...] = small[2, 0:448]
        pair = small[2:3, 512:640]
        bk_o[...] = pair[0, 0:64]
        bv_o[...] = pltpu.roll(pair, 64, 1)[0, 0:64]
        rms_o[...] = line[0, 0:3]
        key_o[...] = kv[pl.ds(0, 64), :].astype(F32)
        value_o[...] = kv[pl.ds(64, 64), :].astype(F32)

    rows = pl.ds(pl.multiple_of(i * 64, 64), 64)
    gate_o[...] = gate[rows, pl.ds(0, 2432)].astype(F32)
    up_o[...] = up[rows, pl.ds(0, 2432)].astype(F32)
    down_o[...] = down[pl.ds(pl.multiple_of(i * 176, 16), 176), :].astype(F32)

    @pl.when(i < 7)
    def _():
        query_o[...] = query[rows, :].astype(F32)
        out_o[...] = out_w[rows, :].astype(F32)

    @pl.when(i < 8)
    def _():
        for j in range(8):
            slot = where_from[jnp.minimum(i, 7) * 8 + j]
            res_o[j] = res[slot]
            gtok_o[j] = gtok[slot]


def unpack(*operands):
    rows = lambda i: (i, 0)
    some = lambda i: (jnp.minimum(i, 6), 0)
    return pl.pallas_call(
        unpack_kernel,
        grid=(14,),
        out_shape=(
            jax.ShapeDtypeStruct((896, 2432), F32),
            jax.ShapeDtypeStruct((896, 2432), F32),
            jax.ShapeDtypeStruct((2432, 896), F32),
            jax.ShapeDtypeStruct((448, 896), F32),
            jax.ShapeDtypeStruct((64, 896), F32),
            jax.ShapeDtypeStruct((64, 896), F32),
            jax.ShapeDtypeStruct((448, 896), F32),
            BLOCK,
            BLOCK,
            *[jax.ShapeDtypeStruct((n,), F32) for n in (896, 896, 448, 64, 64, 3)],
        ),
        in_specs=[SMEM_SPEC] * 2 + [VMEM_SPEC] * 9,
        out_specs=(
            pl.BlockSpec((64, 2432), rows),
            pl.BlockSpec((64, 2432), rows),
            pl.BlockSpec((176, 896), rows),
            pl.BlockSpec((64, 896), some),
            pl.BlockSpec((64, 896), lambda i: (0, 0)),
            pl.BlockSpec((64, 896), lambda i: (0, 0)),
            pl.BlockSpec((64, 896), some),
            pl.BlockSpec((8, 8, 896), lambda i: (jnp.minimum(i, 7), 0, 0)),
            pl.BlockSpec((8, 8, 896), lambda i: (jnp.minimum(i, 7), 0, 0)),
            *[VMEM_SPEC] * 6,
        ),
        scratch_shapes=[pltpu.SMEM((64,), jnp.int32)],
        compiler_params=pltpu.CompilerParams(vmem_limit_bytes=16 << 20),
        name="unpack",
    )(*operands[:2], *[pltpu.with_memory_space_constraint(x, pltpu.VMEM) for x in operands[2:]])


def on_device(
    tokens,
    cotangent,
    lengths,
    deal_order,
    gain_attn,
    w_query,
    b_query,
    w_key,
    b_key,
    w_value,
    b_value,
    w_out,
    gain_mlp,
    w_gate,
    w_up,
    w_down,
):
    table = jnp.asarray(rope_table())
    biases = jnp.concatenate([b_query, b_key, b_value, jnp.zeros((320,), BF)])
    blank = jnp.zeros((896,), BF)
    vecs = jnp.stack([gain_attn, gain_mlp, biases] + [blank] * 5).astype(F32)
    normed, q, k, v, lse, mixed, residual, normed_two, gy, squares, stream = meet(
        deal_order, lengths, tokens, cotangent, w_query.T, w_key.T, w_value.T, w_out, vecs, table
    )
    gn2, mlp, *sums = wide(normed_two, gy, w_gate, w_up, w_down)
    gate, up, down, query, kv, out_w, small, sent_res, sent_tok = finish(
        lengths, *sums, normed, q, k, v, lse, mixed, mlp, residual, gn2, gy, stream,
        w_query.T, w_key.T, w_value.T, w_out, vecs, table, squares,
    )
    (
        gate, up, down, query, key, value, out_w, layer_out, grad_tokens,
        gain_one, gain_two, bias_query, bias_key, bias_value, rms_values,
    ) = unpack(
        deal_order, lengths, gate, up, down, query, kv, out_w, small,
        sent_res.reshape(64, 8, 896), sent_tok.reshape(64, 8, 896),
    )
    return (
        layer_out,
        grad_tokens,
        gain_one,
        query.T,
        bias_query,
        key.T,
        bias_key,
        value.T,
        bias_value,
        out_w,
        gain_two,
        gate,
        up,
        down,
        rms_values,
    )


def solution(mesh):
    in_specs = (
        P(None, "dp", None),
        P(None, "dp", None),
        P(),
        P(),
        P(),
        P(None, "tensor"),
        P("tensor"),
        P(None, "tensor"),
        P("tensor"),
        P(None, "tensor"),
        P("tensor"),
        P("tensor", None),
        P(),
        P(None, "tensor"),
        P(None, "tensor"),
        P("tensor", None),
    )
    out_specs = (
        P(None, "dp", None),
        P(None, "dp", None),
        P(),
        P(None, "tensor"),
        P("tensor"),
        P(None, "tensor"),
        P("tensor"),
        P(None, "tensor"),
        P("tensor"),
        P("tensor", None),
        P(),
        P(None, "tensor"),
        P(None, "tensor"),
        P("tensor", None),
        P(),
    )
    return jax.shard_map(
        on_device, mesh=mesh, in_specs=in_specs, out_specs=out_specs, check_vma=False
    )
```
